128 devices in a mesh: face: 4 (over z_lo, core), tile: 32 (over z_hi, x, y).
Axes of the slice: x: 4, y: 4, z: 4 (z_hi: 2, z_lo: 2; z = z_hi * 2 + z_lo), core: 2. Of those that a mesh axis runs over, the one named last changes fastest.
Arguments:
- atmos_state: bfloat16 [32, 12, 256, 256], P(None, 'face', 'tile'), may hold values from -6 to 6
- land_sea: int32 [12, 256, 256], P('face', 'tile'), may hold values 0 or 1
- owners: int32 [3072, 1], P(('face', 'tile')), may hold values from 0 to 31; in each aligned block of 24 rows (0 to 23, 24 to 47, ...) at most 2 rows name the same one
- seam_table: int32 [48, 2], replicated, may hold values from 0 to 47, as said below
- ocean_state: float32 [4, 32, 64, 2, 256], P('face', 'tile'), may hold values from -6 to 6
- conv_input: bfloat16 [3, 64, 96], replicated, may hold values from -0.375 to 0.375
- conv_encode: bfloat16 [3, 64, 192], replicated, may hold values from -0.25 to 0.25
- conv_coarse: bfloat16 [3, 64, 192], replicated, may hold values from -0.25 to 0.25
- conv_decode: bfloat16 [3, 64, 384], replicated, may hold values from -0.1875 to 0.1875
- output_head: bfloat16 [12, 64], replicated, may hold values from -0.75 to 0.75
- ocean_in: float32 [64, 6], replicated, may hold values from -2.5 to 2.5
- ocean_out: float32 [64], replicated, may hold values from -0.75 to 0.75
Outputs:
- atmos_next: bfloat16 [8, 12, 256, 256], P(None, 'face', 'tile')
- ocean_next: float32 [4, 32, 64, 2, 256], P('face', 'tile')
The draws below stay inside these ranges and needn't reach their ends.
Inputs may be any that keep to these rules, and one draw needn't show every extreme that they name: `owners`: among the 24 tiles of one face group and stripe (an aligned block of rows) no owner appears more than 2 times, and that bound is reached in some block. `seam_table`: row 4 g + s describes side s of face g. Column 0 names the partner side 4 h + u; the pairing is an involution with no fixed points, and paired sides carry the same reversal flag in column 1 (0 or 1).
All inputs are finite; a program needn't handle non-finite values. No bound on the sum of `land_sea` on one device may be relied on, other than what follows from the above.
Results may differ from the reference program's by a relative error of at most 0.0028.
Values may be sent and summed in bfloat16 or wider, within the bound.
A program may use at most 64 MiB of HBM per device.

```python
import math
import jax
import jax.numpy as jnp
import numpy as np
from jax import lax

WIDTH = 64
IN_CH = 32
OUT_VARS = 8
FLUX_CH = 4
OCEAN_CH = 2
OCEAN_HID = 64
FACES = 12
GROUPS = 4
STRIPES = 32
SIDE = 256
TILES_DEV = 24
SEND_CAP = 2
SLOTS = 64
ROUTE_ROWS = 3072


def draw_seam_table(key, part):
    base_key = jax.random.fold_in(key, 7)
    key_order, key_flip = jax.random.split(base_key)
    side_count = 4 * FACES
    shuffled = jax.random.permutation(key_order, side_count).astype(jnp.int32)
    paired = shuffled.reshape(side_count // 2, 2)
    flip_bits = jax.random.randint(key_flip, (side_count // 2,), 0, 2).astype(jnp.int32)
    partner = jnp.zeros((side_count,), jnp.int32).at[paired[:, 0]].set(paired[:, 1]).at[paired[:, 1]].set(paired[:, 0])
    reverse = jnp.zeros((side_count,), jnp.int32).at[paired[:, 0]].set(flip_bits).at[paired[:, 1]].set(flip_bits)
    return jnp.stack([partner, reverse], axis=1)


def set_ends(drawn, stream_key, least, largest):
    dims = drawn.shape
    index_at = [jax.random.randint(jax.random.fold_in(stream_key, axis), (), 0, dims[axis]) for axis in range(len(dims))]
    drawn = drawn.at[tuple(index_at)].set(least)
    longest = dims.index(max(dims))
    index_at[longest] = (index_at[longest] + 1) % dims[longest]
    return drawn.at[tuple(index_at)].set(largest)


def steps_of(own_key, shape, cuts, least, high):
    factor_of, own = 1.0, jax.random.fold_in(own_key, 6)
    for position, parts in cuts:
        draws = jnp.exp(jax.random.uniform(jax.random.fold_in(own, position), (parts,), jnp.float32, least / len(cuts), high / len(cuts)))
        factor_of = factor_of * jnp.repeat(draws, shape[position] // parts).reshape([-1 if axis == position else 1 for axis in range(len(shape))])
    return factor_of


def assign_block(stream_key, own, number, rows, count, top, bound, skew):
    ranking = jax.random.permutation(stream_key, count)
    heavy_load, common = portions_of(count, rows * top, bound, skew, True), portions_of(count, rows * top, bound, skew, False)
    places = jnp.arange(count)

    def named(tallies, offset_by):
        used = int((tallies > 0).sum())
        fixed = max(1, used // 4)
        passed = fixed + (places - fixed + offset_by * (used - fixed)) % max(1, count - fixed)
        return jnp.zeros((count,), jnp.int32).at[ranking[jnp.where(places < fixed, places, passed)]].set(jnp.asarray(tallies, jnp.int32))

    tallies = jnp.where(number % 4 == 0, named(heavy_load, number // 4), named(common, number - number // 4 - 1))
    mixed = jax.random.permutation(jax.random.fold_in(own, 3), count)
    giver, receiver = mixed[0:count // 2 * 2:2], mixed[1:count // 2 * 2:2]
    slack = jnp.minimum(tallies[giver] - 1, bound - tallies[receiver]) // 2
    slack = jnp.where((giver == ranking[0]) | (receiver == ranking[0]) | (tallies[receiver] == 0), 0, jnp.maximum(slack, 0))
    passed = jax.random.randint(jax.random.fold_in(own, 4), (count // 2,), 0, 1 << 20) % (slack + 1)
    tallies = tallies.at[giver].add(-passed).at[receiver].add(passed)
    items = jnp.searchsorted(jnp.cumsum(tallies), jnp.arange(rows * top), side="right").astype(jnp.int32)
    listing = items.reshape(top, rows).T
    listing = listing[jax.random.permutation(jax.random.fold_in(own, 1), rows)]
    offset_by = jax.random.randint(jax.random.fold_in(own, 2), (rows, 1), 0, top)
    return jnp.take_along_axis(listing, (jnp.arange(top)[None, :] + offset_by) % top, axis=1)


def portions_of(count, total, bound, lean, full):
    portions = [(1 << 20) // math.isqrt(standing ** lean) + 1 for standing in range(1, count + 1)]
    largest = bound if full else min(bound, max(-(-total // count), total * portions[0] // sum(portions)))
    least = 1 if total - largest >= count - 1 else 0
    given, surplus = [largest] + [least] * (count - 1), total - largest - least * (count - 1)
    while surplus > 0:
        candidates = [i for i in range(1, count) if given[i] < largest] or [i for i in range(1, count) if given[i] < bound]
        whole, left = sum([portions[i] for i in candidates]), surplus
        for i in candidates:
            addition = min(bound - given[i], max(1, left * portions[i] // whole), surplus)
            given[i] = given[i] + addition
            surplus = surplus - addition
    return np.array(given)


def noise(own_key, extent, width, reach, cuts=(), held_as=jnp.bfloat16):
    factor_of = steps_of(own_key, extent, cuts, -0.22, 0.18) if cuts else 1.0
    result = jax.random.normal(own_key, extent, jnp.float32) * width * factor_of
    return jnp.minimum(jnp.maximum(result, -reach), reach).astype(held_as)


def setup_inputs(seed: int = 0) -> dict:
    key_of = jax.random.split(jax.random.key(seed), 13)
    atmos_state = noise(key_of[0], (IN_CH, FACES, SIDE, SIDE), 1.0, 6.0, ((1, 4), (2, 32)))
    land_sea = set_ends((jax.random.randint(key_of[1], (FACES, SIDE, SIDE), 0, 10) < 7).astype(jnp.int32), jax.random.fold_in(key_of[1], 1), 0, 1)
    owners_keys = jax.random.split(jax.random.fold_in(key_of[2], 1), ROUTE_ROWS // TILES_DEV)
    owners_turns = jax.random.permutation(jax.random.fold_in(key_of[2], 3), ROUTE_ROWS // TILES_DEV)
    owners = jax.vmap(lambda own, number: assign_block(jax.random.fold_in(key_of[2], 2), own, number, TILES_DEV, STRIPES, 1, SEND_CAP, 2))(owners_keys, owners_turns).reshape((ROUTE_ROWS, 1))
    seam_table = draw_seam_table(jax.random.fold_in(key_of[12], 71), 0)
    ocean_state = noise(key_of[4], (GROUPS, STRIPES, SLOTS, OCEAN_CH, SIDE), 1.0, 6.0, ((0, 4), (1, 32)), jnp.float32)
    conv_input = noise(key_of[5], (3, WIDTH, 3 * IN_CH), (9 * IN_CH) ** -0.5, 0.375)
    conv_encode = noise(key_of[6], (3, WIDTH, 3 * WIDTH), (9 * WIDTH) ** -0.5, 0.25)
    conv_coarse = noise(key_of[7], (3, WIDTH, 3 * WIDTH), (9 * WIDTH) ** -0.5, 0.25)
    conv_decode = noise(key_of[8], (3, WIDTH, 6 * WIDTH), (18 * WIDTH) ** -0.5, 0.1875)
    output_head = noise(key_of[9], (OUT_VARS + FLUX_CH, WIDTH), WIDTH ** -0.5, 0.75)
    ocean_in = noise(key_of[10], (OCEAN_HID, OCEAN_CH + FLUX_CH), (OCEAN_CH + FLUX_CH) ** -0.5, 2.5, (), jnp.float32)
    ocean_out = noise(key_of[11], (OCEAN_HID,), OCEAN_HID ** -0.5, 0.75, (), jnp.float32)
    return {"atmos_state": atmos_state, "land_sea": land_sea, "owners": owners, "seam_table": seam_table, "ocean_state": ocean_state, "conv_input": conv_input, "conv_encode": conv_encode, "conv_coarse": conv_coarse, "conv_decode": conv_decode, "output_head": output_head, "ocean_in": ocean_in, "ocean_out": ocean_out}


def seam_pad(values, seam_table):
    channels, faces, face_side, _ = values.shape
    face_edges = jnp.stack([values[:, :, 0, :], values[:, :, face_side - 1, :], values[:, :, :, 0], values[:, :, :, face_side - 1]], axis=2)
    face_edges = face_edges.reshape(channels, faces * 4, face_side)
    strips = jnp.take(face_edges, seam_table[:, 0], axis=1)
    strips = jnp.where(seam_table[:, 1][None, :, None] == 1, strips[:, :, ::-1], strips)
    strips = strips.reshape(channels, faces, 4, face_side)
    padded = jnp.pad(values, ((0, 0), (0, 0), (1, 1), (1, 1)))
    padded = padded.at[:, :, 0, 1:face_side + 1].set(strips[:, :, 0])
    padded = padded.at[:, :, face_side + 1, 1:face_side + 1].set(strips[:, :, 1])
    padded = padded.at[:, :, 1:face_side + 1, 0].set(strips[:, :, 2])
    padded = padded.at[:, :, 1:face_side + 1, face_side + 1].set(strips[:, :, 3])
    return padded


def conv_layer(padded, weight):
    channels = padded.shape[0]
    face_side = padded.shape[2] - 2

    def one_face(face_index):
        face_plane = lax.dynamic_index_in_dim(padded, face_index, 1, keepdims=False)
        summed = jnp.zeros((weight.shape[1], face_side * face_side), jnp.float32)
        for row_shift in range(3):
            tap_rows = jnp.concatenate([face_plane[:, row_shift:row_shift + face_side, col_shift:col_shift + face_side] for col_shift in range(3)], axis=0)
            summed = summed + jnp.dot(weight[row_shift], tap_rows.reshape(3 * channels, face_side * face_side), preferred_element_type=jnp.float32)
        return jax.nn.gelu(summed).astype(jnp.bfloat16).reshape(-1, face_side, face_side)

    stacked = lax.map(one_face, jnp.arange(padded.shape[1]))
    return jnp.transpose(stacked, (1, 0, 2, 3))


def ocean_update(held_state, arrived_flux, ocean_in, ocean_out):
    stacked = jnp.concatenate([held_state, arrived_flux.astype(jnp.float32)], axis=1)
    hidden = jax.nn.gelu(jnp.einsum('hc,ncs->nhs', ocean_in, stacked, precision=lax.Precision.HIGHEST))
    sea_now = held_state[:, 0] + jnp.einsum('h,nhs->ns', ocean_out, hidden, precision=lax.Precision.HIGHEST)
    return jnp.stack([sea_now, held_state[:, 0]], axis=1)


def reference(atmos_state, land_sea, owners, seam_table, ocean_state, conv_input, conv_encode, conv_coarse, conv_decode, output_head, ocean_in, ocean_out):
    encoded = conv_layer(seam_pad(atmos_state, seam_table), conv_input)
    skip_level = conv_layer(seam_pad(encoded, seam_table), conv_encode)
    channels, faces, face_side, _ = skip_level.shape
    pooled = skip_level.astype(jnp.float32).reshape(channels, faces, face_side // 2, 2, face_side // 2, 2).mean(axis=(3, 5)).astype(jnp.bfloat16)
    coarse_out = conv_layer(seam_pad(pooled, seam_table), conv_coarse)
    widened = jnp.repeat(jnp.repeat(coarse_out, 2, axis=2), 2, axis=3)
    decoded = conv_layer(seam_pad(jnp.concatenate([skip_level, widened], axis=0), seam_table), conv_decode)
    head_out = jnp.dot(output_head, decoded.reshape(channels, -1), preferred_element_type=jnp.float32).reshape(-1, faces, face_side, face_side)
    predicted = atmos_state[:OUT_VARS].astype(jnp.float32) + head_out[:OUT_VARS]
    is_ocean = land_sea == 1
    fluxes = jnp.where(is_ocean[None], head_out[OUT_VARS:], 0.0).astype(jnp.bfloat16)
    faces_dev = faces // GROUPS
    stripe_rows = face_side // STRIPES
    tiles_dev = faces_dev * stripe_rows
    flux_tiles = fluxes.reshape(FLUX_CH, GROUPS, faces_dev, STRIPES, stripe_rows, face_side)
    flux_tiles = jnp.transpose(flux_tiles, (1, 3, 2, 4, 0, 5)).reshape(GROUPS, STRIPES, tiles_dev, FLUX_CH * face_side)
    owner_ids = owners.reshape(GROUPS, STRIPES, tiles_dev)
    slot_count = ocean_state.shape[2]
    capacity = slot_count // STRIPES
    owner_hits = (owner_ids[..., None] == jnp.arange(STRIPES)[None, None, None, :]).astype(jnp.int32)
    slot_rank = jnp.sum((jnp.cumsum(owner_hits, axis=2) - 1) * owner_hits, axis=3)
    slot_index = owner_ids * capacity + slot_rank
    selector = (slot_index[:, :, None, :] == jnp.arange(slot_count)[None, None, :, None]).astype(jnp.float32)
    outgoing = jnp.einsum('gtnk,gtkc->gtnc', selector, flux_tiles.astype(jnp.float32))
    outgoing = outgoing.reshape(GROUPS, STRIPES, STRIPES, capacity, FLUX_CH, face_side)
    arrived = jnp.transpose(outgoing, (0, 2, 1, 3, 4, 5)).reshape(GROUPS * STRIPES, slot_count, FLUX_CH, face_side).astype(jnp.bfloat16)
    held_blocks = ocean_state.reshape(GROUPS * STRIPES, slot_count, OCEAN_CH, face_side)
    renewed = lax.map(lambda pair: ocean_update(pair[0], pair[1], ocean_in, ocean_out), (held_blocks, arrived))
    renewed = renewed.reshape(GROUPS, STRIPES, slot_count, OCEAN_CH, face_side)
    sea_slots = renewed[:, :, :, 0, :].astype(jnp.bfloat16).reshape(GROUPS, STRIPES, STRIPES, capacity, face_side)
    returned = jnp.transpose(sea_slots, (0, 2, 1, 3, 4)).reshape(GROUPS, STRIPES, slot_count, face_side)
    sea_tiles = jnp.einsum('gtnk,gtns->gtks', selector, returned.astype(jnp.float32))
    sea_temp = sea_tiles.reshape(GROUPS, STRIPES, faces_dev, stripe_rows, face_side)
    sea_temp = jnp.transpose(sea_temp, (0, 2, 1, 3, 4)).reshape(faces, face_side, face_side)
    surface = jnp.where(is_ocean, sea_temp, predicted[0])
    atmos_next = jnp.concatenate([surface[None], predicted[1:]], axis=0).astype(jnp.bfloat16)
    return atmos_next, renewed
```

```python
import functools

import jax
import jax.numpy as jnp
from jax import lax
from jax.experimental import pallas as pl
from jax.experimental.pallas import tpu as pltpu
from jax.sharding import PartitionSpec as P

MESH = pl.DeviceIdType.MESH
BF = jnp.bfloat16
F32 = jnp.float32
C = 64
OUT_VARS = 8
FLUX_CH = 4
OCEAN_CH = 2
NT = (((1,), (1,)), ((), ()))
TN = (((0,), (0,)), ((), ()))

HALO_SEND, HALO_UP, HALO_DOWN, SCAT_SEND, SCAT_TOP, SCAT_BOT = range(6)
TAB_SEND, TAB_RECV, PICK_SEND, PICK_RECV, SEM_COLS = 6, 7, 8, 10, 12
HALO_DOWN_SEND = 11


def iota(shape, dim):
    return lax.broadcasted_iota(jnp.int32, shape, dim)


def drain(ref, sem):
    pltpu.make_async_copy(ref, ref, sem).wait()


class Level:
    def __init__(self, rows, side, body, sems, bufs, sel):
        self.rows, self.side, self.body, self.sems = rows, side, body, sems
        self.scat, self.scat_in, self.tab, self.tabs, self.pick, self.gath = bufs
        self.sel = sel


def kernel(
    groups,
    tiles,
    rows,
    faces,
    seam_ref,
    inv_ref,
    slot_ref,
    atmos_ref,
    land_ref,
    held_ref,
    w1_ref,
    w2_ref,
    w3_ref,
    w4_ref,
    w5_ref,
    head_ref,
    oin_ref,
    oout_ref,
    out_ref,
    sea_ref,
    body1,
    body2,
    body3,
    bodys,
    body4,
    bodyc,
    sel_f,
    sel_c,
    up_mat,
    down_mat,
    pred,
    flux,
    visit,
    sea_out,
    sea_in,
    *rest,
):
    bufs, (sems, misc) = rest[:-2], rest[-2:]
    f = lax.axis_index("face")
    t = lax.axis_index("tile")
    side = rows * tiles
    half_rows, half_side = rows // 2, side // 2
    is_top, is_bot = t == 0, t == tiles - 1
    last = tiles - 1

    load = pltpu.make_async_copy(
        atmos_ref, body1.at[:, pl.ds(C, rows * C), pl.ds(0, side)], misc.at[0]
    )
    load.start()

    levels = []
    for number, (n, s, body, sel) in enumerate(
        (
            (rows, side, body1, sel_f),
            (rows, side, body2, sel_f),
            (half_rows, half_side, body3, sel_c),
            (rows, side, bodys, sel_f),
            (half_rows, half_side, body4, sel_c),
        )
    ):
        levels.append(Level(n, s, body, sems.at[number], bufs[6 * number : 6 * number + 6], sel))

    for n, s, sel in ((rows, side, sel_f), (half_rows, half_side, sel_c)):
        shape = (tiles * 16, s)
        q, x = iota(shape, 0), iota(shape, 1)
        k = q % 16
        cell = (q // 16) * n + k - 1
        inner = (k >= 1) & (k <= n)
        sel[0] = jnp.where((x == cell) & (k <= n + 1), 1.0, 0.0).astype(BF)
        sel[1] = jnp.where((x == cell) & inner, 1.0, 0.0).astype(BF)
        sel[2] = jnp.where((x == s - 1 - cell) & inner, 1.0, 0.0).astype(BF)
    shape = (half_side, side)
    up_mat[...] = jnp.where(iota(shape, 1) // 2 == iota(shape, 0), 1.0, 0.0).astype(BF)
    shape = (side, half_side)
    down_mat[...] = jnp.where(iota(shape, 0) // 2 == iota(shape, 1), 0.25, 0.0).astype(BF)

    barrier = pltpu.get_barrier_semaphore()

    def greet(d, carry):
        peer = lax.rem(t + d, tiles)
        pl.semaphore_signal(barrier, inc=1, device_id=(f, peer), device_id_type=MESH)
        return carry

    lax.fori_loop(1, tiles, greet, 0)
    for d in range(1, groups):
        g = lax.rem(f + d, groups)
        pl.semaphore_signal(barrier, inc=1, device_id=(g, t), device_id_type=MESH)
        pl.semaphore_signal(barrier, inc=1, device_id=(g, last - t), device_id_type=MESH)
    pl.semaphore_wait(barrier, tiles - 1 + 2 * (groups - 1))

    def remote(src, dst, send, recv, device):
        return pltpu.make_async_remote_copy(
            src_ref=src,
            dst_ref=dst,
            send_sem=send,
            recv_sem=recv,
            device_id=device,
            device_id_type=MESH,
        )

    def halo_up(lv):
        n, s = lv.rows, lv.side
        return remote(
            lv.body.at[:, pl.ds(C, C), pl.ds(0, s)],
            lv.body.at[:, pl.ds((n + 1) * C, C), pl.ds(0, s)],
            lv.sems.at[HALO_SEND],
            lv.sems.at[HALO_DOWN],
            (f, jnp.maximum(t - 1, 0)),
        )

    def halo_down(lv):
        n, s = lv.rows, lv.side
        return remote(
            lv.body.at[:, pl.ds(n * C, C), pl.ds(0, s)],
            lv.body.at[:, pl.ds(0, C), pl.ds(0, s)],
            lv.sems.at[HALO_DOWN_SEND],
            lv.sems.at[HALO_UP],
            (f, jnp.minimum(t + 1, last)),
        )

    def scatter_piece(lv, which, dst):
        return remote(
            lv.scat.at[dst],
            lv.scat_in.at[which],
            lv.sems.at[SCAT_SEND],
            lv.sems.at[SCAT_TOP + which],
            (f, dst),
        )

    def begin_rows(lv):
        n, s = lv.rows, lv.side

        @pl.when(jnp.logical_not(is_top))
        def _():
            halo_up(lv).start()

        @pl.when(jnp.logical_not(is_bot))
        def _():
            halo_down(lv).start()

        for which, cond in ((0, is_top), (1, is_bot)):

            @pl.when(cond)
            def _(which=which):
                for j in range(faces):
                    start = C if which == 0 else n * C
                    edge = lv.body[j, pl.ds(start, C), pl.ds(0, s)]
                    zero = jnp.zeros_like(edge)
                    both = jnp.concatenate([edge, zero] if which == 0 else [zero, edge], axis=0)
                    piece = lax.dot_general(
                        lv.sel[0], both, NT, preferred_element_type=F32
                    ).astype(BF)
                    lv.scat[:, j] = piece.reshape(tiles, 16, 2 * C)
                own = 0 if which == 0 else last
                lv.scat_in[which] = lv.scat[own]

                def send(d, carry):
                    scatter_piece(lv, which, lax.rem(own + d, tiles)).start()
                    return carry

                lax.fori_loop(1, tiles, send, 0)

    def end_rows(lv):
        @pl.when(jnp.logical_not(is_top))
        def _():
            drain(lv.body.at[:, pl.ds(0, C), pl.ds(0, lv.side)], lv.sems.at[HALO_UP])
            drain(lv.scat_in.at[0], lv.sems.at[SCAT_TOP])

        @pl.when(jnp.logical_not(is_bot))
        def _():
            n = lv.rows
            drain(lv.body.at[:, pl.ds((n + 1) * C, C), pl.ds(0, lv.side)], lv.sems.at[HALO_DOWN])
            drain(lv.scat_in.at[1], lv.sems.at[SCAT_BOT])

    def table_copy(lv, d):
        mirrored = d // groups
        g = lax.rem(f + d % groups, groups)
        peer = last - t if mirrored else t
        width = 2 * faces
        return remote(
            lv.tab,
            lv.tabs.at[pl.ds((mirrored * groups + f) * width, width)],
            lv.sems.at[TAB_SEND],
            lv.sems.at[TAB_RECV],
            (g, peer),
        )

    def begin_tables(lv):
        n, s = lv.rows, lv.side
        shape = (32, s)
        row, lane = iota(shape, 0), iota(shape, 1)

        def one_face(j, carry):
            total = jnp.zeros((32, C), F32)
            for k in range(n + 2):
                pick = ((row == k) & (lane == 0)) | ((row == 16 + k) & (lane == s - 1))
                data = lv.body[j, pl.ds(k * C, C), pl.ds(0, s)]
                if k == 0:
                    data = jnp.where(is_top, jnp.zeros_like(data), data)
                if k == n + 1:
                    data = jnp.where(is_bot, jnp.zeros_like(data), data)
                total += lax.dot_general(
                    jnp.where(pick, 1.0, 0.0).astype(BF), data, NT, preferred_element_type=F32
                )
            lv.tab[2 * j + 1] = jnp.concatenate([total[:16], total[16:]], axis=1).astype(BF)
            lv.tab[2 * j] = lv.scat_in[0, j] + lv.scat_in[1, j]
            return carry

        lax.fori_loop(0, faces, one_face, 0)
        for d in range(1, 2 * groups):
            table_copy(lv, d).start()
        lv.tabs[pl.ds(f * 2 * faces, 2 * faces)] = lv.tab[...]

    def end_tables(lv):
        drain(lv.tabs.at[pl.ds(0, (2 * groups - 1) * 2 * faces)], lv.sems.at[TAB_RECV])

    def row_copy(lv, which):
        return remote(
            lv.pick.at[which],
            lv.gath.at[t],
            lv.sems.at[PICK_SEND + which],
            lv.sems.at[PICK_RECV],
            (f, 0 if which == 0 else last),
        )

    def seam(j, s):
        at = (f * faces + j) * 4 + s
        return seam_ref[at, 0], seam_ref[at, 1]

    def begin_strips(lv):
        for which, cond in ((0, is_top), (1, is_bot)):
            for j in range(faces):
                p, _ = seam(j, which)
                lv.pick[which, j] = lv.tabs[p // 2]

            @pl.when(jnp.logical_not(cond))
            def _(which=which):
                row_copy(lv, which).start()

            @pl.when(cond)
            def _(which=which):
                lv.gath[0 if which == 0 else last] = lv.pick[which]

    def column_strips(lv, j, store):
        n = lv.rows
        shape = (16, 128)
        k, lane = iota(shape, 0), iota(shape, 1)
        total = jnp.zeros((C, 128), F32)
        for s in (2, 3):
            p, rev = seam(j, s)
            piece = lv.tabs[rev * (groups * 2 * faces) + p // 2]
            kk = jnp.where(rev == 1, n + 1 - k, k)
            good = (kk >= jnp.where(is_top, 1, 0)) & (kk <= jnp.where(is_bot, n, n + 1))
            want = (2 * kk + 127) % 128 if s == 2 else 2 * kk
            chosen = jnp.where(good & (lane == want), 1.0, 0.0).astype(BF)
            both = lax.dot_general(piece, chosen, TN, preferred_element_type=F32)
            total += jnp.where(p % 2 == 1, both[C:], both[:C])
        store(j, total)

    def store_columns(lv):
        def store(j, total):
            for k in range(lv.rows + 2):
                lv.body[j, pl.ds(k * C, C), pl.ds(lv.side, 128)] = pltpu.roll(
                    total, (128 - 2 * k) % 128, 1
                ).astype(BF)

        def one_face(j, carry):
            column_strips(lv, j, store)
            return carry

        lax.fori_loop(0, faces, one_face, 0)

    def end_strips(lv):
        n, s = lv.rows, lv.side
        for which, cond in ((0, is_top), (1, is_bot)):

            @pl.when(cond)
            def _(which=which):
                drain(lv.gath.at[pl.ds(0, tiles - 1)], lv.sems.at[PICK_RECV])
                for j in range(faces):
                    p, rev = seam(j, which)
                    pieces = lv.gath[:, j].reshape(tiles * 16, 2 * C)
                    both = lax.dot_general(
                        pieces, lv.sel[1 + rev], TN, preferred_element_type=F32
                    )
                    strip = jnp.where(p % 2 == 1, both[C:], both[:C])
                    at = 0 if which == 0 else (n + 1) * C
                    lv.body[j, pl.ds(at, C), pl.ds(0, s)] = strip.astype(BF)

    def finish_sends(lv):
        n, s = lv.rows, lv.side

        @pl.when(jnp.logical_not(is_top))
        def _():
            halo_up(lv).wait_send()
            row_copy(lv, 0).wait_send()

        @pl.when(jnp.logical_not(is_bot))
        def _():
            halo_down(lv).wait_send()
            row_copy(lv, 1).wait_send()

        @pl.when(is_top | is_bot)
        def _():
            drain(lv.scat.at[pl.ds(0, tiles - 1)], lv.sems.at[SCAT_SEND])

        drain(lv.tabs.at[pl.ds(0, (2 * groups - 1) * 2 * faces)], lv.sems.at[TAB_SEND])

    def taps(product, s):
        wide = s + 128
        mid = product[C : 2 * C, :s]
        left = pltpu.roll(product[:C], 1, 1)[:, :s]
        right = pltpu.roll(product[2 * C :], wide - 1, 1)[:, :s]
        return mid + left + right

    def conv(lv, w_ref, target):
        n, s = lv.rows, lv.side

        def one_row(i, carry):
            j, r = i // n, i % n
            window = lv.body[j, pl.ds(pl.multiple_of(r * C, C), 3 * C), :]
            product = jnp.dot(w_ref[...], window, preferred_element_type=F32)
            made = jax.nn.gelu(taps(product, s)).astype(BF)
            target[j, pl.ds(pl.multiple_of(r * C + C, C), C), pl.ds(0, s)] = made
            return carry

        lax.fori_loop(0, faces * n, one_row, 0)

    def state_copy(d):
        dst = lax.rem(t + d, tiles)
        return remote(
            held_ref.at[pl.ds(2 * dst, 2)],
            visit.at[pl.ds(2 * t, 2)],
            misc.at[1],
            misc.at[2],
            (f, dst),
        )

    def sea_copy(d):
        dst = lax.rem(t + d, tiles)
        return remote(
            sea_out.at[pl.ds(2 * dst, 2)],
            sea_in.at[pl.ds(2 * t, 2)],
            misc.at[3],
            misc.at[4],
            (f, dst),
        )

    def start_all(copy):
        def body(d, carry):
            copy(d).start()
            return carry

        lax.fori_loop(1, tiles, body, 0)

    lv1, lv2, lv3, lvs, lv4 = levels
    load.wait()
    begin_rows(lv1)
    start_all(state_copy)
    visit[pl.ds(2 * t, 2)] = held_ref[pl.ds(2 * t, 2)]

    def exchange(lv):
        end_rows(lv)
        begin_tables(lv)
        end_tables(lv)
        begin_strips(lv)

    exchange(lv1)
    store_columns(lv1)
    end_strips(lv1)
    conv(lv1, w1_ref, body2)

    begin_rows(lv2)
    exchange(lv2)
    store_columns(lv2)
    end_strips(lv2)
    conv(lv2, w2_ref, bodys)

    def pool(i, carry):
        j, q = i // half_rows, i % half_rows
        pair = bodys[j, pl.ds(pl.multiple_of((2 * q + 1) * C, C), 2 * C), pl.ds(0, side)]
        summed = jnp.dot(pair, down_mat[...], preferred_element_type=F32)
        at = pl.ds(pl.multiple_of((q + 1) * C, C), C)
        body3[j, at, pl.ds(0, half_side)] = (summed[:C] + summed[C:]).astype(BF)
        return carry

    lax.fori_loop(0, faces * half_rows, pool, 0)

    begin_rows(lv3)
    begin_rows(lvs)
    exchange(lv3)
    store_columns(lv3)
    end_strips(lv3)
    conv(lv3, w3_ref, body4)

    begin_rows(lv4)
    exchange(lvs)
    store_columns(lvs)
    exchange(lv4)
    end_strips(lvs)

    def store_coarse(j, total):
        for k in range(rows + 2):
            bodyc[j, pl.ds(k * C, C), pl.ds(side, 128)] = pltpu.roll(
                total, (128 - 2 * ((k + 1) // 2)) % 128, 1
            ).astype(BF)

    def coarse_columns(j, carry):
        column_strips(lv4, j, store_coarse)
        return carry

    lax.fori_loop(0, faces, coarse_columns, 0)
    end_strips(lv4)

    def widen(j, carry):
        for q in range(half_rows + 2):
            made = jnp.dot(
                body4[j, pl.ds(q * C, C), :], up_mat[...], preferred_element_type=F32
            ).astype(BF)
            for k in (2 * q - 1, 2 * q):
                if 0 <= k <= rows + 1:
                    bodyc[j, pl.ds(k * C, C), pl.ds(0, side)] = made
        return carry

    lax.fori_loop(0, faces, widen, 0)

    def decode(i, carry):
        j, r = i // rows, i % rows
        window = pl.ds(pl.multiple_of(r * C, C), 3 * C)
        product = jnp.dot(w4_ref[...], bodys[j, window, :], preferred_element_type=F32)
        product += jnp.dot(w5_ref[...], bodyc[j, window, :], preferred_element_type=F32)
        decoded = jax.nn.gelu(taps(product, side)).astype(BF)
        head = jnp.dot(head_ref[...], decoded, preferred_element_type=F32)
        state = body1[j, pl.ds(pl.multiple_of(r * C + C, C), 16), pl.ds(0, side)]
        pred[i] = state[:OUT_VARS].astype(F32) + head[:OUT_VARS]
        ocean = jnp.broadcast_to(land_ref[i] == 1, (8, side))
        flux[i] = jnp.where(ocean, head[OUT_VARS:], 0.0).astype(BF).astype(F32)
        return carry

    lax.fori_loop(0, faces * rows, decode, 0)
    flux[faces * rows] = jnp.zeros((8, side), F32)

    drain(visit.at[pl.ds(0, 2 * (tiles - 1))], misc.at[2])

    def ocean(n, carry):
        old = visit[n]
        stacked = jnp.concatenate([old, jnp.zeros((6, side), F32)], axis=0) + flux[inv_ref[n]]
        hidden = jax.nn.gelu(
            jnp.dot(
                oin_ref[...],
                stacked,
                preferred_element_type=F32,
                precision=lax.Precision.HIGHEST,
            )
        )
        moved = jnp.sum(oout_ref[...] * hidden, axis=0, keepdims=True)
        sea_out[n] = old[:1] + moved
        return carry

    lax.fori_loop(0, 2 * tiles, ocean, 0)
    start_all(sea_copy)
    sea_in[pl.ds(2 * t, 2)] = sea_out[pl.ds(2 * t, 2)]

    def surface(i, carry):
        sea = jnp.broadcast_to(sea_out[slot_ref[i]], (8, side))
        wet = jnp.broadcast_to(land_ref[i] == 1, (8, side)) & (iota((8, side), 0) == 0)
        out_ref[i] = jnp.where(wet, sea, pred[i])
        return carry

    lax.fori_loop(0, faces * rows, surface, 0)
    drain(sea_in.at[pl.ds(0, 2 * (tiles - 1))], misc.at[4])
    sea_ref[...] = sea_in[...]

    for lv in levels:
        finish_sends(lv)
    drain(held_ref.at[pl.ds(0, 2 * (tiles - 1))], misc.at[1])
    drain(sea_out.at[pl.ds(0, 2 * (tiles - 1))], misc.at[3])


def stacked_weight(weight):
    taps, made, wide = weight.shape
    channels = wide // 3
    folded = jnp.transpose(weight.reshape(taps, made, 3, channels), (2, 1, 0, 3))
    if channels < C:
        folded = jnp.pad(folded, ((0, 0), (0, 0), (0, 0), (0, C - channels)))
    pieces = []
    for at in range(0, folded.shape[3], C):
        pieces.append(folded[..., at : at + C].reshape(3 * made, taps * C))
    return pieces


def on_device(
    atmos_state,
    land_sea,
    owners,
    seam_table,
    ocean_state,
    conv_input,
    conv_encode,
    conv_coarse,
    conv_decode,
    output_head,
    ocean_in,
    ocean_out,
):
    channels, faces, rows, side = atmos_state.shape
    groups, tiles = lax.axis_size("face"), lax.axis_size("tile")
    count = faces * rows
    slots = ocean_state.shape[2]
    atmos = jnp.pad(jnp.transpose(atmos_state, (1, 2, 0, 3)), ((0, 0), (0, 0), (0, C - channels), (0, 0)))
    atmos = atmos.reshape(faces, rows * C, side)
    land = land_sea.reshape(count, 1, side)
    owner_ids = owners[:, 0]
    same = owner_ids[:, None] == owner_ids[None, :]
    earlier = jnp.arange(count)[None, :] < jnp.arange(count)[:, None]
    rank = jnp.sum((same & earlier).astype(jnp.int32), axis=1)
    slot = owner_ids * (slots // tiles) + rank
    hits = jnp.arange(slots)[:, None] == slot[None, :]
    inverse = count + jnp.sum(
        jnp.where(hits, jnp.arange(count)[None, :] - count, 0), axis=1
    )
    held = ocean_state[0, 0]
    (w1,) = stacked_weight(conv_input)
    (w2,) = stacked_weight(conv_encode)
    (w3,) = stacked_weight(conv_coarse)
    w4, w5 = stacked_weight(conv_decode)
    gap = jnp.zeros((OCEAN_CH, output_head.shape[1]), output_head.dtype)
    head = jnp.concatenate([output_head[:OUT_VARS], gap, output_head[OUT_VARS:], gap], axis=0)
    oin = jnp.pad(ocean_in, ((0, 0), (0, 8 - ocean_in.shape[1])))
    oout = ocean_out[:, None]

    half_rows, half_side = rows // 2, side // 2
    vmem = pltpu.VMEM
    scratch = [
        vmem((faces, (rows + 2) * C, side + 128), BF),
        vmem((faces, (rows + 2) * C, side + 128), BF),
        vmem((faces, (half_rows + 2) * C, half_side + 128), BF),
        vmem((faces, (rows + 2) * C, side + 128), BF),
        vmem((faces, (half_rows + 2) * C, half_side), BF),
        vmem((faces, (rows + 2) * C, side + 128), BF),
        vmem((3, tiles * 16, side), BF),
        vmem((3, tiles * 16, half_side), BF),
        vmem((half_side, side), BF),
        vmem((side, half_side), BF),
        vmem((count, OUT_VARS, side), F32),
        vmem((count + 1, 8, side), F32),
        vmem((slots, OCEAN_CH, side), F32),
        vmem((slots, 1, side), F32),
        vmem((slots, 1, side), F32),
    ]
    for _ in range(5):
        scratch += [
            vmem((tiles, faces, 16, 2 * C), BF),
            vmem((2, faces, 16, 2 * C), BF),
            vmem((2 * faces, 16, 2 * C), BF),
            vmem((2 * groups * 2 * faces, 16, 2 * C), BF),
            vmem((2, faces, 16, 2 * C), BF),
            vmem((tiles, faces, 16, 2 * C), BF),
        ]
    scratch += [pltpu.SemaphoreType.DMA((5, SEM_COLS)), pltpu.SemaphoreType.DMA((5,))]
    smem = pl.BlockSpec(memory_space=pltpu.SMEM)
    whole = pl.BlockSpec(memory_space=pltpu.VMEM)
    out, sea = pl.pallas_call(
        functools.partial(kernel, groups, tiles, rows, faces),
        out_shape=(
            jax.ShapeDtypeStruct((count, OUT_VARS, side), F32),
            jax.ShapeDtypeStruct((slots, 1, side), F32),
        ),
        in_specs=[smem] * 3 + [pl.BlockSpec(memory_space=pl.ANY)] + [whole] * 10,
        out_specs=(whole, whole),
        scratch_shapes=scratch,
        compiler_params=pltpu.CompilerParams(
            collective_id=0, has_side_effects=True, vmem_limit_bytes=56 * 1024 * 1024
        ),
        name="coupled_step",
    )(
        seam_table, inverse, slot, atmos, land, held, w1, w2, w3, w4, w5, head, oin, oout
    )
    atmos_next = jnp.transpose(out.reshape(faces, rows, OUT_VARS, side), (2, 0, 1, 3)).astype(BF)
    ocean_next = jnp.concatenate([sea, held[:, :1]], axis=1)
    return atmos_next, ocean_next[None, None]


def solution(mesh):
    in_specs = (
        P(None, "face", "tile", None),
        P("face", "tile", None),
        P(("face", "tile"), None),
        P(),
        P("face", "tile", None, None, None),
        P(),
        P(),
        P(),
        P(),
        P(),
        P(),
        P(),
    )
    out_specs = (P(None, "face", "tile", None), P("face", "tile", None, None, None))
    return jax.shard_map(
        on_device, mesh=mesh, in_specs=in_specs, out_specs=out_specs, check_vma=False
    )
```

```python
import functools

import jax
import jax.numpy as jnp
from jax import lax
from jax.experimental import pallas as pl
from jax.experimental.pallas import tpu as pltpu
from jax.sharding import PartitionSpec as P

MESH = pl.DeviceIdType.MESH
BF = jnp.bfloat16
F32 = jnp.float32
C = 64
OUT_VARS = 8
FLUX_CH = 4
OCEAN_CH = 2
NT = (((1,), (1,)), ((), ()))
TN = (((0,), (0,)), ((), ()))

HALO_SEND, HALO_UP, HALO_DOWN, SCAT_SEND, SCAT_TOP, SCAT_BOT = range(6)
TAB_SEND, TAB_RECV, PICK_SEND, PICK_RECV, HALO_DOWN_SEND = 6, 7, 8, 10, 11
MIRROR_SEND, MIRROR_RECV, SEM_COLS = 12, 13, 14


def iota(shape, dim):
    return lax.broadcasted_iota(jnp.int32, shape, dim)


def drain(ref, sem):
    pltpu.make_async_copy(ref, ref, sem).wait()


class Level:
    def __init__(self, rows, side, body, sems, bufs, sel):
        self.rows, self.side, self.body, self.sems = rows, side, body, sems
        self.scat, self.scat_in, self.tab, self.tabs, self.pick, self.gath = bufs[:6]
        self.send, self.mirror = bufs[6:]
        self.sel = sel


def kernel(
    groups,
    tiles,
    rows,
    faces,
    seam_ref,
    inv_ref,
    slot_ref,
    atmos_ref,
    land_ref,
    held_ref,
    w1_ref,
    w2_ref,
    w3_ref,
    w4_ref,
    head_ref,
    oin_ref,
    oout_ref,
    out_ref,
    sea_ref,
    body1,
    body2,
    body3,
    bodys,
    body4,
    bodyc,
    sel_f,
    sel_c,
    up_mat,
    down_mat,
    pred,
    flux,
    visit,
    sea_out,
    sea_in,
    w1,
    w2,
    w3,
    w4,
    w5,
    head,
    oout,
    before,
    idle,
    tile_sea,
    *rest,
):
    bufs, (sems, misc) = rest[:-2], rest[-2:]
    f = lax.axis_index("face")
    t = lax.axis_index("tile")
    side = rows * tiles
    half_rows, half_side = rows // 2, side // 2
    is_top, is_bot = t == 0, t == tiles - 1
    last = tiles - 1

    load = pltpu.make_async_copy(
        atmos_ref, body1.at[:, pl.ds(C, rows * C), pl.ds(0, side)], misc.at[0]
    )
    load.start()

    levels = []
    for number, (n, s, body, sel) in enumerate(
        (
            (rows, side, body1, sel_f),
            (rows, side, body2, sel_f),
            (half_rows, half_side, body3, sel_c),
            (rows, side, bodys, sel_f),
            (half_rows, half_side, body4, sel_c),
        )
    ):
        levels.append(Level(n, s, body, sems.at[number], bufs[8 * number : 8 * number + 8], sel))

    barrier = pltpu.get_barrier_semaphore()

    def greet(d, carry):
        peer = lax.rem(t + d, tiles)
        pl.semaphore_signal(barrier, inc=1, device_id=(f, peer), device_id_type=MESH)
        return carry

    lax.fori_loop(1, tiles, greet, 0)
    for d in range(1, groups):
        g = lax.rem(f + d, groups)
        pl.semaphore_signal(barrier, inc=1, device_id=(g, t), device_id_type=MESH)

    @pl.when(is_top | is_bot)
    def _():
        for n, s, sel in ((rows, side, sel_f), (half_rows, half_side, sel_c)):
            shape = (tiles * 16, s)
            q, x = iota(shape, 0), iota(shape, 1)
            k = q % 16
            start = (q // 16) * n
            sel[0] = jnp.where((x == start + k - 1) & (k <= n + 1), 1.0, 0.0).astype(BF)
            for at, least in ((1, 0), (2, 8)):
                cell = start + k - least
                inner = (k >= least) & (k < least + n)
                sel[at] = jnp.where((x == cell) & inner, 1.0, 0.0).astype(BF)
                sel[at + 2] = jnp.where((x == s - 1 - cell) & inner, 1.0, 0.0).astype(BF)

    shape = (half_side, side)
    up_mat[...] = jnp.where(iota(shape, 1) // 2 == iota(shape, 0), 1.0, 0.0).astype(BF)
    shape = (side, half_side)
    down_mat[...] = jnp.where(iota(shape, 0) // 2 == iota(shape, 1), 0.25, 0.0).astype(BF)

    for target, ref, first, width in (
        (w1, w1_ref, 0, w1_ref.shape[2] // 3),
        (w2, w2_ref, 0, C),
        (w3, w3_ref, 0, C),
        (w4, w4_ref, 0, C),
        (w5, w4_ref, C, C),
    ):
        channels = ref.shape[2] // 3
        for a in range(3):
            whole = ref[a].astype(F32)
            for b in range(3):
                at = b * channels + first
                block = whole[:, at : at + width]
                if width < C:
                    block = jnp.concatenate([block, jnp.zeros((C, C - width), F32)], axis=1)
                target[pl.ds(b * C, C), pl.ds(a * C, C)] = block.astype(BF)
    made = head_ref[...].astype(F32)
    gap = jnp.zeros((2, C), F32)
    head[...] = jnp.concatenate([made[:OUT_VARS], gap, made[OUT_VARS:], gap], axis=0).astype(BF)
    diagonal = iota((C, C), 0) == iota((C, C), 1)
    column = jnp.sum(
        jnp.where(diagonal, jnp.broadcast_to(oout_ref[...], (C, C)), 0.0), axis=1, keepdims=True
    )
    oout[...] = jnp.broadcast_to(column, (C, side))

    load.wait()
    pl.semaphore_wait(barrier, tiles - 1 + groups - 1)

    def remote(src, dst, send, recv, device):
        return pltpu.make_async_remote_copy(
            src_ref=src,
            dst_ref=dst,
            send_sem=send,
            recv_sem=recv,
            device_id=device,
            device_id_type=MESH,
        )

    def halo_up(lv):
        n, s = lv.rows, lv.side
        return remote(
            lv.body.at[:, pl.ds(C, C), pl.ds(0, s)],
            lv.body.at[:, pl.ds((n + 1) * C, C), pl.ds(0, s)],
            lv.sems.at[HALO_SEND],
            lv.sems.at[HALO_DOWN],
            (f, jnp.maximum(t - 1, 0)),
        )

    def halo_down(lv):
        n, s = lv.rows, lv.side
        return remote(
            lv.body.at[:, pl.ds(n * C, C), pl.ds(0, s)],
            lv.body.at[:, pl.ds(0, C), pl.ds(0, s)],
            lv.sems.at[HALO_DOWN_SEND],
            lv.sems.at[HALO_UP],
            (f, jnp.minimum(t + 1, last)),
        )

    def scatter_piece(lv, which, dst):
        return remote(
            lv.scat.at[dst],
            lv.scat_in.at[which],
            lv.sems.at[SCAT_SEND],
            lv.sems.at[SCAT_TOP + which],
            (f, dst),
        )

    def begin_rows(lv):
        n, s = lv.rows, lv.side

        @pl.when(jnp.logical_not(is_top))
        def _():
            halo_up(lv).start()

        @pl.when(jnp.logical_not(is_bot))
        def _():
            halo_down(lv).start()

        for which, cond in ((0, is_top), (1, is_bot)):

            @pl.when(cond)
            def _(which=which):
                for j in range(faces):
                    start = C if which == 0 else n * C
                    edge = lv.body[j, pl.ds(start, C), pl.ds(0, s)]
                    zero = jnp.zeros_like(edge)
                    both = jnp.concatenate([edge, zero] if which == 0 else [zero, edge], axis=0)
                    piece = lax.dot_general(
                        lv.sel[0], both, NT, preferred_element_type=F32
                    ).astype(BF)
                    lv.scat[:, j] = piece.reshape(tiles, 16, 2 * C)
                own = 0 if which == 0 else last
                lv.scat_in[which] = lv.scat[own]

                def send(d, carry):
                    scatter_piece(lv, which, lax.rem(own + d, tiles)).start()
                    return carry

                lax.fori_loop(1, tiles, send, 0)

    def end_rows(lv):
        @pl.when(jnp.logical_not(is_top))
        def _():
            drain(lv.body.at[:, pl.ds(0, C), pl.ds(0, lv.side)], lv.sems.at[HALO_UP])
            drain(lv.scat_in.at[0], lv.sems.at[SCAT_TOP])

        @pl.when(jnp.logical_not(is_bot))
        def _():
            n = lv.rows
            drain(lv.body.at[:, pl.ds((n + 1) * C, C), pl.ds(0, lv.side)], lv.sems.at[HALO_DOWN])
            drain(lv.scat_in.at[1], lv.sems.at[SCAT_BOT])

    def table_copy(lv, d):
        width = 2 * faces
        return remote(
            lv.tab,
            lv.tabs.at[pl.ds(f * width, width)],
            lv.sems.at[TAB_SEND],
            lv.sems.at[TAB_RECV],
            (lax.rem(f + d, groups), t),
        )

    def begin_tables(lv):
        n, s = lv.rows, lv.side
        shape = (32, s)
        row, lane = iota(shape, 0), iota(shape, 1)

        def one_face(j, carry):
            total = jnp.zeros((32, C), F32)
            for k in range(n + 2):
                pick = ((row == k) & (lane == 0)) | ((row == 16 + k) & (lane == s - 1))
                data = lv.body[j, pl.ds(k * C, C), pl.ds(0, s)]
                if k == 0:
                    data = jnp.where(is_top, jnp.zeros_like(data), data)
                if k == n + 1:
                    data = jnp.where(is_bot, jnp.zeros_like(data), data)
                total += lax.dot_general(
                    jnp.where(pick, 1.0, 0.0).astype(BF), data, NT, preferred_element_type=F32
                )
            lv.tab[2 * j + 1] = jnp.concatenate([total[:16], total[16:]], axis=1).astype(BF)
            lv.tab[2 * j] = lv.scat_in[0, j] + lv.scat_in[1, j]
            return carry

        lax.fori_loop(0, faces, one_face, 0)
        for d in range(1, groups):
            table_copy(lv, d).start()
        lv.tabs[pl.ds(f * 2 * faces, 2 * faces)] = lv.tab[...]

    def end_tables(lv):
        drain(lv.tabs.at[pl.ds(0, (groups - 1) * 2 * faces)], lv.sems.at[TAB_RECV])

    def row_copy(lv, which):
        return remote(
            lv.send.at[which],
            lv.gath.at[t],
            lv.sems.at[PICK_SEND + which],
            lv.sems.at[PICK_RECV],
            (f, 0 if which == 0 else last),
        )

    def mirror_copy(lv):
        return remote(
            lv.pick, lv.mirror, lv.sems.at[MIRROR_SEND], lv.sems.at[MIRROR_RECV], (f, last - t)
        )

    def seam(j, s):
        at = (f * faces + j) * 4 + s
        return seam_ref[0, at], seam_ref[1, at]

    def begin_strips(lv):
        n = lv.rows
        shape = (16, 16)
        r, k = iota(shape, 0), iota(shape, 1)
        low = jnp.where((k == r + 1) & (r < n), 1.0, 0.0).astype(BF)
        high = jnp.where((k == r - 7) & (r >= 8) & (r < 8 + n), 1.0, 0.0).astype(BF)
        for which, cond in ((0, is_top), (1, is_bot)):
            parts = []
            for j in range(faces):
                p, _ = seam(j, which)
                spread = jnp.dot(
                    high if j == 2 else low, lv.tabs[p // 2], preferred_element_type=F32
                )
                parts.append(jnp.where(p % 2 == 1, spread[:, C:], spread[:, :C]))
            lv.send[which] = jnp.concatenate([parts[0] + parts[2], parts[1]], axis=1).astype(BF)

            @pl.when(jnp.logical_not(cond))
            def _(which=which):
                row_copy(lv, which).start()

            @pl.when(cond)
            def _(which=which):
                lv.gath[0 if which == 0 else last] = lv.send[which]

        for s in (2, 3):
            for j in range(faces):
                p, _ = seam(j, s)
                lv.pick[s - 2, j] = lv.tabs[p // 2]
        mirror_copy(lv).start()

    def column_strips(lv, j, store):
        n = lv.rows
        shape = (16, 128)
        k, lane = iota(shape, 0), iota(shape, 1)
        total = jnp.zeros((C, 128), F32)
        for s in (2, 3):
            p, rev = seam(j, s)
            piece = jnp.where(rev == 1, lv.mirror[s - 2, j], lv.pick[s - 2, j])
            kk = jnp.where(rev == 1, n + 1 - k, k)
            good = (kk >= jnp.where(is_top, 1, 0)) & (kk <= jnp.where(is_bot, n, n + 1))
            want = (2 * kk + 127) % 128 if s == 2 else 2 * kk
            chosen = jnp.where(good & (lane == want), 1.0, 0.0).astype(BF)
            both = lax.dot_general(piece, chosen, TN, preferred_element_type=F32)
            total += jnp.where(p % 2 == 1, both[C:], both[:C])
        store(j, total)

    def end_mirror(lv):
        drain(lv.mirror, lv.sems.at[MIRROR_RECV])

    def store_columns(lv):
        end_mirror(lv)

        def store(j, total):
            for k in range(lv.rows + 2):
                lv.body[j, pl.ds(k * C, C), pl.ds(lv.side, 128)] = pltpu.roll(
                    total, (128 - 2 * k) % 128, 1
                ).astype(BF)

        def one_face(j, carry):
            column_strips(lv, j, store)
            return carry

        lax.fori_loop(0, faces, one_face, 0)

    def end_strips(lv):
        n, s = lv.rows, lv.side
        for which, cond in ((0, is_top), (1, is_bot)):

            @pl.when(cond)
            def _(which=which):
                drain(lv.gath.at[pl.ds(0, tiles - 1)], lv.sems.at[PICK_RECV])
                for j in range(faces):
                    _, rev = seam(j, which)
                    pieces = lv.gath[...].reshape(tiles * 16, 2 * C)
                    chosen = lv.sel[(2 if j == 2 else 1) + 2 * rev]
                    both = lax.dot_general(pieces, chosen, TN, preferred_element_type=F32)
                    strip = both[C:] if j == 1 else both[:C]
                    at = 0 if which == 0 else (n + 1) * C
                    lv.body[j, pl.ds(at, C), pl.ds(0, s)] = strip.astype(BF)

    def finish_sends(lv):
        n, s = lv.rows, lv.side

        @pl.when(jnp.logical_not(is_top))
        def _():
            halo_up(lv).wait_send()
            row_copy(lv, 0).wait_send()

        @pl.when(jnp.logical_not(is_bot))
        def _():
            halo_down(lv).wait_send()
            row_copy(lv, 1).wait_send()

        @pl.when(is_top | is_bot)
        def _():
            drain(lv.scat.at[pl.ds(0, tiles - 1)], lv.sems.at[SCAT_SEND])

        drain(lv.tabs.at[pl.ds(0, (groups - 1) * 2 * faces)], lv.sems.at[TAB_SEND])
        mirror_copy(lv).wait_send()

    def taps(product, s):
        wide = s + 128
        mid = product[C : 2 * C, :s]
        left = pltpu.roll(product[:C], 1, 1)[:, :s]
        right = pltpu.roll(product[2 * C :], wide - 1, 1)[:, :s]
        return mid + left + right

    def conv(lv, w_ref, target):
        n, s = lv.rows, lv.side

        def one_row(i, carry):
            j, r = i // n, i % n
            window = lv.body[j, pl.ds(pl.multiple_of(r * C, C), 3 * C), :]
            product = jnp.dot(w_ref[...], window, preferred_element_type=F32)
            made = jax.nn.gelu(taps(product, s)).astype(BF)
            target[j, pl.ds(pl.multiple_of(r * C + C, C), C), pl.ds(0, s)] = made
            return carry

        lax.fori_loop(0, faces * n, one_row, 0)

    def state_copy(d):
        dst = lax.rem(t + d, tiles)
        return remote(
            held_ref.at[pl.ds(2 * dst, 2)],
            visit.at[pl.ds(2 * t, 2)],
            misc.at[1],
            misc.at[2],
            (f, dst),
        )

    def sea_copy(d):
        dst = lax.rem(t + d, tiles)
        return remote(
            sea_out.at[pl.ds(2 * dst, 2)],
            sea_in.at[pl.ds(2 * t, 2)],
            misc.at[3],
            misc.at[4],
            (f, dst),
        )

    def start_all(copy):
        def body(d, carry):
            copy(d).start()
            return carry

        lax.fori_loop(1, tiles, body, 0)

    lv1, lv2, lv3, lvs, lv4 = levels
    begin_rows(lv1)
    start_all(state_copy)
    visit[pl.ds(2 * t, 2)] = held_ref[pl.ds(2 * t, 2)]

    def exchange(lv):
        end_rows(lv)
        begin_tables(lv)
        end_tables(lv)
        begin_strips(lv)

    def early_ocean():
        drain(visit.at[pl.ds(0, 2 * (tiles - 1))], misc.at[2])
        w_a = jnp.broadcast_to(oin_ref[:, 0:1], (C, side))
        w_b = jnp.broadcast_to(oin_ref[:, 1:2], (C, side))

        def one_slot(n, carry):
            old = visit[n]
            total = w_a * old[:1] + w_b * old[1:]
            before[n] = total
            moved = jnp.sum(oout[...] * jax.nn.gelu(total), axis=0, keepdims=True)
            idle[n] = old[:1] + moved
            return carry

        lax.fori_loop(0, 2 * tiles, one_slot, 0)

    exchange(lv1)
    early_ocean()
    store_columns(lv1)
    end_strips(lv1)
    conv(lv1, w1, body2)

    begin_rows(lv2)
    exchange(lv2)
    store_columns(lv2)
    end_strips(lv2)
    conv(lv2, w2, bodys)

    def pool(i, carry):
        j, q = i // half_rows, i % half_rows
        pair = bodys[j, pl.ds(pl.multiple_of((2 * q + 1) * C, C), 2 * C), pl.ds(0, side)]
        summed = jnp.dot(pair, down_mat[...], preferred_element_type=F32)
        at = pl.ds(pl.multiple_of((q + 1) * C, C), C)
        body3[j, at, pl.ds(0, half_side)] = (summed[:C] + summed[C:]).astype(BF)
        return carry

    lax.fori_loop(0, faces * half_rows, pool, 0)

    begin_rows(lv3)
    begin_rows(lvs)
    exchange(lv3)
    store_columns(lv3)
    end_strips(lv3)
    conv(lv3, w3, body4)

    begin_rows(lv4)
    exchange(lvs)
    store_columns(lvs)
    exchange(lv4)
    end_strips(lvs)

    def store_coarse(j, total):
        for k in range(rows + 2):
            bodyc[j, pl.ds(k * C, C), pl.ds(side, 128)] = pltpu.roll(
                total, (128 - 2 * ((k + 1) // 2)) % 128, 1
            ).astype(BF)

    def coarse_columns(j, carry):
        column_strips(lv4, j, store_coarse)
        return carry

    end_mirror(lv4)
    lax.fori_loop(0, faces, coarse_columns, 0)
    end_strips(lv4)

    def widen(j, carry):
        for q in range(half_rows + 2):
            made = jnp.dot(
                body4[j, pl.ds(q * C, C), :], up_mat[...], preferred_element_type=F32
            ).astype(BF)
            for k in (2 * q - 1, 2 * q):
                if 0 <= k <= rows + 1:
                    bodyc[j, pl.ds(k * C, C), pl.ds(0, side)] = made
        return carry

    lax.fori_loop(0, faces, widen, 0)

    def decode(i, carry):
        j, r = i // rows, i % rows
        window = pl.ds(pl.multiple_of(r * C, C), 3 * C)
        product = jnp.dot(w4[...], bodys[j, window, :], preferred_element_type=F32)
        product += jnp.dot(w5[...], bodyc[j, window, :], preferred_element_type=F32)
        decoded = jax.nn.gelu(taps(product, side)).astype(BF)
        out = jnp.dot(head[...], decoded, preferred_element_type=F32)
        state = body1[j, pl.ds(pl.multiple_of(r * C + C, C), 16), pl.ds(0, side)]
        pred[i] = state[:OUT_VARS].astype(F32) + out[:OUT_VARS]
        wet = jnp.broadcast_to(land_ref[j, pl.ds(r, 1), :] == 1, (8, side))
        flux[i] = jnp.where(wet, out[OUT_VARS:], 0.0).astype(BF)
        return carry

    lax.fori_loop(0, faces * rows, decode, 0)

    flux_in = jnp.concatenate(
        [jnp.zeros((C, 2), F32), oin_ref[:, OCEAN_CH:], jnp.zeros((C, 2), F32)], axis=1
    )
    first = flux_in.astype(BF)
    second = (flux_in - first.astype(F32)).astype(BF)
    third = (flux_in - first.astype(F32) - second.astype(F32)).astype(BF)
    split = jnp.concatenate([first, second, third], axis=0)

    def ocean(i, carry):
        slot = slot_ref[i]
        parts = jnp.dot(split, flux[i], preferred_element_type=F32)
        hidden = jax.nn.gelu(
            before[slot] + (parts[:C] + (parts[C : 2 * C] + parts[2 * C :]))
        )
        moved = jnp.sum(oout[...] * hidden, axis=0, keepdims=True)
        tile_sea[i] = visit[slot][:1] + moved
        return carry

    lax.fori_loop(0, faces * rows, ocean, 0)

    def fill(n, carry):
        tile = inv_ref[n]
        used = tile < faces * rows
        sea_out[n] = jnp.where(used, tile_sea[jnp.where(used, tile, 0)], idle[n])
        return carry

    lax.fori_loop(0, 2 * tiles, fill, 0)
    start_all(sea_copy)
    sea_in[pl.ds(2 * t, 2)] = sea_out[pl.ds(2 * t, 2)]

    def surface(i, carry):
        sea = jnp.broadcast_to(tile_sea[i], (8, side))
        wet = jnp.broadcast_to(land_ref[i // rows, pl.ds(i % rows, 1), :] == 1, (8, side))
        wet = wet & (iota((8, side), 0) == 0)
        out_ref[i] = jnp.where(wet, sea, pred[i])
        return carry

    lax.fori_loop(0, faces * rows, surface, 0)
    drain(sea_in.at[pl.ds(0, 2 * (tiles - 1))], misc.at[4])
    sea_ref[...] = sea_in[...]

    for lv in levels:
        finish_sends(lv)
    drain(held_ref.at[pl.ds(0, 2 * (tiles - 1))], misc.at[1])
    drain(sea_out.at[pl.ds(0, 2 * (tiles - 1))], misc.at[3])


def on_device(
    atmos_state,
    land_sea,
    owners,
    seam_table,
    ocean_state,
    conv_input,
    conv_encode,
    conv_coarse,
    conv_decode,
    output_head,
    ocean_in,
    ocean_out,
):
    channels, faces, rows, side = atmos_state.shape
    groups, tiles = lax.axis_size("face"), lax.axis_size("tile")
    count = faces * rows
    slots = ocean_state.shape[2]
    atmos = jnp.pad(jnp.transpose(atmos_state, (1, 2, 0, 3)), ((0, 0), (0, 0), (0, C - channels), (0, 0)))
    atmos = atmos.reshape(faces, rows * C, side)
    owner_ids = owners[:, 0]
    same = owner_ids[:, None] == owner_ids[None, :]
    earlier = jnp.arange(count)[None, :] < jnp.arange(count)[:, None]
    rank = jnp.sum((same & earlier).astype(jnp.int32), axis=1)
    slot = owner_ids * (slots // tiles) + rank
    hits = jnp.arange(slots)[:, None] == slot[None, :]
    inverse = count + jnp.sum(
        jnp.where(hits, jnp.arange(count)[None, :] - count, 0), axis=1
    )
    held = ocean_state[0, 0]
    half_rows, half_side = rows // 2, side // 2
    vmem = pltpu.VMEM
    scratch = [
        vmem((faces, (rows + 2) * C, side + 128), BF),
        vmem((faces, (rows + 2) * C, side + 128), BF),
        vmem((faces, (half_rows + 2) * C, half_side + 128), BF),
        vmem((faces, (rows + 2) * C, side + 128), BF),
        vmem((faces, (half_rows + 2) * C, half_side), BF),
        vmem((faces, (rows + 2) * C, side + 128), BF),
        vmem((5, tiles * 16, side), BF),
        vmem((5, tiles * 16, half_side), BF),
        vmem((half_side, side), BF),
        vmem((side, half_side), BF),
        vmem((count, OUT_VARS, side), F32),
        vmem((count, 8, side), BF),
        vmem((slots, OCEAN_CH, side), F32),
        vmem((slots, 1, side), F32),
        vmem((slots, 1, side), F32),
    ]
    scratch += [vmem((3 * C, 3 * C), BF)] * 5
    scratch += [
        vmem((16, C), BF),
        vmem((C, side), F32),
        vmem((slots, C, side), F32),
        vmem((slots, 1, side), F32),
        vmem((count, 1, side), F32),
    ]
    for _ in range(5):
        scratch += [
            vmem((tiles, faces, 16, 2 * C), BF),
            vmem((2, faces, 16, 2 * C), BF),
            vmem((2 * faces, 16, 2 * C), BF),
            vmem((groups * 2 * faces, 16, 2 * C), BF),
            vmem((2, faces, 16, 2 * C), BF),
            vmem((tiles, 16, 2 * C), BF),
            vmem((2, 16, 2 * C), BF),
            vmem((2, faces, 16, 2 * C), BF),
        ]
    scratch += [pltpu.SemaphoreType.DMA((5, SEM_COLS)), pltpu.SemaphoreType.DMA((5,))]
    smem = pl.BlockSpec(memory_space=pltpu.SMEM)
    whole = pl.BlockSpec(memory_space=pltpu.VMEM)
    out, sea = pl.pallas_call(
        functools.partial(kernel, groups, tiles, rows, faces),
        out_shape=(
            jax.ShapeDtypeStruct((count, OUT_VARS, side), F32),
            jax.ShapeDtypeStruct((slots, 1, side), F32),
        ),
        in_specs=[smem] * 3 + [pl.BlockSpec(memory_space=pl.ANY)] + [whole] * 9,
        out_specs=(whole, whole),
        scratch_shapes=scratch,
        compiler_params=pltpu.CompilerParams(
            collective_id=0, has_side_effects=True, vmem_limit_bytes=56 * 1024 * 1024
        ),
        name="coupled_step",
    )(
        seam_table.T,
        inverse,
        slot,
        atmos,
        land_sea,
        held,
        conv_input,
        conv_encode,
        conv_coarse,
        conv_decode,
        output_head,
        ocean_in,
        ocean_out[None],
    )
    atmos_next = jnp.transpose(out.reshape(faces, rows, OUT_VARS, side), (2, 0, 1, 3)).astype(BF)
    ocean_next = jnp.concatenate([sea, held[:, :1]], axis=1)
    return atmos_next, ocean_next[None, None]


def solution(mesh):
    in_specs = (
        P(None, "face", "tile", None),
        P("face", "tile", None),
        P(("face", "tile"), None),
        P(),
        P("face", "tile", None, None, None),
        P(),
        P(),
        P(),
        P(),
        P(),
        P(),
        P(),
    )
    out_specs = (P(None, "face", "tile", None), P("face", "tile", None, None, None))
    return jax.shard_map(
        on_device, mesh=mesh, in_specs=in_specs, out_specs=out_specs, check_vma=False
    )
```

```python
import functools

import jax
import jax.numpy as jnp
from jax import lax
from jax.experimental import pallas as pl
from jax.experimental.pallas import tpu as pltpu
from jax.sharding import PartitionSpec as P

MESH = pl.DeviceIdType.MESH
BF = jnp.bfloat16
F32 = jnp.float32
C = 64
OUT_VARS = 8
FLUX_CH = 4
OCEAN_CH = 2
NT = (((1,), (1,)), ((), ()))
TN = (((0,), (0,)), ((), ()))

HALO_SEND, HALO_UP, HALO_DOWN, SCAT_SEND, SCAT_TOP, SCAT_BOT = range(6)
TAB_SEND, TAB_RECV, PICK_SEND, PICK_RECV, HALO_DOWN_SEND = 6, 7, 8, 10, 11
MIRROR_SEND, MIRROR_RECV, SEM_COLS = 12, 13, 14


def iota(shape, dim):
    return lax.broadcasted_iota(jnp.int32, shape, dim)


def gelu(x):
    inner = x * (0.7978845608028654 + 0.035677408136300125 * (x * x))
    half = 0.5 * x
    return half + half * jnp.tanh(inner)


def drain(ref, sem):
    pltpu.make_async_copy(ref, ref, sem).wait()


class Level:
    def __init__(self, rows, side, body, sems, bufs, sel, edge, strip):
        self.edge, self.strip = edge, strip
        self.rows, self.side, self.body, self.sems = rows, side, body, sems
        self.scat, self.scat_in, self.tab, self.tabs, self.pick, self.gath = bufs[:6]
        self.send, self.mirror = bufs[6:]
        self.sel = sel


def kernel(
    groups,
    tiles,
    rows,
    faces,
    seam_ref,
    inv_ref,
    slot_ref,
    atmos_ref,
    land_ref,
    held_ref,
    w1_ref,
    w2_ref,
    w3_ref,
    w4_ref,
    head_ref,
    oin_ref,
    oout_ref,
    out_ref,
    sea_ref,
    body1,
    body2,
    body3,
    bodys,
    body4,
    bodyc,
    sel_f,
    sel_c,
    up_mat,
    down_mat,
    pred,
    flux,
    visit,
    sea_out,
    sea_in,
    w1,
    w2,
    w3,
    w4,
    w5,
    head,
    oout,
    before,
    idle,
    tile_sea,
    a1,
    a2,
    a3,
    a4,
    a5,
    edges,
    strips,
    edgec,
    made_edge,
    *rest,
):
    bufs, (sems, misc) = rest[:-2], rest[-2:]
    f = lax.axis_index("face")
    t = lax.axis_index("tile")
    side = rows * tiles
    half_rows, half_side = rows // 2, side // 2
    is_top, is_bot = t == 0, t == tiles - 1
    last = tiles - 1

    load = pltpu.make_async_copy(
        atmos_ref, body1.at[:, pl.ds(C, rows * C), pl.ds(0, side)], misc.at[0]
    )
    load.start()

    levels = []
    for number, (n, s, body, sel) in enumerate(
        (
            (rows, side, body1, sel_f),
            (rows, side, body2, sel_f),
            (half_rows, half_side, body3, sel_c),
            (rows, side, bodys, sel_f),
            (half_rows, half_side, body4, sel_c),
        )
    ):
        own = bufs[8 * number : 8 * number + 8]
        levels.append(
            Level(n, s, body, sems.at[number], own, sel, edges.at[number], strips.at[number])
        )

    barrier = pltpu.get_barrier_semaphore()

    def greet(d, carry):
        peer = lax.rem(t + d, tiles)
        pl.semaphore_signal(barrier, inc=1, device_id=(f, peer), device_id_type=MESH)
        return carry

    lax.fori_loop(1, tiles, greet, 0)
    for d in range(1, groups):
        g = lax.rem(f + d, groups)
        pl.semaphore_signal(barrier, inc=1, device_id=(g, t), device_id_type=MESH)

    @pl.when(is_top | is_bot)
    def _():
        for n, s, sel in ((rows, side, sel_f), (half_rows, half_side, sel_c)):
            shape = (tiles * 16, s)
            q, x = iota(shape, 0), iota(shape, 1)
            k = q % 16
            start = (q // 16) * n
            sel[0] = jnp.where((x == start + k - 1) & (k <= n + 1), 1.0, 0.0).astype(BF)
            for at, least in ((1, 0), (2, 8)):
                cell = start + k - least
                inner = (k >= least) & (k < least + n)
                sel[at] = jnp.where((x == cell) & inner, 1.0, 0.0).astype(BF)
                sel[at + 2] = jnp.where((x == s - 1 - cell) & inner, 1.0, 0.0).astype(BF)

    shape = (half_side, side)
    up_mat[...] = jnp.where(iota(shape, 1) // 2 == iota(shape, 0), 1.0, 0.0).astype(BF)
    shape = (side, half_side)
    down_mat[...] = jnp.where(iota(shape, 0) // 2 == iota(shape, 1), 0.25, 0.0).astype(BF)

    for target, along, ref, first, width in (
        (w1, a1, w1_ref, 0, w1_ref.shape[2] // 3),
        (w2, a2, w2_ref, 0, C),
        (w3, a3, w3_ref, 0, C),
        (w4, a4, w4_ref, 0, C),
        (w5, a5, w4_ref, C, C),
    ):
        channels = ref.shape[2] // 3
        for a in range(3):
            whole = ref[a].astype(F32)
            for b in range(3):
                at = b * channels + first
                block = whole[:, at : at + width]
                if width < C:
                    block = jnp.concatenate([block, jnp.zeros((C, C - width), F32)], axis=1)
                target[pl.ds(b * C, C), pl.ds(a * C, C)] = block.astype(BF)
                along[pl.ds(a * C, C), pl.ds(b * C, C)] = block.astype(BF)
    made = head_ref[...].astype(F32)
    gap = jnp.zeros((2, C), F32)
    head[...] = jnp.concatenate([made[:OUT_VARS], gap, made[OUT_VARS:], gap], axis=0).astype(BF)
    diagonal = iota((C, C), 0) == iota((C, C), 1)
    column = jnp.sum(
        jnp.where(diagonal, jnp.broadcast_to(oout_ref[...], (C, C)), 0.0), axis=1, keepdims=True
    )
    oout[...] = jnp.broadcast_to(column, (C, side))

    load.wait()
    pl.semaphore_wait(barrier, tiles - 1 + groups - 1)

    def remote(src, dst, send, recv, device):
        return pltpu.make_async_remote_copy(
            src_ref=src,
            dst_ref=dst,
            send_sem=send,
            recv_sem=recv,
            device_id=device,
            device_id_type=MESH,
        )

    def halo_up(lv):
        n, s = lv.rows, lv.side
        return remote(
            lv.body.at[:, pl.ds(C, C), pl.ds(0, s)],
            lv.body.at[:, pl.ds((n + 1) * C, C), pl.ds(0, s)],
            lv.sems.at[HALO_SEND],
            lv.sems.at[HALO_DOWN],
            (f, jnp.maximum(t - 1, 0)),
        )

    def halo_down(lv):
        n, s = lv.rows, lv.side
        return remote(
            lv.body.at[:, pl.ds(n * C, C), pl.ds(0, s)],
            lv.body.at[:, pl.ds(0, C), pl.ds(0, s)],
            lv.sems.at[HALO_DOWN_SEND],
            lv.sems.at[HALO_UP],
            (f, jnp.minimum(t + 1, last)),
        )

    def scatter_piece(lv, which, dst):
        return remote(
            lv.scat.at[dst],
            lv.scat_in.at[which],
            lv.sems.at[SCAT_SEND],
            lv.sems.at[SCAT_TOP + which],
            (f, dst),
        )

    def begin_rows(lv):
        n, s = lv.rows, lv.side

        @pl.when(jnp.logical_not(is_top))
        def _():
            halo_up(lv).start()

        @pl.when(jnp.logical_not(is_bot))
        def _():
            halo_down(lv).start()

        for which, cond in ((0, is_top), (1, is_bot)):

            @pl.when(cond)
            def _(which=which):
                for j in range(faces):
                    start = C if which == 0 else n * C
                    edge = lv.body[j, pl.ds(start, C), pl.ds(0, s)]
                    zero = jnp.zeros_like(edge)
                    both = jnp.concatenate([edge, zero] if which == 0 else [zero, edge], axis=0)
                    piece = lax.dot_general(
                        lv.sel[0], both, NT, preferred_element_type=F32
                    ).astype(BF)
                    lv.scat[:, j] = piece.reshape(tiles, 16, 2 * C)
                own = 0 if which == 0 else last
                lv.scat_in[which] = lv.scat[own]

                def send(d, carry):
                    scatter_piece(lv, which, lax.rem(own + d, tiles)).start()
                    return carry

                lax.fori_loop(1, tiles, send, 0)

    def end_rows(lv):
        @pl.when(jnp.logical_not(is_top))
        def _():
            drain(lv.body.at[:, pl.ds(0, C), pl.ds(0, lv.side)], lv.sems.at[HALO_UP])
            drain(lv.scat_in.at[0], lv.sems.at[SCAT_TOP])

        @pl.when(jnp.logical_not(is_bot))
        def _():
            n = lv.rows
            drain(lv.body.at[:, pl.ds((n + 1) * C, C), pl.ds(0, lv.side)], lv.sems.at[HALO_DOWN])
            drain(lv.scat_in.at[1], lv.sems.at[SCAT_BOT])

    def table_copy(lv, d):
        width = 2 * faces
        return remote(
            lv.tab,
            lv.tabs.at[pl.ds(f * width, width)],
            lv.sems.at[TAB_SEND],
            lv.sems.at[TAB_RECV],
            (lax.rem(f + d, groups), t),
        )

    lane = iota((C, 128), 1)

    def widened(data, right):
        missing = 128 - data.shape[1]
        if missing <= 0:
            return data
        zero = jnp.zeros((C, missing), data.dtype)
        return jnp.concatenate([zero, data] if right else [data, zero], axis=1)

    def extract(body, edge, s, j, ks, fresh, clear):
        total = jnp.zeros((C, 128), F32) if fresh else edge[j]
        wide = min(s, 128)
        for k in ks:
            here = pl.ds(k * C, C)
            left = widened(body[j, here, pl.ds(0, wide)].astype(F32), False)
            right = widened(body[j, here, pl.ds(s - wide, wide)].astype(F32), True)
            if clear and k == 0:
                left, right = (jnp.where(is_top, 0.0, v) for v in (left, right))
            if clear and k == ks[-1]:
                left, right = (jnp.where(is_bot, 0.0, v) for v in (left, right))
            total = jnp.where(lane // 2 == k, pltpu.roll(left, 2 * k, 1), total)
            total = jnp.where(
                lane // 2 == 32 + k, pltpu.roll(right, (66 + 2 * k) % 128, 1), total
            )
        edge[j] = total
        return total

    def begin_tables(lv):
        n, s = lv.rows, lv.side
        shape = (32, 128)
        row, at = iota(shape, 0), iota(shape, 1)
        want = jnp.where(row < 16, 2 * row, 64 + 2 * (row - 16) + 1)
        pick = jnp.where((at == want) & (row % 16 < n + 2), 1.0, 0.0).astype(BF)

        def one_face(j, carry):
            edge = extract(lv.body, lv.edge, s, j, range(n + 2), True, True)
            total = lax.dot_general(pick, edge.astype(BF), NT, preferred_element_type=F32)
            lv.tab[2 * j + 1] = jnp.concatenate([total[:16], total[16:]], axis=1).astype(BF)
            lv.tab[2 * j] = lv.scat_in[0, j] + lv.scat_in[1, j]
            return carry

        lax.fori_loop(0, faces, one_face, 0)
        for d in range(1, groups):
            table_copy(lv, d).start()
        lv.tabs[pl.ds(f * 2 * faces, 2 * faces)] = lv.tab[...]

    def end_tables(lv):
        drain(lv.tabs.at[pl.ds(0, (groups - 1) * 2 * faces)], lv.sems.at[TAB_RECV])

    def row_copy(lv, which):
        return remote(
            lv.send.at[which],
            lv.gath.at[t],
            lv.sems.at[PICK_SEND + which],
            lv.sems.at[PICK_RECV],
            (f, 0 if which == 0 else last),
        )

    def mirror_copy(lv):
        return remote(
            lv.pick, lv.mirror, lv.sems.at[MIRROR_SEND], lv.sems.at[MIRROR_RECV], (f, last - t)
        )

    def seam(j, s):
        at = (f * faces + j) * 4 + s
        return seam_ref[0, at], seam_ref[1, at]

    def begin_strips(lv):
        n = lv.rows
        shape = (16, 16)
        r, k = iota(shape, 0), iota(shape, 1)
        low = jnp.where((k == r + 1) & (r < n), 1.0, 0.0).astype(BF)
        high = jnp.where((k == r - 7) & (r >= 8) & (r < 8 + n), 1.0, 0.0).astype(BF)
        for which, cond in ((0, is_top), (1, is_bot)):
            parts = []
            for j in range(faces):
                p, _ = seam(j, which)
                spread = jnp.dot(
                    high if j == 2 else low, lv.tabs[p // 2], preferred_element_type=F32
                )
                parts.append(jnp.where(p % 2 == 1, spread[:, C:], spread[:, :C]))
            lv.send[which] = jnp.concatenate([parts[0] + parts[2], parts[1]], axis=1).astype(BF)

            @pl.when(jnp.logical_not(cond))
            def _(which=which):
                row_copy(lv, which).start()

            @pl.when(cond)
            def _(which=which):
                lv.gath[0 if which == 0 else last] = lv.send[which]

        for s in (2, 3):
            for j in range(faces):
                p, _ = seam(j, s)
                lv.pick[s - 2, j] = lv.tabs[p // 2]
        mirror_copy(lv).start()

    def column_strips(lv, fine):
        n = lv.rows
        shape = (16, 128)
        k, at = iota(shape, 0), iota(shape, 1)

        def one_face(j, carry):
            total = jnp.zeros((C, 128), F32)
            for s in (2, 3):
                p, rev = seam(j, s)
                piece = jnp.where(rev == 1, lv.mirror[s - 2, j], lv.pick[s - 2, j])
                kk = jnp.where(rev == 1, n + 1 - k, k)
                good = (kk >= jnp.where(is_top, 1, 0)) & (kk <= jnp.where(is_bot, n, n + 1))
                spot = at if s == 2 else at - 65
                index = (spot // 2 + 1) // 2 if fine else spot // 2
                good = good & (index == kk) & (spot % 2 == 0)
                good = good & ((at < 64) if s == 2 else (at > 64))
                chosen = jnp.where(good, 1.0, 0.0).astype(BF)
                both = lax.dot_general(piece, chosen, TN, preferred_element_type=F32)
                total += jnp.where(p % 2 == 1, both[C:], both[:C])
            lv.strip[j] = total
            return carry

        lax.fori_loop(0, faces, one_face, 0)

    def end_mirror(lv):
        drain(lv.mirror, lv.sems.at[MIRROR_RECV])

    def edge_terms(along, edge, strip):
        near = jnp.where(lane < 64, strip, pltpu.roll(edge, 1, 1))
        far = jnp.where(lane < 64, pltpu.roll(edge, 127, 1), strip)
        stack = jnp.concatenate([near, edge, far], axis=0).astype(BF)
        return jnp.dot(along[...], stack, preferred_element_type=F32)

    def edge_sum(terms):
        return (
            terms[:C]
            + pltpu.roll(terms[C : 2 * C], 126, 1)
            + pltpu.roll(terms[2 * C :], 124, 1)
        )

    def make_edges(lv, along):
        def one_face(j, carry):
            made_edge[j] = gelu(edge_sum(edge_terms(along, lv.edge[j], lv.strip[j])))
            return carry

        lax.fori_loop(0, faces, one_face, 0)

    def patch(s, r, values):
        wide = min(s, 128)
        spot = iota((values.shape[0], wide), 1)
        low = pltpu.roll(values, (128 - 2 * r) % 128, 1)[:, :wide]
        high = pltpu.roll(values, (2 * 128 + wide - 1 - 65 - 2 * r) % 128, 1)[:, :wide]
        return low, high, spot == 0, spot == wide - 1, pl.ds(0, wide), pl.ds(s - wide, wide)

    def fix(lv, target, r_list):
        n, s = lv.rows, lv.side

        def one_face(j, carry):
            values = made_edge[j]
            for r in r_list:
                low, high, is_low, is_high, left, right = patch(s, r, values)
                here = pl.ds((r + 1) * C, C)
                old = target[j, here, left].astype(F32)
                target[j, here, left] = jnp.where(is_low, low, old).astype(BF)
                old = target[j, here, right].astype(F32)
                target[j, here, right] = jnp.where(is_high, high, old).astype(BF)
            return carry

        lax.fori_loop(0, faces, one_face, 0)

    def end_strips(lv):
        n, s = lv.rows, lv.side
        for which, cond in ((0, is_top), (1, is_bot)):

            @pl.when(cond)
            def _(which=which):
                drain(lv.gath.at[pl.ds(0, tiles - 1)], lv.sems.at[PICK_RECV])
                for j in range(faces):
                    _, rev = seam(j, which)
                    pieces = lv.gath[...].reshape(tiles * 16, 2 * C)
                    chosen = lv.sel[(2 if j == 2 else 1) + 2 * rev]
                    both = lax.dot_general(pieces, chosen, TN, preferred_element_type=F32)
                    strip = both[C:] if j == 1 else both[:C]
                    at = 0 if which == 0 else (n + 1) * C
                    lv.body[j, pl.ds(at, C), pl.ds(0, s)] = strip.astype(BF)

    def finish_sends(lv):
        n, s = lv.rows, lv.side

        @pl.when(jnp.logical_not(is_top))
        def _():
            halo_up(lv).wait_send()
            row_copy(lv, 0).wait_send()

        @pl.when(jnp.logical_not(is_bot))
        def _():
            halo_down(lv).wait_send()
            row_copy(lv, 1).wait_send()

        @pl.when(is_top | is_bot)
        def _():
            drain(lv.scat.at[pl.ds(0, tiles - 1)], lv.sems.at[SCAT_SEND])

        drain(lv.tabs.at[pl.ds(0, (groups - 1) * 2 * faces)], lv.sems.at[TAB_SEND])
        mirror_copy(lv).wait_send()

    def taps(product, s):
        left = pltpu.roll(product[:C], 1, 1)
        right = pltpu.roll(product[2 * C :], s - 1, 1)
        return product[C : 2 * C] + left + right

    def conv_row(lv, w, target, j, r):
        n, s = lv.rows, lv.side
        window = lv.body[j, pl.ds(pl.multiple_of(r * C, C), 3 * C), :]
        product = jnp.dot(w[...], window, preferred_element_type=F32)
        made = gelu(taps(product, s)).astype(BF)
        target[j, pl.ds(pl.multiple_of(r * C + C, C), C), :] = made

    def inner_rows(n, one_row):
        def body(i, carry):
            one_row(i // (n - 2), 1 + i % (n - 2))
            return carry

        lax.fori_loop(0, faces * (n - 2), body, 0)

    def outer_rows(n, one_row):
        def body(j, carry):
            @pl.when(jnp.logical_not(is_top))
            def _():
                one_row(j, 0)

            @pl.when(jnp.logical_not(is_bot))
            def _():
                one_row(j, n - 1)

            return carry

        lax.fori_loop(0, faces, body, 0)

    def end_row(lv, one_row):
        n = lv.rows
        for cond, k, r in ((is_top, 0, 0), (is_bot, n + 1, n - 1)):

            @pl.when(cond)
            def _(k=k, r=r):
                def body(j, carry):
                    extract(lv.body, lv.edge, lv.side, j, (k,), False, False)
                    one_row(j, r)
                    return carry

                lax.fori_loop(0, faces, body, 0)

    def state_copy(d):
        dst = lax.rem(t + d, tiles)
        return remote(
            held_ref.at[pl.ds(2 * dst, 2)],
            visit.at[pl.ds(2 * t, 2)],
            misc.at[1],
            misc.at[2],
            (f, dst),
        )

    def sea_copy(d):
        dst = lax.rem(t + d, tiles)
        return remote(
            sea_out.at[pl.ds(2 * dst, 2)],
            sea_in.at[pl.ds(2 * t, 2)],
            misc.at[3],
            misc.at[4],
            (f, dst),
        )

    def start_all(copy):
        def body(d, carry):
            copy(d).start()
            return carry

        lax.fori_loop(1, tiles, body, 0)

    lv1, lv2, lv3, lvs, lv4 = levels
    begin_rows(lv1)
    start_all(state_copy)
    visit[pl.ds(2 * t, 2)] = held_ref[pl.ds(2 * t, 2)]

    def early_ocean():
        drain(visit.at[pl.ds(0, 2 * (tiles - 1))], misc.at[2])
        w_a = jnp.broadcast_to(oin_ref[:, 0:1], (C, side))
        w_b = jnp.broadcast_to(oin_ref[:, 1:2], (C, side))

        def one_slot(n, carry):
            old = visit[n]
            total = w_a * old[:1] + w_b * old[1:]
            before[n] = total
            moved = jnp.sum(oout[...] * gelu(total), axis=0, keepdims=True)
            idle[n] = old[:1] + moved
            return carry

        lax.fori_loop(0, 2 * tiles, one_slot, 0)

    def level(lv, w, along, target, filler):
        n = lv.rows

        def one_row(j, r):
            conv_row(lv, w, target, j, r)

        inner_rows(n, one_row)
        end_rows(lv)
        begin_tables(lv)
        outer_rows(n, one_row)
        end_tables(lv)
        begin_strips(lv)
        filler()
        end_mirror(lv)
        column_strips(lv, False)
        end_strips(lv)
        end_row(lv, one_row)
        make_edges(lv, along)

    level(lv1, w1, a1, body2, early_ocean)
    fix(lv1, body2, (0, rows - 1))
    begin_rows(lv2)
    fix(lv1, body2, range(1, rows - 1))
    level(lv2, w2, a2, bodys, lambda: None)
    fix(lv2, bodys, range(rows))

    def pool(i, carry):
        j, q = i // half_rows, i % half_rows
        pair = bodys[j, pl.ds(pl.multiple_of((2 * q + 1) * C, C), 2 * C), :]
        summed = jnp.dot(pair, down_mat[...], preferred_element_type=F32)
        at = pl.ds(pl.multiple_of((q + 1) * C, C), C)
        body3[j, at, :] = (summed[:C] + summed[C:]).astype(BF)
        return carry

    lax.fori_loop(0, faces * half_rows, pool, 0)
    begin_rows(lv3)
    begin_rows(lvs)

    def skip_tables():
        end_rows(lvs)
        begin_tables(lvs)

    level(lv3, w3, a3, body4, skip_tables)
    fix(lv3, body4, range(half_rows))
    begin_rows(lv4)

    def widen(j, qs):
        for q in qs:
            made = jnp.dot(
                body4[j, pl.ds(q * C, C), :], up_mat[...], preferred_element_type=F32
            ).astype(BF)
            for k in (2 * q - 1, 2 * q):
                if 0 <= k <= rows + 1:
                    bodyc[j, pl.ds(k * C, C), :] = made

    def widen_all(qs):
        def body(j, carry):
            widen(j, qs)
            return carry

        lax.fori_loop(0, faces, body, 0)

    def tile_values(i, j, r, out, width, start):
        where = pl.ds(start, width)
        state = body1[j, pl.ds(pl.multiple_of(r * C + C, C), 16), where]
        wet = jnp.broadcast_to(land_ref[j, pl.ds(r, 1), where] == 1, (8, width))
        return (
            state[:OUT_VARS].astype(F32) + out[:OUT_VARS],
            jnp.where(wet, out[OUT_VARS:], 0.0),
        )

    def decode_row(j, r):
        i = j * rows + r
        window = pl.ds(pl.multiple_of(r * C, C), 3 * C)
        product = jnp.dot(w4[...], bodys[j, window, :], preferred_element_type=F32)
        product += jnp.dot(w5[...], bodyc[j, window, :], preferred_element_type=F32)
        decoded = gelu(taps(product, side)).astype(BF)
        out = jnp.dot(head[...], decoded, preferred_element_type=F32)
        kept, wet = tile_values(i, j, r, out, side, 0)
        pred[i] = kept
        flux[i] = wet.astype(BF)

    widen_all(range(1, half_rows + 1))
    inner_rows(rows, decode_row)
    end_tables(lvs)
    begin_strips(lvs)
    end_rows(lv4)
    begin_tables(lv4)
    widen_all((0, half_rows + 1))
    outer_rows(rows, decode_row)
    end_tables(lv4)
    begin_strips(lv4)

    def coarse_edges(j, carry):
        extract(bodyc, edgec, side, j, range(rows + 2), True, True)
        return carry

    lax.fori_loop(0, faces, coarse_edges, 0)
    end_mirror(lvs)
    column_strips(lvs, False)
    end_strips(lvs)
    end_mirror(lv4)
    column_strips(lv4, True)
    end_strips(lv4)
    for cond, q, k, r in (
        (is_top, 0, 0, 0),
        (is_bot, half_rows + 1, rows + 1, rows - 1),
    ):

        @pl.when(cond)
        def _(q=q, k=k, r=r):
            def body(j, carry):
                widen(j, (q,))
                extract(bodys, lvs.edge, side, j, (k,), False, False)
                extract(bodyc, edgec, side, j, (k,), False, False)
                decode_row(j, r)
                return carry

            lax.fori_loop(0, faces, body, 0)

    def decode_edges(j, carry):
        terms = edge_terms(a4, lvs.edge[j], lvs.strip[j])
        terms += edge_terms(a5, edgec[j], lv4.strip[j])
        values = gelu(edge_sum(terms)).astype(BF)
        out = jnp.dot(head[...], values, preferred_element_type=F32)
        for r in range(rows):
            low, high, is_low, is_high, left, right = patch(side, r, out)
            i = j * rows + r
            for part, mask, where in ((low, is_low[:8], left), (high, is_high[:8], right)):
                kept, wet = tile_values(i, j, r, part, where.size, where.start)
                pred[i, :, where] = jnp.where(mask, kept, pred[i, :, where])
                old = flux[i, :, where].astype(F32)
                flux[i, :, where] = jnp.where(mask, wet, old).astype(BF)
        return carry

    lax.fori_loop(0, faces, decode_edges, 0)

    flux_in = jnp.concatenate(
        [jnp.zeros((C, 2), F32), oin_ref[:, OCEAN_CH:], jnp.zeros((C, 2), F32)], axis=1
    )
    first = flux_in.astype(BF)
    second = (flux_in - first.astype(F32)).astype(BF)
    third = (flux_in - first.astype(F32) - second.astype(F32)).astype(BF)
    split = jnp.concatenate([first, second, third], axis=0)

    def ocean(i, carry):
        slot = slot_ref[i]
        parts = jnp.dot(split, flux[i], preferred_element_type=F32)
        hidden = gelu(
            before[slot] + (parts[:C] + (parts[C : 2 * C] + parts[2 * C :]))
        )
        moved = jnp.sum(oout[...] * hidden, axis=0, keepdims=True)
        tile_sea[i] = visit[slot][:1] + moved
        return carry

    lax.fori_loop(0, faces * rows, ocean, 0)

    def fill(n, carry):
        tile = inv_ref[n]
        used = tile < faces * rows
        sea_out[n] = jnp.where(used, tile_sea[jnp.where(used, tile, 0)], idle[n])
        return carry

    lax.fori_loop(0, 2 * tiles, fill, 0)
    start_all(sea_copy)
    sea_in[pl.ds(2 * t, 2)] = sea_out[pl.ds(2 * t, 2)]

    def surface(i, carry):
        sea = jnp.broadcast_to(tile_sea[i], (8, side))
        wet = jnp.broadcast_to(land_ref[i // rows, pl.ds(i % rows, 1), :] == 1, (8, side))
        wet = wet & (iota((8, side), 0) == 0)
        out_ref[i] = jnp.where(wet, sea, pred[i])
        return carry

    lax.fori_loop(0, faces * rows, surface, 0)
    drain(sea_in.at[pl.ds(0, 2 * (tiles - 1))], misc.at[4])
    sea_ref[...] = sea_in[...]

    for lv in levels:
        finish_sends(lv)
    drain(held_ref.at[pl.ds(0, 2 * (tiles - 1))], misc.at[1])
    drain(sea_out.at[pl.ds(0, 2 * (tiles - 1))], misc.at[3])


def on_device(
    atmos_state,
    land_sea,
    owners,
    seam_table,
    ocean_state,
    conv_input,
    conv_encode,
    conv_coarse,
    conv_decode,
    output_head,
    ocean_in,
    ocean_out,
):
    channels, faces, rows, side = atmos_state.shape
    groups, tiles = lax.axis_size("face"), lax.axis_size("tile")
    count = faces * rows
    slots = ocean_state.shape[2]
    atmos = jnp.pad(jnp.transpose(atmos_state, (1, 2, 0, 3)), ((0, 0), (0, 0), (0, C - channels), (0, 0)))
    atmos = atmos.reshape(faces, rows * C, side)
    owner_ids = owners[:, 0]
    same = owner_ids[:, None] == owner_ids[None, :]
    earlier = jnp.arange(count)[None, :] < jnp.arange(count)[:, None]
    rank = jnp.sum((same & earlier).astype(jnp.int32), axis=1)
    slot = owner_ids * (slots // tiles) + rank
    hits = jnp.arange(slots)[:, None] == slot[None, :]
    inverse = count + jnp.sum(
        jnp.where(hits, jnp.arange(count)[None, :] - count, 0), axis=1
    )
    held = ocean_state[0, 0]
    half_rows, half_side = rows // 2, side // 2
    vmem = pltpu.VMEM
    scratch = [
        vmem((faces, (rows + 2) * C, side), BF),
        vmem((faces, (rows + 2) * C, side), BF),
        vmem((faces, (half_rows + 2) * C, half_side), BF),
        vmem((faces, (rows + 2) * C, side), BF),
        vmem((faces, (half_rows + 2) * C, half_side), BF),
        vmem((faces, (rows + 2) * C, side), BF),
        vmem((5, tiles * 16, side), BF),
        vmem((5, tiles * 16, half_side), BF),
        vmem((half_side, side), BF),
        vmem((side, half_side), BF),
        vmem((count, OUT_VARS, side), F32),
        vmem((count, 8, side), BF),
        vmem((slots, OCEAN_CH, side), F32),
        vmem((slots, 1, side), F32),
        vmem((slots, 1, side), F32),
    ]
    scratch += [vmem((3 * C, 3 * C), BF)] * 5
    scratch += [
        vmem((16, C), BF),
        vmem((C, side), F32),
        vmem((slots, C, side), F32),
        vmem((slots, 1, side), F32),
        vmem((count, 1, side), F32),
    ]
    scratch += [vmem((3 * C, 3 * C), BF)] * 5
    scratch += [
        vmem((5, faces, C, 128), F32),
        vmem((5, faces, C, 128), F32),
        vmem((faces, C, 128), F32),
        vmem((faces, C, 128), F32),
    ]
    for _ in range(5):
        scratch += [
            vmem((tiles, faces, 16, 2 * C), BF),
            vmem((2, faces, 16, 2 * C), BF),
            vmem((2 * faces, 16, 2 * C), BF),
            vmem((groups * 2 * faces, 16, 2 * C), BF),
            vmem((2, faces, 16, 2 * C), BF),
            vmem((tiles, 16, 2 * C), BF),
            vmem((2, 16, 2 * C), BF),
            vmem((2, faces, 16, 2 * C), BF),
        ]
    scratch += [pltpu.SemaphoreType.DMA((5, SEM_COLS)), pltpu.SemaphoreType.DMA((5,))]
    smem = pl.BlockSpec(memory_space=pltpu.SMEM)
    whole = pl.BlockSpec(memory_space=pltpu.VMEM)
    out, sea = pl.pallas_call(
        functools.partial(kernel, groups, tiles, rows, faces),
        out_shape=(
            jax.ShapeDtypeStruct((count, OUT_VARS, side), F32),
            jax.ShapeDtypeStruct((slots, 1, side), F32),
        ),
        in_specs=[smem] * 3 + [pl.BlockSpec(memory_space=pl.ANY)] + [whole] * 9,
        out_specs=(whole, whole),
        scratch_shapes=scratch,
        compiler_params=pltpu.CompilerParams(
            collective_id=0, has_side_effects=True, vmem_limit_bytes=56 * 1024 * 1024
        ),
        name="coupled_step",
    )(
        seam_table.T,
        inverse,
        slot,
        atmos,
        land_sea,
        held,
        conv_input,
        conv_encode,
        conv_coarse,
        conv_decode,
        output_head,
        ocean_in,
        ocean_out[None],
    )
    atmos_next = jnp.transpose(out.reshape(faces, rows, OUT_VARS, side), (2, 0, 1, 3)).astype(BF)
    ocean_next = jnp.concatenate([sea, held[:, :1]], axis=1)
    return atmos_next, ocean_next[None, None]


def solution(mesh):
    in_specs = (
        P(None, "face", "tile", None),
        P("face", "tile", None),
        P(("face", "tile"), None),
        P(),
        P("face", "tile", None, None, None),
        P(),
        P(),
        P(),
        P(),
        P(),
        P(),
        P(),
    )
    out_specs = (P(None, "face", "tile", None), P("face", "tile", None, None, None))
    return jax.shard_map(
        on_device, mesh=mesh, in_specs=in_specs, out_specs=out_specs, check_vma=False
    )
```

```python
import functools

import jax
import jax.numpy as jnp
from jax import lax
from jax.experimental import pallas as pl
from jax.experimental.pallas import tpu as pltpu
from jax.sharding import PartitionSpec as P

MESH = pl.DeviceIdType.MESH
BF = jnp.bfloat16
F32 = jnp.float32
C = 64
OUT_VARS = 8
FLUX_CH = 4
OCEAN_CH = 2
NT = (((1,), (1,)), ((), ()))
TN = (((0,), (0,)), ((), ()))

HALO_SEND, HALO_UP, HALO_DOWN, SCAT_SEND, SCAT_TOP, SCAT_BOT = range(6)
TAB_SEND, TAB_RECV, PICK_SEND, PICK_RECV, HALO_DOWN_SEND = 6, 7, 8, 10, 11
MIRROR_SEND, MIRROR_RECV, SEM_COLS = 12, 13, 14


def iota(shape, dim):
    return lax.broadcasted_iota(jnp.int32, shape, dim)


def gelu(x):
    inner = x * (0.7978845608028654 + 0.035677408136300125 * (x * x))
    half = 0.5 * x
    return half + half * jnp.tanh(inner)


def drain(ref, sem):
    pltpu.make_async_copy(ref, ref, sem).wait()


class Level:
    def __init__(self, rows, side, body, sems, bufs, sel, edge, strip):
        self.edge, self.strip = edge, strip
        self.rows, self.side, self.body, self.sems = rows, side, body, sems
        self.scat, self.scat_in, self.tab, self.tabs, self.pick, self.gath = bufs[:6]
        self.send, self.mirror = bufs[6:]
        self.sel = sel


def kernel(
    groups,
    tiles,
    rows,
    faces,
    seam_ref,
    inv_ref,
    slot_ref,
    atmos_ref,
    land_hbm,
    held_hbm,
    w1_hbm,
    w2_hbm,
    w3_hbm,
    w4_hbm,
    head_hbm,
    oin_hbm,
    oout_hbm,
    out_ref,
    sea_ref,
    body1,
    body2,
    body3,
    bodys,
    body4,
    bodyc,
    sel_f,
    sel_c,
    up_mat,
    down_mat,
    pred,
    visit,
    sea_out,
    sea_in,
    w1,
    w2,
    w3,
    w4,
    w5,
    head,
    oout,
    before,
    idle,
    tile_sea,
    a1,
    a2,
    a3,
    a4,
    a5,
    edges,
    strips,
    edgec,
    made_edge,
    skip_sum,
    wet_edge,
    before_edge,
    state_edge,
    out_vmem,
    land_ref,
    held_ref,
    w1_ref,
    w2_ref,
    w3_ref,
    w4_ref,
    head_ref,
    oin_ref,
    oout_ref,
    loaded,
    oin_a,
    oin_b,
    split,
    *rest,
):
    bufs, (sems, misc) = rest[:-2], rest[-2:]
    f = lax.axis_index("face")
    t = lax.axis_index("tile")
    side = rows * tiles
    half_rows, half_side = rows // 2, side // 2
    is_top, is_bot = t == 0, t == tiles - 1
    last = tiles - 1

    inputs = (
        (land_hbm, land_ref),
        (held_hbm, held_ref),
        (w1_hbm, w1_ref),
        (w2_hbm, w2_ref),
        (w3_hbm, w3_ref),
        (w4_hbm, w4_ref),
        (head_hbm, head_ref),
        (oin_hbm, oin_ref),
        (oout_hbm, oout_ref),
    )
    loads = [
        pltpu.make_async_copy(src, dst, loaded.at[i]) for i, (src, dst) in enumerate(inputs)
    ]
    atmos_ch = atmos_ref.shape[2]
    for j in range(faces):
        for r in range(rows):
            pltpu.make_async_copy(
                atmos_ref.at[j, r], body1.at[j, pl.ds((r + 1) * C, atmos_ch)], misc.at[0]
            ).start()
    for load in loads:
        load.start()

    levels = []
    for number, (n, s, body, sel) in enumerate(
        (
            (rows, side, body1, sel_f),
            (rows, side, body2, sel_f),
            (half_rows, half_side, body3, sel_c),
            (rows, side, bodys, sel_f),
            (half_rows, half_side, body4, sel_c),
        )
    ):
        own = bufs[8 * number : 8 * number + 8]
        levels.append(
            Level(n, s, body, sems.at[number], own, sel, edges.at[number], strips.at[number])
        )

    barrier = pltpu.get_barrier_semaphore()

    def greet(d, carry):
        peer = lax.rem(t + d, tiles)
        pl.semaphore_signal(barrier, inc=1, device_id=(f, peer), device_id_type=MESH)
        return carry

    lax.fori_loop(1, tiles, greet, 0)
    for d in range(1, groups):
        g = lax.rem(f + d, groups)
        pl.semaphore_signal(barrier, inc=1, device_id=(g, t), device_id_type=MESH)

    @pl.when(is_top | is_bot)
    def _():
        for n, s, sel in ((rows, side, sel_f), (half_rows, half_side, sel_c)):
            shape = (tiles * 16, s)
            q, x = iota(shape, 0), iota(shape, 1)
            k = q % 16
            start = (q // 16) * n
            sel[0] = jnp.where((x == start + k - 1) & (k <= n + 1), 1.0, 0.0).astype(BF)
            for at, least in ((1, 0), (2, 8)):
                cell = start + k - least
                inner = (k >= least) & (k < least + n)
                sel[at] = jnp.where((x == cell) & inner, 1.0, 0.0).astype(BF)
                sel[at + 2] = jnp.where((x == s - 1 - cell) & inner, 1.0, 0.0).astype(BF)

    shape = (half_side, side)
    up_mat[...] = jnp.where(iota(shape, 1) // 2 == iota(shape, 0), 1.0, 0.0).astype(BF)
    shape = (side, half_side)
    down_mat[...] = jnp.where(iota(shape, 0) // 2 == iota(shape, 1), 0.25, 0.0).astype(BF)

    for j in range(faces):
        for r in range(rows):
            spare = C - atmos_ch
            if spare:
                body1[j, pl.ds((r + 1) * C + atmos_ch, spare), :] = jnp.zeros((spare, side), BF)
    for load in loads:
        load.wait()

    for target, along, ref, first, width in (
        (w1, a1, w1_ref, 0, w1_ref.shape[2] // 3),
        (w2, a2, w2_ref, 0, C),
        (w3, a3, w3_ref, 0, C),
        (w4, a4, w4_ref, 0, C),
        (w5, a5, w4_ref, C, C),
    ):
        channels = ref.shape[2] // 3
        for a in range(3):
            whole = ref[a].astype(F32)
            for b in range(3):
                at = b * channels + first
                block = whole[:, at : at + width]
                if width < C:
                    block = jnp.concatenate([block, jnp.zeros((C, C - width), F32)], axis=1)
                target[pl.ds(b * C, C), pl.ds(a * C, C)] = block.astype(BF)
                along[pl.ds(a * C, C), pl.ds(b * C, C)] = block.astype(BF)
    made = head_ref[...].astype(F32)
    gap = jnp.zeros((FLUX_CH, C), F32)
    head[...] = jnp.concatenate([made[:OUT_VARS]] + [made[OUT_VARS:]] * 3 + [gap], axis=0).astype(
        BF
    )
    diagonal = iota((C, C), 0) == iota((C, C), 1)

    def column(row):
        spread = jnp.where(diagonal, jnp.broadcast_to(row, (C, C)), 0.0)
        return jnp.sum(spread, axis=1, keepdims=True)

    oout[...] = jnp.broadcast_to(column(oout_ref[...]), oout.shape)
    oin = [column(oin_ref[c : c + 1, :]) for c in range(OCEAN_CH + FLUX_CH)]
    w_a, w_b = (jnp.broadcast_to(oin[c], (C, side)) for c in range(OCEAN_CH))
    oin_a[...] = w_a
    oin_b[...] = w_b
    flux_in = jnp.concatenate(oin[OCEAN_CH:], axis=1)
    first = flux_in.astype(BF)
    second = (flux_in - first.astype(F32)).astype(BF)
    third = (flux_in - first.astype(F32) - second.astype(F32)).astype(BF)
    split[...] = jnp.concatenate(
        [v.astype(F32) for v in (first, second, third)] + [jnp.zeros((C, FLUX_CH), F32)], axis=1
    ).astype(BF)

    drain(body1.at[:, pl.ds(0, rows * atmos_ch), :], misc.at[0])
    pl.semaphore_wait(barrier, tiles - 1 + groups - 1)

    def remote(src, dst, send, recv, device):
        return pltpu.make_async_remote_copy(
            src_ref=src,
            dst_ref=dst,
            send_sem=send,
            recv_sem=recv,
            device_id=device,
            device_id_type=MESH,
        )

    def halo_up(lv):
        n, s = lv.rows, lv.side
        return remote(
            lv.body.at[:, pl.ds(C, C), pl.ds(0, s)],
            lv.body.at[:, pl.ds((n + 1) * C, C), pl.ds(0, s)],
            lv.sems.at[HALO_SEND],
            lv.sems.at[HALO_DOWN],
            (f, jnp.maximum(t - 1, 0)),
        )

    def halo_down(lv):
        n, s = lv.rows, lv.side
        return remote(
            lv.body.at[:, pl.ds(n * C, C), pl.ds(0, s)],
            lv.body.at[:, pl.ds(0, C), pl.ds(0, s)],
            lv.sems.at[HALO_DOWN_SEND],
            lv.sems.at[HALO_UP],
            (f, jnp.minimum(t + 1, last)),
        )

    def scatter_piece(lv, which, dst):
        return remote(
            lv.scat.at[dst],
            lv.scat_in.at[which],
            lv.sems.at[SCAT_SEND],
            lv.sems.at[SCAT_TOP + which],
            (f, dst),
        )

    def begin_rows(lv):
        n, s = lv.rows, lv.side

        @pl.when(jnp.logical_not(is_top))
        def _():
            halo_up(lv).start()

        @pl.when(jnp.logical_not(is_bot))
        def _():
            halo_down(lv).start()

        for which, cond in ((0, is_top), (1, is_bot)):

            @pl.when(cond)
            def _(which=which):
                for j in range(faces):
                    start = C if which == 0 else n * C
                    edge = lv.body[j, pl.ds(start, C), pl.ds(0, s)]
                    zero = jnp.zeros_like(edge)
                    both = jnp.concatenate([edge, zero] if which == 0 else [zero, edge], axis=0)
                    piece = lax.dot_general(
                        lv.sel[0], both, NT, preferred_element_type=F32
                    ).astype(BF)
                    lv.scat[:, j] = piece.reshape(tiles, 16, 2 * C)
                own = 0 if which == 0 else last
                lv.scat_in[which] = lv.scat[own]

                def send(d, carry):
                    scatter_piece(lv, which, lax.rem(own + d, tiles)).start()
                    return carry

                lax.fori_loop(1, tiles, send, 0)

    def end_rows(lv):
        @pl.when(jnp.logical_not(is_top))
        def _():
            drain(lv.body.at[:, pl.ds(0, C), pl.ds(0, lv.side)], lv.sems.at[HALO_UP])
            drain(lv.scat_in.at[0], lv.sems.at[SCAT_TOP])

        @pl.when(jnp.logical_not(is_bot))
        def _():
            n = lv.rows
            drain(lv.body.at[:, pl.ds((n + 1) * C, C), pl.ds(0, lv.side)], lv.sems.at[HALO_DOWN])
            drain(lv.scat_in.at[1], lv.sems.at[SCAT_BOT])

    def table_copy(lv, d):
        width = 2 * faces
        return remote(
            lv.tab,
            lv.tabs.at[pl.ds(f * width, width)],
            lv.sems.at[TAB_SEND],
            lv.sems.at[TAB_RECV],
            (lax.rem(f + d, groups), t),
        )

    lane = iota((C, 128), 1)

    def widened(data, right):
        missing = 128 - data.shape[1]
        if missing <= 0:
            return data
        zero = jnp.zeros((C, missing), data.dtype)
        return jnp.concatenate([zero, data] if right else [data, zero], axis=1)

    def extract(body, edge, s, j, ks, fresh, clear):
        total = jnp.zeros((C, 128), F32) if fresh else edge[j]
        wide = min(s, 128)
        for k in ks:
            here = pl.ds(k * C, C)
            left = widened(body[j, here, pl.ds(0, wide)].astype(F32), False)
            right = widened(body[j, here, pl.ds(s - wide, wide)].astype(F32), True)
            if clear and k == 0:
                left, right = (jnp.where(is_top, 0.0, v) for v in (left, right))
            if clear and k == ks[-1]:
                left, right = (jnp.where(is_bot, 0.0, v) for v in (left, right))
            total = jnp.where(lane // 2 == k, pltpu.roll(left, 2 * k, 1), total)
            total = jnp.where(
                lane // 2 == 32 + k, pltpu.roll(right, (66 + 2 * k) % 128, 1), total
            )
        edge[j] = total
        return total

    def extract_inner(body, edge, n, s):
        def one_face(j, carry):
            extract(body, edge, s, j, range(1, n + 1), True, False)
            return carry

        lax.fori_loop(0, faces, one_face, 0)

    def begin_tables(lv):
        n, s = lv.rows, lv.side
        shape = (32, 128)
        row, at = iota(shape, 0), iota(shape, 1)
        want = jnp.where(row < 16, 2 * row, 64 + 2 * (row - 16) + 1)
        pick = jnp.where((at == want) & (row % 16 < n + 2), 1.0, 0.0).astype(BF)

        def one_face(j, carry):
            edge = extract(lv.body, lv.edge, s, j, (0, n + 1), False, True)
            total = lax.dot_general(pick, edge.astype(BF), NT, preferred_element_type=F32)
            lv.tab[2 * j + 1] = jnp.concatenate([total[:16], total[16:]], axis=1).astype(BF)
            lv.tab[2 * j] = lv.scat_in[0, j] + lv.scat_in[1, j]
            return carry

        lax.fori_loop(0, faces, one_face, 0, unroll=True)
        for d in range(1, groups):
            table_copy(lv, d).start()
        lv.tabs[pl.ds(f * 2 * faces, 2 * faces)] = lv.tab[...]

    def end_tables(lv):
        drain(lv.tabs.at[pl.ds(0, (groups - 1) * 2 * faces)], lv.sems.at[TAB_RECV])

    def row_copy(lv, which):
        return remote(
            lv.send.at[which],
            lv.gath.at[t],
            lv.sems.at[PICK_SEND + which],
            lv.sems.at[PICK_RECV],
            (f, 0 if which == 0 else last),
        )

    def mirror_copy(lv):
        return remote(
            lv.pick, lv.mirror, lv.sems.at[MIRROR_SEND], lv.sems.at[MIRROR_RECV], (f, last - t)
        )

    def seam(j, s):
        at = (f * faces + j) * 4 + s
        return seam_ref[0, at], seam_ref[1, at]

    def begin_strips(lv):
        n = lv.rows
        shape = (16, 16)
        r, k = iota(shape, 0), iota(shape, 1)
        low = jnp.where((k == r + 1) & (r < n), 1.0, 0.0).astype(BF)
        high = jnp.where((k == r - 7) & (r >= 8) & (r < 8 + n), 1.0, 0.0).astype(BF)
        for which, cond in ((0, is_top), (1, is_bot)):
            parts = []
            for j in range(faces):
                p, _ = seam(j, which)
                spread = jnp.dot(
                    high if j == 2 else low, lv.tabs[p // 2], preferred_element_type=F32
                )
                parts.append(jnp.where(p % 2 == 1, spread[:, C:], spread[:, :C]))
            lv.send[which] = jnp.concatenate([parts[0] + parts[2], parts[1]], axis=1).astype(BF)

            @pl.when(jnp.logical_not(cond))
            def _(which=which):
                row_copy(lv, which).start()

            @pl.when(cond)
            def _(which=which):
                lv.gath[0 if which == 0 else last] = lv.send[which]

        for s in (2, 3):
            for j in range(faces):
                p, _ = seam(j, s)
                lv.pick[s - 2, j] = lv.tabs[p // 2]
        mirror_copy(lv).start()

    def column_strips(lv, fine):
        n = lv.rows
        shape = (16, 128)
        k, at = iota(shape, 0), iota(shape, 1)

        def one_face(j, carry):
            total = jnp.zeros((C, 128), F32)
            for s in (2, 3):
                p, rev = seam(j, s)
                piece = jnp.where(rev == 1, lv.mirror[s - 2, j], lv.pick[s - 2, j])
                kk = jnp.where(rev == 1, n + 1 - k, k)
                good = (kk >= jnp.where(is_top, 1, 0)) & (kk <= jnp.where(is_bot, n, n + 1))
                spot = at if s == 2 else at - 65
                index = (spot // 2 + 1) // 2 if fine else spot // 2
                good = good & (index == kk) & (spot % 2 == 0)
                good = good & ((at < 64) if s == 2 else (at > 64))
                chosen = jnp.where(good, 1.0, 0.0).astype(BF)
                both = lax.dot_general(piece, chosen, TN, preferred_element_type=F32)
                total += jnp.where(p % 2 == 1, both[C:], both[:C])
            lv.strip[j] = total
            return carry

        lax.fori_loop(0, faces, one_face, 0, unroll=True)

    def end_mirror(lv):
        drain(lv.mirror, lv.sems.at[MIRROR_RECV])

    def edge_terms(along, edge, strip):
        near = jnp.where(lane < 64, strip, pltpu.roll(edge, 1, 1))
        far = jnp.where(lane < 64, pltpu.roll(edge, 127, 1), strip)
        stack = jnp.concatenate([near, edge, far], axis=0).astype(BF)
        return jnp.dot(along[...], stack, preferred_element_type=F32)

    def edge_sum(terms):
        return (
            terms[:C]
            + pltpu.roll(terms[C : 2 * C], 126, 1)
            + pltpu.roll(terms[2 * C :], 124, 1)
        )

    def make_edges(lv, along):
        def one_face(j, carry):
            made_edge[j] = gelu(edge_sum(edge_terms(along, lv.edge[j], lv.strip[j])))
            return carry

        lax.fori_loop(0, faces, one_face, 0, unroll=True)

    def patch(s, r, values):
        wide = min(s, 128)
        spot = iota((values.shape[0], wide), 1)
        low = pltpu.roll(values, (128 - 2 * r) % 128, 1)[:, :wide]
        high = pltpu.roll(values, (2 * 128 + wide - 1 - 65 - 2 * r) % 128, 1)[:, :wide]
        return low, high, spot == 0, spot == wide - 1, pl.ds(0, wide), pl.ds(s - wide, wide)

    def fix(lv, target, r_list):
        n, s = lv.rows, lv.side

        def one_face(j, carry):
            values = made_edge[j]
            for r in r_list:
                low, high, is_low, is_high, left, right = patch(s, r, values)
                here = pl.ds((r + 1) * C, C)
                old = target[j, here, left].astype(F32)
                target[j, here, left] = jnp.where(is_low, low, old).astype(BF)
                old = target[j, here, right].astype(F32)
                target[j, here, right] = jnp.where(is_high, high, old).astype(BF)
            return carry

        lax.fori_loop(0, faces, one_face, 0, unroll=True)

    def end_strips(lv):
        n, s = lv.rows, lv.side
        for which, cond in ((0, is_top), (1, is_bot)):

            @pl.when(cond)
            def _(which=which):
                drain(lv.gath.at[pl.ds(0, tiles - 1)], lv.sems.at[PICK_RECV])
                for j in range(faces):
                    _, rev = seam(j, which)
                    pieces = lv.gath[...].reshape(tiles * 16, 2 * C)
                    chosen = lv.sel[(2 if j == 2 else 1) + 2 * rev]
                    both = lax.dot_general(pieces, chosen, TN, preferred_element_type=F32)
                    strip = both[C:] if j == 1 else both[:C]
                    at = 0 if which == 0 else (n + 1) * C
                    lv.body[j, pl.ds(at, C), pl.ds(0, s)] = strip.astype(BF)

    def finish_sends(lv):
        n, s = lv.rows, lv.side

        @pl.when(jnp.logical_not(is_top))
        def _():
            halo_up(lv).wait_send()
            row_copy(lv, 0).wait_send()

        @pl.when(jnp.logical_not(is_bot))
        def _():
            halo_down(lv).wait_send()
            row_copy(lv, 1).wait_send()

        @pl.when(is_top | is_bot)
        def _():
            drain(lv.scat.at[pl.ds(0, tiles - 1)], lv.sems.at[SCAT_SEND])

        drain(lv.tabs.at[pl.ds(0, (groups - 1) * 2 * faces)], lv.sems.at[TAB_SEND])
        mirror_copy(lv).wait_send()

    def taps(product, s):
        left = pltpu.roll(product[:C], 1, 1)
        right = pltpu.roll(product[2 * C :], s - 1, 1)
        return product[C : 2 * C] + left + right

    def conv_row(lv, w, target, j, r):
        n, s = lv.rows, lv.side
        window = lv.body[j, pl.ds(pl.multiple_of(r * C, C), 3 * C), :]
        product = jnp.dot(w[...], window, preferred_element_type=F32)
        made = gelu(taps(product, s)).astype(BF)
        target[j, pl.ds(pl.multiple_of(r * C + C, C), C), :] = made

    def inner_rows(first, stop, one_row):
        count = stop - first

        def body(i, carry):
            one_row(i // count, first + i % count)
            return carry

        if count > 0:
            lax.fori_loop(0, faces * count, body, 0)

    def outer_rows(n, one_row):
        def body(j, carry):
            @pl.when(jnp.logical_not(is_top))
            def _():
                one_row(j, 0)

            @pl.when(jnp.logical_not(is_bot))
            def _():
                one_row(j, n - 1)

            return carry

        lax.fori_loop(0, faces, body, 0)

    def end_row(lv, one_row):
        n = lv.rows
        for cond, k, r in ((is_top, 0, 0), (is_bot, n + 1, n - 1)):

            @pl.when(cond)
            def _(k=k, r=r):
                def body(j, carry):
                    extract(lv.body, lv.edge, lv.side, j, (k,), False, False)
                    one_row(j, r)
                    return carry

                lax.fori_loop(0, faces, body, 0)

    def state_copy(d):
        dst = lax.rem(t + d, tiles)
        return remote(
            held_ref.at[pl.ds(2 * dst, 2)],
            visit.at[pl.ds(2 * t, 2)],
            misc.at[1],
            misc.at[2],
            (f, dst),
        )

    def sea_copy(d):
        dst = lax.rem(t + d, tiles)
        return remote(
            sea_out.at[pl.ds(2 * dst, 2)],
            sea_in.at[pl.ds(2 * t, 2)],
            misc.at[3],
            misc.at[4],
            (f, dst),
        )

    def start_all(copy):
        def body(d, carry):
            copy(d).start()
            return carry

        lax.fori_loop(1, tiles, body, 0)

    lv1, lv2, lv3, lvs, lv4 = levels
    begin_rows(lv1)
    start_all(state_copy)
    visit[pl.ds(2 * t, 2)] = held_ref[pl.ds(2 * t, 2)]

    def early_ocean():
        drain(visit.at[pl.ds(0, 2 * (tiles - 1))], misc.at[2])

        def one_slot(n, carry):
            old = visit[n]
            total = oin_a[...] * old[:1] + oin_b[...] * old[1:]
            before[n] = total
            moved = jnp.sum(oout[:, :side] * gelu(total), axis=0, keepdims=True)
            idle[n] = old[:1] + moved
            return carry

        lax.fori_loop(0, 2 * tiles, one_slot, 0, unroll=2)

    def to_edges(total, row, r, wide):
        spot = iota(total.shape, 1)
        low, high = row[:, :wide], row[:, side - wide :]
        if wide < 128:
            zero = jnp.zeros((row.shape[0], 128 - wide), row.dtype)
            low = jnp.concatenate([low, zero], axis=1)
            high = jnp.concatenate([zero, high], axis=1)
        total = jnp.where(spot == 2 * r, pltpu.roll(low, 2 * r, 1), total)
        return jnp.where(spot == 65 + 2 * r, pltpu.roll(high, (66 + 2 * r) % 128, 1), total)

    def ocean_edges():
        wide = min(side, 128)

        def one_face(j, carry):
            wet = jnp.zeros((8, 128), F32)
            state = jnp.zeros((8, 128), F32)
            total = jnp.zeros((C, 128), F32)
            for r in range(rows):
                slot = slot_ref[j * rows + r]
                land = jnp.broadcast_to(land_ref[j, pl.ds(r, 1), :], (8, side)).astype(F32)
                wet = to_edges(wet, land, r, wide)
                old = jnp.broadcast_to(visit[slot][:1], (8, side))
                state = to_edges(state, old, r, wide)
                total = to_edges(total, before[slot], r, wide)
            wet_edge[j] = wet
            state_edge[j] = state
            before_edge[j] = total
            return carry

        lax.fori_loop(0, faces, one_face, 0)

    def level(lv, w, along, target, held_back, fill_rows, fill_strips):
        n = lv.rows

        def one_row(j, r):
            conv_row(lv, w, target, j, r)

        extract_inner(lv.body, lv.edge, n, lv.side)
        inner_rows(1, n - 1 - held_back, one_row)
        fill_rows()
        end_rows(lv)
        begin_tables(lv)
        outer_rows(n, one_row)
        end_tables(lv)
        begin_strips(lv)
        inner_rows(n - 1 - held_back, n - 1, one_row)
        fill_strips()
        end_mirror(lv)
        column_strips(lv, False)
        end_strips(lv)
        end_row(lv, one_row)
        make_edges(lv, along)

    def nothing():
        pass

    level(lv1, w1, a1, body2, 0, nothing, early_ocean)
    fix(lv1, body2, (0, rows - 1))
    begin_rows(lv2)
    fix(lv1, body2, range(1, rows - 1))
    level(lv2, w2, a2, bodys, 2, nothing, ocean_edges)

    def pool(qs):
        def one_face(j, carry):
            for q in qs:
                pair = bodys[j, pl.ds((2 * q + 1) * C, 2 * C), :]
                summed = jnp.dot(pair, down_mat[...], preferred_element_type=F32)
                body3[j, pl.ds((q + 1) * C, C), :] = (summed[:C] + summed[C:]).astype(BF)
            return carry

        lax.fori_loop(0, faces, one_face, 0, unroll=True)

    outer = (0, 1, rows - 2, rows - 1)
    fix(lv2, bodys, outer)
    pool((0, half_rows - 1))
    begin_rows(lv3)
    fix(lv2, bodys, [r for r in range(rows) if r not in outer])
    pool(range(1, half_rows - 1))
    begin_rows(lvs)

    def skip_row(j, r):
        window = pl.ds(pl.multiple_of(r * C, C), 3 * C)
        product = jnp.dot(w4[...], bodys[j, window, :], preferred_element_type=F32)
        skip_sum[j * rows + r] = taps(product, side)

    def fill_rows3():
        extract_inner(bodys, lvs.edge, rows, side)
        inner_rows(1, rows // 2, skip_row)

    def fill_strips3():
        end_rows(lvs)
        begin_tables(lvs)
        outer_rows(rows, skip_row)
        inner_rows(rows // 2, rows - 1, skip_row)

    level(lv3, w3, a3, body4, 0, fill_rows3, fill_strips3)
    fix(lv3, body4, (0, half_rows - 1))
    begin_rows(lv4)
    fix(lv3, body4, range(1, half_rows - 1))

    def widen(j, qs):
        for q in qs:
            made = jnp.dot(
                body4[j, pl.ds(q * C, C), :], up_mat[...], preferred_element_type=F32
            ).astype(BF)
            for k in (2 * q - 1, 2 * q):
                if 0 <= k <= rows + 1:
                    bodyc[j, pl.ds(k * C, C), :] = made

    def widen_all(qs):
        def body(j, carry):
            widen(j, qs)
            return carry

        lax.fori_loop(0, faces, body, 0, unroll=True)

    def tile_values(j, r, out, width, start):
        where = pl.ds(start, width)
        state = body1[j, pl.ds(pl.multiple_of(r * C + C, C), 16), where]
        wet = jnp.broadcast_to(land_ref[j, pl.ds(r, 1), where] == 1, (16, width))
        return (
            state[:OUT_VARS].astype(F32) + out[:OUT_VARS],
            jnp.where(wet, out[OUT_VARS:], 0.0).astype(BF),
        )

    def decode_row(j, r):
        i = j * rows + r
        window = pl.ds(pl.multiple_of(r * C, C), 3 * C)
        product = jnp.dot(w5[...], bodyc[j, window, :], preferred_element_type=F32)
        decoded = gelu(skip_sum[i] + taps(product, side)).astype(BF)
        out = jnp.dot(head[...], decoded, preferred_element_type=F32)
        pred[i], flux = tile_values(j, r, out, side, 0)
        slot = slot_ref[i]
        hidden = gelu(before[slot] + jnp.dot(split[...], flux, preferred_element_type=F32))
        moved = jnp.sum(oout[:, :side] * hidden, axis=0, keepdims=True)
        tile_sea[i] = visit[slot][:1] + moved

    widen_all(range(1, half_rows + 1))
    extract_inner(body4, lv4.edge, half_rows, half_side)
    end_tables(lvs)
    begin_strips(lvs)
    early = 1 + (rows - 2) // 3
    inner_rows(1, early, decode_row)
    end_rows(lv4)
    begin_tables(lv4)
    widen_all((0, half_rows + 1))
    outer_rows(rows, decode_row)
    end_tables(lv4)
    begin_strips(lv4)

    def coarse_edges(j, carry):
        extract(bodyc, edgec, side, j, range(rows + 2), True, True)
        return carry

    lax.fori_loop(0, faces, coarse_edges, 0)
    inner_rows(early, rows - 1, decode_row)
    end_mirror(lvs)
    column_strips(lvs, False)
    end_strips(lvs)
    end_mirror(lv4)
    column_strips(lv4, True)
    end_strips(lv4)
    for cond, q, k, r in (
        (is_top, 0, 0, 0),
        (is_bot, half_rows + 1, rows + 1, rows - 1),
    ):

        @pl.when(cond)
        def _(q=q, k=k, r=r):
            def body(j, carry):
                widen(j, (q,))
                extract(bodys, lvs.edge, side, j, (k,), False, False)
                extract(bodyc, edgec, side, j, (k,), False, False)
                skip_row(j, r)
                decode_row(j, r)
                return carry

            lax.fori_loop(0, faces, body, 0)

    def decode_edges(j, carry):
        terms = edge_terms(a4, lvs.edge[j], lvs.strip[j])
        terms += edge_terms(a5, edgec[j], lv4.strip[j])
        values = gelu(edge_sum(terms)).astype(BF)
        out = jnp.dot(head[...], values, preferred_element_type=F32)
        wet = jnp.concatenate([wet_edge[j]] * 2, axis=0) == 1.0
        flux = jnp.where(wet, out[OUT_VARS:], 0.0).astype(BF)
        hidden = gelu(before_edge[j] + jnp.dot(split[...], flux, preferred_element_type=F32))
        moved = jnp.sum(oout[:, :128] * hidden, axis=0, keepdims=True)
        sea = state_edge[j] + moved
        for r in range(rows):
            low, high, is_low, is_high, left, right = patch(side, r, out)
            sea_low, sea_high, _, _, _, _ = patch(side, r, sea)
            i = j * rows + r
            for part, sea_part, mask, where in (
                (low, sea_low, is_low[:8], left),
                (high, sea_high, is_high[:8], right),
            ):
                kept, _ = tile_values(j, r, part, where.size, where.start)
                pred[i, :, where] = jnp.where(mask, kept, pred[i, :, where])
                tile_sea[i, :, where] = jnp.where(
                    mask[:1], sea_part[:1], tile_sea[i, :, where]
                )
        return carry

    lax.fori_loop(0, faces, decode_edges, 0, unroll=True)

    def fill(n, carry):
        tile = inv_ref[n]
        used = tile < faces * rows
        sea_out[n] = jnp.where(used, tile_sea[jnp.where(used, tile, 0)], idle[n])
        return carry

    lax.fori_loop(0, 2 * tiles, fill, 0, unroll=4)
    start_all(sea_copy)
    sea_in[pl.ds(2 * t, 2)] = sea_out[pl.ds(2 * t, 2)]

    def surface(i, carry):
        sea = jnp.broadcast_to(tile_sea[i], (8, side))
        wet = jnp.broadcast_to(land_ref[i // rows, pl.ds(i % rows, 1), :] == 1, (8, side))
        wet = wet & (iota((8, side), 0) == 0)
        out_vmem[i] = jnp.where(wet, sea, pred[i])
        return carry

    lax.fori_loop(0, faces * rows, surface, 0)
    save = pltpu.make_async_copy(out_vmem, out_ref, loaded.at[0])
    save.start()
    drain(sea_in.at[pl.ds(0, 2 * (tiles - 1))], misc.at[4])
    save_sea = pltpu.make_async_copy(sea_in, sea_ref, loaded.at[1])
    save_sea.start()

    for lv in levels:
        finish_sends(lv)
    drain(held_ref.at[pl.ds(0, 2 * (tiles - 1))], misc.at[1])
    drain(sea_out.at[pl.ds(0, 2 * (tiles - 1))], misc.at[3])
    save.wait()
    save_sea.wait()


def on_device(
    atmos_state,
    land_sea,
    owners,
    seam_table,
    ocean_state,
    conv_input,
    conv_encode,
    conv_coarse,
    conv_decode,
    output_head,
    ocean_in,
    ocean_out,
):
    channels, faces, rows, side = atmos_state.shape
    groups, tiles = lax.axis_size("face"), lax.axis_size("tile")
    count = faces * rows
    slots = ocean_state.shape[2]
    atmos = jnp.transpose(atmos_state, (1, 2, 0, 3))
    owner_ids = owners[:, 0]
    same = owner_ids[:, None] == owner_ids[None, :]
    earlier = jnp.arange(count)[None, :] < jnp.arange(count)[:, None]
    rank = jnp.sum((same & earlier).astype(jnp.int32), axis=1)
    slot = owner_ids * (slots // tiles) + rank
    hits = jnp.arange(slots)[:, None] == slot[None, :]
    inverse = count + jnp.sum(
        jnp.where(hits, jnp.arange(count)[None, :] - count, 0), axis=1
    )
    held = ocean_state[0, 0]
    half_rows, half_side = rows // 2, side // 2
    vmem = pltpu.VMEM
    scratch = [
        vmem((faces, (rows + 2) * C, side), BF),
        vmem((faces, (rows + 2) * C, side), BF),
        vmem((faces, (half_rows + 2) * C, half_side), BF),
        vmem((faces, (rows + 2) * C, side), BF),
        vmem((faces, (half_rows + 2) * C, half_side), BF),
        vmem((faces, (rows + 2) * C, side), BF),
        vmem((5, tiles * 16, side), BF),
        vmem((5, tiles * 16, half_side), BF),
        vmem((half_side, side), BF),
        vmem((side, half_side), BF),
        vmem((count, OUT_VARS, side), F32),
        vmem((slots, OCEAN_CH, side), F32),
        vmem((slots, 1, side), F32),
        vmem((slots, 1, side), F32),
    ]
    scratch += [vmem((3 * C, 3 * C), BF)] * 5
    scratch += [
        vmem((24, C), BF),
        vmem((C, max(side, 128)), F32),
        vmem((slots, C, side), F32),
        vmem((slots, 1, side), F32),
        vmem((count, 1, side), F32),
    ]
    scratch += [vmem((3 * C, 3 * C), BF)] * 5
    scratch += [
        vmem((5, faces, C, 128), F32),
        vmem((5, faces, C, 128), F32),
        vmem((faces, C, 128), F32),
        vmem((faces, C, 128), F32),
        vmem((count, C, side), F32),
        vmem((faces, 8, 128), F32),
        vmem((faces, C, 128), F32),
        vmem((faces, 8, 128), F32),
        vmem((count, OUT_VARS, side), F32),
    ]
    loaded = (
        land_sea,
        held,
        conv_input,
        conv_encode,
        conv_coarse,
        conv_decode,
        output_head,
        ocean_in.T,
        ocean_out[None],
    )
    scratch += [vmem(v.shape, v.dtype) for v in loaded]
    scratch += [
        pltpu.SemaphoreType.DMA((len(loaded),)),
        vmem((C, side), F32),
        vmem((C, side), F32),
        vmem((C, 16), BF),
    ]
    for _ in range(5):
        scratch += [
            vmem((tiles, faces, 16, 2 * C), BF),
            vmem((2, faces, 16, 2 * C), BF),
            vmem((2 * faces, 16, 2 * C), BF),
            vmem((groups * 2 * faces, 16, 2 * C), BF),
            vmem((2, faces, 16, 2 * C), BF),
            vmem((tiles, 16, 2 * C), BF),
            vmem((2, 16, 2 * C), BF),
            vmem((2, faces, 16, 2 * C), BF),
        ]
    scratch += [pltpu.SemaphoreType.DMA((5, SEM_COLS)), pltpu.SemaphoreType.DMA((5,))]
    smem = pl.BlockSpec(memory_space=pltpu.SMEM)
    anywhere = pl.BlockSpec(memory_space=pl.ANY)
    out, sea = pl.pallas_call(
        functools.partial(kernel, groups, tiles, rows, faces),
        out_shape=(
            jax.ShapeDtypeStruct((count, OUT_VARS, side), F32),
            jax.ShapeDtypeStruct((slots, 1, side), F32),
        ),
        in_specs=[smem] * 3 + [anywhere] * (1 + len(loaded)),
        out_specs=(anywhere, anywhere),
        scratch_shapes=scratch,
        compiler_params=pltpu.CompilerParams(
            collective_id=0, has_side_effects=True, vmem_limit_bytes=56 * 1024 * 1024
        ),
        name="coupled_step",
    )(
        seam_table.T,
        inverse,
        slot,
        atmos,
        *loaded,
    )
    atmos_next = jnp.transpose(out.reshape(faces, rows, OUT_VARS, side), (2, 0, 1, 3)).astype(BF)
    ocean_next = jnp.concatenate([sea, held[:, :1]], axis=1)
    return atmos_next, ocean_next[None, None]


def solution(mesh):
    in_specs = (
        P(None, "face", "tile", None),
        P("face", "tile", None),
        P(("face", "tile"), None),
        P(),
        P("face", "tile", None, None, None),
        P(),
        P(),
        P(),
        P(),
        P(),
        P(),
        P(),
    )
    out_specs = (P(None, "face", "tile", None), P("face", "tile", None, None, None))
    return jax.shard_map(
        on_device, mesh=mesh, in_specs=in_specs, out_specs=out_specs, check_vma=False
    )
```

```python
import functools

import jax
import jax.numpy as jnp
from jax import lax
from jax.experimental import pallas as pl
from jax.experimental.pallas import tpu as pltpu
from jax.sharding import PartitionSpec as P

MESH = pl.DeviceIdType.MESH
BF = jnp.bfloat16
F32 = jnp.float32
C = 64
OUT_VARS = 8
FLUX_CH = 4
OCEAN_CH = 2
NT = (((1,), (1,)), ((), ()))
TN = (((0,), (0,)), ((), ()))

HALO_SEND, HALO_UP, HALO_DOWN, SCAT_SEND, SCAT_TOP, SCAT_BOT = range(6)
TAB_SEND, TAB_RECV, PICK_SEND, PICK_RECV, HALO_DOWN_SEND = 6, 7, 8, 10, 11
MIRROR_SEND, MIRROR_RECV, SEM_COLS = 12, 13, 14


def iota(shape, dim):
    return lax.broadcasted_iota(jnp.int32, shape, dim)


def gelu(x):
    inner = x * (0.7978845608028654 + 0.035677408136300125 * (x * x))
    half = 0.5 * x
    return half + half * jnp.tanh(inner)


def drain(ref, sem):
    pltpu.make_async_copy(ref, ref, sem).wait()


class Level:
    def __init__(self, rows, side, body, sems, bufs, sel, edge, strip):
        self.edge, self.strip = edge, strip
        self.rows, self.side, self.body, self.sems = rows, side, body, sems
        self.scat, self.scat_in, self.tab, self.tabs, self.pick, self.gath = bufs[:6]
        self.send, self.mirror = bufs[6:]
        self.sel = sel


def kernel(
    groups,
    tiles,
    rows,
    faces,
    seam_ref,
    inv_ref,
    slot_ref,
    atmos_ref,
    land_hbm,
    held_hbm,
    w1_hbm,
    w2_hbm,
    w3_hbm,
    w4_hbm,
    head_hbm,
    oin_hbm,
    oout_hbm,
    out_ref,
    sea_ref,
    body1,
    body2,
    body3,
    bodys,
    body4,
    bodyc,
    sel_f,
    sel_c,
    up_mat,
    down_mat,
    pred,
    visit,
    sea_out,
    sea_in,
    w1,
    w2,
    w3,
    w4,
    w5,
    head,
    oout,
    before,
    idle,
    tile_sea,
    a1,
    a2,
    a3,
    a4,
    a5,
    edges,
    strips,
    edgec,
    made_edge,
    skip_sum,
    wet_edge,
    before_edge,
    state_edge,
    out_vmem,
    out_edge,
    land_ref,
    held_ref,
    w1_ref,
    w2_ref,
    w3_ref,
    w4_ref,
    head_ref,
    oin_ref,
    oout_ref,
    loaded,
    oin_a,
    oin_b,
    split,
    *rest,
):
    bufs, (sems, misc) = rest[:-2], rest[-2:]
    f = lax.axis_index("face")
    t = lax.axis_index("tile")
    side = rows * tiles
    half_rows, half_side = rows // 2, side // 2
    is_top, is_bot = t == 0, t == tiles - 1
    last = tiles - 1

    inputs = (
        (land_hbm, land_ref),
        (held_hbm, held_ref),
        (w1_hbm, w1_ref),
        (w2_hbm, w2_ref),
        (w3_hbm, w3_ref),
        (w4_hbm, w4_ref),
        (head_hbm, head_ref),
        (oin_hbm, oin_ref),
        (oout_hbm, oout_ref),
    )
    loads = [
        pltpu.make_async_copy(src, dst, loaded.at[i]) for i, (src, dst) in enumerate(inputs)
    ]
    atmos_ch = atmos_ref.shape[2]
    for j in range(faces):
        for r in range(rows):
            pltpu.make_async_copy(
                atmos_ref.at[j, r], body1.at[j, pl.ds((r + 1) * C, atmos_ch)], misc.at[0]
            ).start()
    for load in loads:
        load.start()

    levels = []
    for number, (n, s, body, sel) in enumerate(
        (
            (rows, side, body1, sel_f),
            (rows, side, body2, sel_f),
            (half_rows, half_side, body3, sel_c),
            (rows, side, bodys, sel_f),
            (half_rows, half_side, body4, sel_c),
        )
    ):
        own = bufs[8 * number : 8 * number + 8]
        levels.append(
            Level(n, s, body, sems.at[number], own, sel, edges.at[number], strips.at[number])
        )

    barrier = pltpu.get_barrier_semaphore()

    def greet(d, carry):
        peer = lax.rem(t + d, tiles)
        pl.semaphore_signal(barrier, inc=1, device_id=(f, peer), device_id_type=MESH)
        return carry

    lax.fori_loop(1, tiles, greet, 0)
    for d in range(1, groups):
        g = lax.rem(f + d, groups)
        pl.semaphore_signal(barrier, inc=1, device_id=(g, t), device_id_type=MESH)

    @pl.when(is_top | is_bot)
    def _():
        for n, s, sel in ((rows, side, sel_f), (half_rows, half_side, sel_c)):
            shape = (tiles * 16, s)
            q, x = iota(shape, 0), iota(shape, 1)
            k = q % 16
            start = (q // 16) * n
            for at, low, high, base in ((0, 0, 10, 0), (5, 10, 15, 10), (6, 10, 15, 5)):
                cell = k - base
                inner = (k >= low) & (k < high) & (cell <= n + 1)
                sel[at] = jnp.where((x == start + cell - 1) & inner, 1.0, 0.0).astype(BF)
            for at, least in ((1, 0), (2, 8)):
                cell = start + k - least
                inner = (k >= least) & (k < least + n)
                sel[at] = jnp.where((x == cell) & inner, 1.0, 0.0).astype(BF)
                sel[at + 2] = jnp.where((x == s - 1 - cell) & inner, 1.0, 0.0).astype(BF)

    shape = (half_side, side)
    up_mat[...] = jnp.where(iota(shape, 1) // 2 == iota(shape, 0), 1.0, 0.0).astype(BF)
    shape = (side, half_side)
    down_mat[...] = jnp.where(iota(shape, 0) // 2 == iota(shape, 1), 0.25, 0.0).astype(BF)

    for j in range(faces):
        for r in range(rows):
            spare = C - atmos_ch
            if spare:
                body1[j, pl.ds((r + 1) * C + atmos_ch, spare), :] = jnp.zeros((spare, side), BF)
    for load in loads:
        load.wait()

    for target, along, ref, first, width in (
        (w1, a1, w1_ref, 0, w1_ref.shape[2] // 3),
        (w2, a2, w2_ref, 0, C),
        (w3, a3, w3_ref, 0, C),
        (w4, a4, w4_ref, 0, C),
        (w5, a5, w4_ref, C, C),
    ):
        channels = ref.shape[2] // 3
        for a in range(3):
            whole = ref[a].astype(F32)
            for b in range(3):
                at = b * channels + first
                block = whole[:, at : at + width]
                if width < C:
                    block = jnp.concatenate([block, jnp.zeros((C, C - width), F32)], axis=1)
                target[pl.ds(b * C, C), pl.ds(a * C, C)] = block.astype(BF)
                along[pl.ds(a * C, C), pl.ds(b * C, C)] = block.astype(BF)
    made = head_ref[...].astype(F32)
    gap = jnp.zeros((FLUX_CH, C), F32)
    head[...] = jnp.concatenate([made[:OUT_VARS]] + [made[OUT_VARS:]] * 3 + [gap], axis=0).astype(
        BF
    )
    diagonal = iota((C, C), 0) == iota((C, C), 1)

    def column(row):
        spread = jnp.where(diagonal, jnp.broadcast_to(row, (C, C)), 0.0)
        return jnp.sum(spread, axis=1, keepdims=True)

    oout[...] = jnp.broadcast_to(column(oout_ref[...]), oout.shape)
    oin = [column(oin_ref[c : c + 1, :]) for c in range(OCEAN_CH + FLUX_CH)]
    w_a, w_b = (jnp.broadcast_to(oin[c], (C, side)) for c in range(OCEAN_CH))
    oin_a[...] = w_a
    oin_b[...] = w_b
    flux_in = jnp.concatenate(oin[OCEAN_CH:], axis=1)
    first = flux_in.astype(BF)
    second = (flux_in - first.astype(F32)).astype(BF)
    third = (flux_in - first.astype(F32) - second.astype(F32)).astype(BF)
    split[...] = jnp.concatenate(
        [v.astype(F32) for v in (first, second, third)] + [jnp.zeros((C, FLUX_CH), F32)], axis=1
    ).astype(BF)

    drain(body1.at[:, pl.ds(0, rows * atmos_ch), :], misc.at[0])
    pl.semaphore_wait(barrier, tiles - 1 + groups - 1)

    def remote(src, dst, send, recv, device):
        return pltpu.make_async_remote_copy(
            src_ref=src,
            dst_ref=dst,
            send_sem=send,
            recv_sem=recv,
            device_id=device,
            device_id_type=MESH,
        )

    def halo_up(lv):
        n, s = lv.rows, lv.side
        return remote(
            lv.body.at[:, pl.ds(C, C), pl.ds(0, s)],
            lv.body.at[:, pl.ds((n + 1) * C, C), pl.ds(0, s)],
            lv.sems.at[HALO_SEND],
            lv.sems.at[HALO_DOWN],
            (f, jnp.maximum(t - 1, 0)),
        )

    def halo_down(lv):
        n, s = lv.rows, lv.side
        return remote(
            lv.body.at[:, pl.ds(n * C, C), pl.ds(0, s)],
            lv.body.at[:, pl.ds(0, C), pl.ds(0, s)],
            lv.sems.at[HALO_DOWN_SEND],
            lv.sems.at[HALO_UP],
            (f, jnp.minimum(t + 1, last)),
        )

    def scatter_piece(lv, which, dst):
        return remote(
            lv.scat.at[dst],
            lv.scat_in.at[which],
            lv.sems.at[SCAT_SEND],
            lv.sems.at[SCAT_TOP + which],
            (f, dst),
        )

    def begin_rows(lv):
        n, s = lv.rows, lv.side

        @pl.when(jnp.logical_not(is_top))
        def _():
            halo_up(lv).start()

        @pl.when(jnp.logical_not(is_bot))
        def _():
            halo_down(lv).start()

        for which, cond in ((0, is_top), (1, is_bot)):

            @pl.when(cond)
            def _(which=which):
                start = C if which == 0 else n * C
                a, b, c = (lv.body[j, pl.ds(start, C), pl.ds(0, s)] for j in range(faces))
                zero = jnp.zeros_like(a)
                total = jnp.zeros((tiles * 16, 2 * C), F32)
                for at, pair in ((0, [a, b]), (5, [c, zero]), (6, [zero, c])):
                    total += lax.dot_general(
                        lv.sel[at],
                        jnp.concatenate(pair, axis=0),
                        NT,
                        preferred_element_type=F32,
                    )
                lv.scat[...] = total.astype(BF).reshape(tiles, 16, 2 * C)
                own = 0 if which == 0 else last
                lv.scat_in[which] = lv.scat[own]

                def send(d, carry):
                    scatter_piece(lv, which, lax.rem(own + d, tiles)).start()
                    return carry

                lax.fori_loop(1, tiles, send, 0)

    def end_halos(lv):
        @pl.when(jnp.logical_not(is_top))
        def _():
            drain(lv.body.at[:, pl.ds(0, C), pl.ds(0, lv.side)], lv.sems.at[HALO_UP])

        @pl.when(jnp.logical_not(is_bot))
        def _():
            n = lv.rows
            drain(lv.body.at[:, pl.ds((n + 1) * C, C), pl.ds(0, lv.side)], lv.sems.at[HALO_DOWN])

    def end_scatter(lv):
        @pl.when(jnp.logical_not(is_top))
        def _():
            drain(lv.scat_in.at[0], lv.sems.at[SCAT_TOP])

        @pl.when(jnp.logical_not(is_bot))
        def _():
            drain(lv.scat_in.at[1], lv.sems.at[SCAT_BOT])

    def table_copy(lv, d):
        width = 2 * faces
        return remote(
            lv.tab,
            lv.tabs.at[pl.ds(f * width, width)],
            lv.sems.at[TAB_SEND],
            lv.sems.at[TAB_RECV],
            (lax.rem(f + d, groups), t),
        )

    lane = iota((C, 128), 1)

    def widened(data, right):
        missing = 128 - data.shape[1]
        if missing <= 0:
            return data
        zero = jnp.zeros((C, missing), data.dtype)
        return jnp.concatenate([zero, data] if right else [data, zero], axis=1)

    def extract(body, edge, s, j, ks, fresh, clear):
        total = jnp.zeros((C, 128), F32) if fresh else edge[j]
        wide = min(s, 128)
        for k in ks:
            here = pl.ds(k * C, C)
            left = widened(body[j, here, pl.ds(0, wide)].astype(F32), False)
            right = widened(body[j, here, pl.ds(s - wide, wide)].astype(F32), True)
            if clear and k == 0:
                left, right = (jnp.where(is_top, 0.0, v) for v in (left, right))
            if clear and k == ks[-1]:
                left, right = (jnp.where(is_bot, 0.0, v) for v in (left, right))
            total = jnp.where(lane // 2 == k, pltpu.roll(left, 2 * k, 1), total)
            total = jnp.where(
                lane // 2 == 32 + k, pltpu.roll(right, (66 + 2 * k) % 128, 1), total
            )
        edge[j] = total
        return total

    def extract_inner(body, edge, n, s):
        def one_face(j, carry):
            extract(body, edge, s, j, range(1, n + 1), True, False)
            return carry

        lax.fori_loop(0, faces, one_face, 0)

    def begin_tables(lv):
        end_halos(lv)
        n, s = lv.rows, lv.side
        shape = (32, 128)
        row, at = iota(shape, 0), iota(shape, 1)
        want = jnp.where(row < 16, 2 * row, 64 + 2 * (row - 16) + 1)
        pick = jnp.where((at == want) & (row % 16 < n + 2), 1.0, 0.0).astype(BF)

        def one_face(j, carry):
            edge = extract(lv.body, lv.edge, s, j, (0, n + 1), False, True)
            total = lax.dot_general(pick, edge.astype(BF), NT, preferred_element_type=F32)
            lv.tab[2 * j + 1] = jnp.concatenate([total[:16], total[16:]], axis=1).astype(BF)
            return carry

        lax.fori_loop(0, faces, one_face, 0, unroll=True)
        end_scatter(lv)
        lows, highs = [], []
        spot, row = iota((16, 128), 1), iota((16, 128), 0)
        for which in range(2):
            got = lv.scat_in[which].astype(F32)
            swapped = pltpu.roll(got, 64, 1)
            third = jnp.where(row < 5, pltpu.roll(got, 6, 0), pltpu.roll(swapped, 11, 0))
            lows.append((got, swapped, third))
            highs.append((swapped, got, pltpu.roll(third, 64, 1)))
        for j in range(faces):
            lv.tab[2 * j] = jnp.where(spot < 64, lows[0][j], highs[1][j]).astype(BF)
        for d in range(1, groups):
            table_copy(lv, d).start()
        lv.tabs[pl.ds(f * 2 * faces, 2 * faces)] = lv.tab[...]

    def end_tables(lv):
        drain(lv.tabs.at[pl.ds(0, (groups - 1) * 2 * faces)], lv.sems.at[TAB_RECV])

    def row_copy(lv, which):
        return remote(
            lv.send.at[which],
            lv.gath.at[t],
            lv.sems.at[PICK_SEND + which],
            lv.sems.at[PICK_RECV],
            (f, 0 if which == 0 else last),
        )

    def mirror_copy(lv):
        return remote(
            lv.pick, lv.mirror, lv.sems.at[MIRROR_SEND], lv.sems.at[MIRROR_RECV], (f, last - t)
        )

    def seam(j, s):
        at = (f * faces + j) * 4 + s
        return seam_ref[0, at], seam_ref[1, at]

    def begin_strips(lv):
        n = lv.rows
        shape = (16, 16)
        r, k = iota(shape, 0), iota(shape, 1)
        low = jnp.where((k == r + 1) & (r < n), 1.0, 0.0).astype(BF)
        high = jnp.where((k == r - 7) & (r >= 8) & (r < 8 + n), 1.0, 0.0).astype(BF)
        for which, cond in ((0, is_top), (1, is_bot)):
            parts = []
            for j in range(faces):
                p, _ = seam(j, which)
                spread = jnp.dot(
                    high if j == 2 else low, lv.tabs[p // 2], preferred_element_type=F32
                )
                parts.append(jnp.where(p % 2 == 1, spread[:, C:], spread[:, :C]))
            lv.send[which] = jnp.concatenate([parts[0] + parts[2], parts[1]], axis=1).astype(BF)

            @pl.when(jnp.logical_not(cond))
            def _(which=which):
                row_copy(lv, which).start()

            @pl.when(cond)
            def _(which=which):
                lv.gath[0 if which == 0 else last] = lv.send[which]

        for s in (2, 3):
            for j in range(faces):
                p, _ = seam(j, s)
                lv.pick[s - 2, j] = lv.tabs[p // 2]
        mirror_copy(lv).start()

    def column_strips(lv, fine):
        n = lv.rows
        shape = (16, 128)
        k, at = iota(shape, 0), iota(shape, 1)

        def one_face(j, carry):
            total = jnp.zeros((C, 128), F32)
            for s in (2, 3):
                p, rev = seam(j, s)
                piece = jnp.where(rev == 1, lv.mirror[s - 2, j], lv.pick[s - 2, j])
                kk = jnp.where(rev == 1, n + 1 - k, k)
                good = (kk >= jnp.where(is_top, 1, 0)) & (kk <= jnp.where(is_bot, n, n + 1))
                spot = at if s == 2 else at - 65
                index = (spot // 2 + 1) // 2 if fine else spot // 2
                good = good & (index == kk) & (spot % 2 == 0)
                good = good & ((at < 64) if s == 2 else (at > 64))
                chosen = jnp.where(good, 1.0, 0.0).astype(BF)
                both = lax.dot_general(piece, chosen, TN, preferred_element_type=F32)
                total += jnp.where(p % 2 == 1, both[C:], both[:C])
            lv.strip[j] = total
            return carry

        lax.fori_loop(0, faces, one_face, 0, unroll=True)

    def end_mirror(lv):
        drain(lv.mirror, lv.sems.at[MIRROR_RECV])

    def edge_terms(along, edge, strip):
        near = jnp.where(lane < 64, strip, pltpu.roll(edge, 1, 1))
        far = jnp.where(lane < 64, pltpu.roll(edge, 127, 1), strip)
        stack = jnp.concatenate([near, edge, far], axis=0).astype(BF)
        return jnp.dot(along[...], stack, preferred_element_type=F32)

    def edge_sum(terms):
        return (
            terms[:C]
            + pltpu.roll(terms[C : 2 * C], 126, 1)
            + pltpu.roll(terms[2 * C :], 124, 1)
        )

    def make_edges(lv, along):
        def one_face(j, carry):
            made_edge[j] = gelu(edge_sum(edge_terms(along, lv.edge[j], lv.strip[j])))
            return carry

        lax.fori_loop(0, faces, one_face, 0, unroll=True)

    def patch(s, r, values):
        wide = min(s, 128)
        spot = iota((values.shape[0], wide), 1)
        low = pltpu.roll(values, (128 - 2 * r) % 128, 1)[:, :wide]
        high = pltpu.roll(values, (2 * 128 + wide - 1 - 65 - 2 * r) % 128, 1)[:, :wide]
        return low, high, spot == 0, spot == wide - 1, pl.ds(0, wide), pl.ds(s - wide, wide)

    def fix(lv, target, r_list):
        n, s = lv.rows, lv.side

        def one_face(j, carry):
            values = made_edge[j]
            for r in r_list:
                low, high, is_low, is_high, left, right = patch(s, r, values)
                here = pl.ds((r + 1) * C, C)
                old = target[j, here, left].astype(F32)
                target[j, here, left] = jnp.where(is_low, low, old).astype(BF)
                old = target[j, here, right].astype(F32)
                target[j, here, right] = jnp.where(is_high, high, old).astype(BF)
            return carry

        lax.fori_loop(0, faces, one_face, 0, unroll=True)

    def end_strips(lv):
        n, s = lv.rows, lv.side
        for which, cond in ((0, is_top), (1, is_bot)):

            @pl.when(cond)
            def _(which=which):
                drain(lv.gath.at[pl.ds(0, tiles - 1)], lv.sems.at[PICK_RECV])
                for j in range(faces):
                    _, rev = seam(j, which)
                    pieces = lv.gath[...].reshape(tiles * 16, 2 * C)
                    chosen = lv.sel[(2 if j == 2 else 1) + 2 * rev]
                    both = lax.dot_general(pieces, chosen, TN, preferred_element_type=F32)
                    strip = both[C:] if j == 1 else both[:C]
                    at = 0 if which == 0 else (n + 1) * C
                    lv.body[j, pl.ds(at, C), pl.ds(0, s)] = strip.astype(BF)

    def finish_sends(lv):
        n, s = lv.rows, lv.side

        @pl.when(jnp.logical_not(is_top))
        def _():
            halo_up(lv).wait_send()
            row_copy(lv, 0).wait_send()

        @pl.when(jnp.logical_not(is_bot))
        def _():
            halo_down(lv).wait_send()
            row_copy(lv, 1).wait_send()

        @pl.when(is_top | is_bot)
        def _():
            drain(lv.scat.at[pl.ds(0, tiles - 1)], lv.sems.at[SCAT_SEND])

        drain(lv.tabs.at[pl.ds(0, (groups - 1) * 2 * faces)], lv.sems.at[TAB_SEND])
        mirror_copy(lv).wait_send()

    def taps(product, s):
        left = pltpu.roll(product[:C], 1, 1)
        right = pltpu.roll(product[2 * C :], s - 1, 1)
        return product[C : 2 * C] + left + right

    def conv_row(lv, w, target, j, r):
        n, s = lv.rows, lv.side
        window = lv.body[j, pl.ds(pl.multiple_of(r * C, C), 3 * C), :]
        product = jnp.dot(w[...], window, preferred_element_type=F32)
        made = gelu(taps(product, s)).astype(BF)
        target[j, pl.ds(pl.multiple_of(r * C + C, C), C), :] = made

    def inner_rows(first, stop, one_row):
        count = stop - first

        def body(i, carry):
            one_row(i // count, first + i % count)
            return carry

        if count > 0:
            lax.fori_loop(0, faces * count, body, 0, unroll=3)

    def outer_rows(n, one_row):
        for cond, r in ((is_top, 0), (is_bot, n - 1)):

            @pl.when(jnp.logical_not(cond))
            def _(r=r):
                for j in range(faces):
                    one_row(j, r)

    def end_row(lv, one_row):
        n = lv.rows
        for cond, k, r in ((is_top, 0, 0), (is_bot, n + 1, n - 1)):

            @pl.when(cond)
            def _(k=k, r=r):
                for j in range(faces):
                    extract(lv.body, lv.edge, lv.side, j, (k,), False, False)
                    one_row(j, r)

    def state_copy(d):
        dst = lax.rem(t + d, tiles)
        return remote(
            held_ref.at[pl.ds(2 * dst, 2)],
            visit.at[pl.ds(2 * t, 2)],
            misc.at[1],
            misc.at[2],
            (f, dst),
        )

    def sea_copy(d):
        dst = lax.rem(t + d, tiles)
        return remote(
            sea_out.at[pl.ds(2 * dst, 2)],
            sea_in.at[pl.ds(2 * t, 2)],
            misc.at[3],
            misc.at[4],
            (f, dst),
        )

    def start_all(copy):
        def body(d, carry):
            copy(d).start()
            return carry

        lax.fori_loop(1, tiles, body, 0)

    lv1, lv2, lv3, lvs, lv4 = levels
    begin_rows(lv1)
    start_all(state_copy)
    visit[pl.ds(2 * t, 2)] = held_ref[pl.ds(2 * t, 2)]

    def early_ocean():
        drain(visit.at[pl.ds(0, 2 * (tiles - 1))], misc.at[2])

        def one_slot(n, carry):
            old = visit[n]
            total = oin_a[...] * old[:1] + oin_b[...] * old[1:]
            before[n] = total
            moved = jnp.sum(oout[:, :side] * gelu(total), axis=0, keepdims=True)
            idle[n] = old[:1] + moved
            return carry

        lax.fori_loop(0, 2 * tiles, one_slot, 0, unroll=2)

    def to_edges(total, row, r, wide):
        spot = iota(total.shape, 1)
        low, high = row[:, :wide], row[:, side - wide :]
        if wide < 128:
            zero = jnp.zeros((row.shape[0], 128 - wide), row.dtype)
            low = jnp.concatenate([low, zero], axis=1)
            high = jnp.concatenate([zero, high], axis=1)
        total = jnp.where(spot == 2 * r, pltpu.roll(low, 2 * r, 1), total)
        return jnp.where(spot == 65 + 2 * r, pltpu.roll(high, (66 + 2 * r) % 128, 1), total)

    def ocean_edges():
        wide = min(side, 128)

        def one_face(j, carry):
            wet = jnp.zeros((8, 128), F32)
            state = jnp.zeros((8, 128), F32)
            total = jnp.zeros((C, 128), F32)
            for r in range(rows):
                slot = slot_ref[j * rows + r]
                land = jnp.broadcast_to(land_ref[j, pl.ds(r, 1), :], (8, side)).astype(F32)
                wet = to_edges(wet, land, r, wide)
                old = jnp.broadcast_to(visit[slot][:1], (8, side))
                state = to_edges(state, old, r, wide)
                total = to_edges(total, before[slot], r, wide)
            wet_edge[j] = wet
            state_edge[j] = state
            before_edge[j] = total
            return carry

        lax.fori_loop(0, faces, one_face, 0)

    def level(lv, w, along, target, held_back, fill_rows, fill_strips):
        n = lv.rows

        def one_row(j, r):
            conv_row(lv, w, target, j, r)

        extract_inner(lv.body, lv.edge, n, lv.side)
        inner_rows(1, n - 1 - held_back, one_row)
        fill_rows()
        begin_tables(lv)
        outer_rows(n, one_row)
        end_tables(lv)
        begin_strips(lv)
        inner_rows(n - 1 - held_back, n - 1, one_row)
        fill_strips()
        end_mirror(lv)
        column_strips(lv, False)
        end_strips(lv)
        end_row(lv, one_row)
        make_edges(lv, along)

    def nothing():
        pass

    level(lv1, w1, a1, body2, 0, nothing, early_ocean)
    fix(lv1, body2, (0, rows - 1))
    begin_rows(lv2)
    fix(lv1, body2, range(1, rows - 1))
    level(lv2, w2, a2, bodys, 2, nothing, ocean_edges)

    def pool(qs):
        def one_face(j, carry):
            for q in qs:
                pair = bodys[j, pl.ds((2 * q + 1) * C, 2 * C), :]
                summed = jnp.dot(pair, down_mat[...], preferred_element_type=F32)
                body3[j, pl.ds((q + 1) * C, C), :] = (summed[:C] + summed[C:]).astype(BF)
            return carry

        lax.fori_loop(0, faces, one_face, 0, unroll=True)

    outer = (0, 1, rows - 2, rows - 1)
    fix(lv2, bodys, outer)
    pool((0, half_rows - 1))
    begin_rows(lv3)
    fix(lv2, bodys, [r for r in range(rows) if r not in outer])
    pool(range(1, half_rows - 1))
    begin_rows(lvs)

    def skip_row(j, r):
        window = pl.ds(pl.multiple_of(r * C, C), 3 * C)
        product = jnp.dot(w4[...], bodys[j, window, :], preferred_element_type=F32)
        skip_sum[j * rows + r] = taps(product, side)

    skip_early = 1 + (rows - 2) // 3

    def fill_rows3():
        extract_inner(bodys, lvs.edge, rows, side)
        inner_rows(1, skip_early, skip_row)

    def fill_strips3():
        begin_tables(lvs)
        outer_rows(rows, skip_row)
        inner_rows(skip_early, rows - 1, skip_row)

    level(lv3, w3, a3, body4, 0, fill_rows3, fill_strips3)
    fix(lv3, body4, (0, half_rows - 1))
    begin_rows(lv4)
    fix(lv3, body4, range(1, half_rows - 1))

    def widen(j, qs):
        for q in qs:
            made = jnp.dot(
                body4[j, pl.ds(q * C, C), :], up_mat[...], preferred_element_type=F32
            ).astype(BF)
            for k in (2 * q - 1, 2 * q):
                if 0 <= k <= rows + 1:
                    bodyc[j, pl.ds(k * C, C), :] = made

    def widen_all(qs):
        def body(j, carry):
            widen(j, qs)
            return carry

        lax.fori_loop(0, faces, body, 0, unroll=True)

    def tile_values(j, r, out, width, start):
        where = pl.ds(start, width)
        state = body1[j, pl.ds(pl.multiple_of(r * C + C, C), 16), where]
        wet = jnp.broadcast_to(land_ref[j, pl.ds(r, 1), where] == 1, (16, width))
        return (
            state[:OUT_VARS].astype(F32) + out[:OUT_VARS],
            jnp.where(wet, out[OUT_VARS:], 0.0).astype(BF),
        )

    def decode_row(j, r):
        i = j * rows + r
        window = pl.ds(pl.multiple_of(r * C, C), 3 * C)
        product = jnp.dot(w5[...], bodyc[j, window, :], preferred_element_type=F32)
        decoded = gelu(skip_sum[i] + taps(product, side)).astype(BF)
        out = jnp.dot(head[...], decoded, preferred_element_type=F32)
        pred[i], flux = tile_values(j, r, out, side, 0)
        slot = slot_ref[i]
        hidden = gelu(before[slot] + jnp.dot(split[...], flux, preferred_element_type=F32))
        moved = jnp.sum(oout[:, :side] * hidden, axis=0, keepdims=True)
        tile_sea[i] = visit[slot][:1] + moved

    widen_all(range(1, half_rows + 1))
    extract_inner(body4, lv4.edge, half_rows, half_side)
    end_tables(lvs)
    begin_strips(lvs)
    early = 1 + (rows - 2) // 3
    inner_rows(1, early, decode_row)
    begin_tables(lv4)
    widen_all((0, half_rows + 1))
    outer_rows(rows, decode_row)
    end_tables(lv4)
    begin_strips(lv4)

    def coarse_edges(j, carry):
        extract(bodyc, edgec, side, j, range(rows + 2), True, True)
        return carry

    lax.fori_loop(0, faces, coarse_edges, 0, unroll=True)
    inner_rows(early, rows - 1, decode_row)
    end_mirror(lvs)
    column_strips(lvs, False)
    end_strips(lvs)
    for cond, k, r in ((is_top, 0, 0), (is_bot, rows + 1, rows - 1)):

        @pl.when(cond)
        def _(k=k, r=r):
            for j in range(faces):
                extract(bodys, lvs.edge, side, j, (k,), False, False)
                skip_row(j, r)

    end_mirror(lv4)
    column_strips(lv4, True)
    end_strips(lv4)
    for cond, q, k, r in (
        (is_top, 0, 0, 0),
        (is_bot, half_rows + 1, rows + 1, rows - 1),
    ):

        @pl.when(cond)
        def _(q=q, k=k, r=r):
            for j in range(faces):
                widen(j, (q,))
                extract(bodyc, edgec, side, j, (k,), False, False)
                decode_row(j, r)

    def decode_edges(j, carry):
        terms = edge_terms(a4, lvs.edge[j], lvs.strip[j])
        terms += edge_terms(a5, edgec[j], lv4.strip[j])
        values = gelu(edge_sum(terms)).astype(BF)
        out = jnp.dot(head[...], values, preferred_element_type=F32)
        out_edge[j] = out[:OUT_VARS]
        wet = jnp.concatenate([wet_edge[j]] * 2, axis=0) == 1.0
        flux = jnp.where(wet, out[OUT_VARS:], 0.0).astype(BF)
        hidden = gelu(before_edge[j] + jnp.dot(split[...], flux, preferred_element_type=F32))
        moved = jnp.sum(oout[:, :128] * hidden, axis=0, keepdims=True)
        sea = state_edge[j] + moved
        for r in range(rows):
            low, high, is_low, is_high, left, right = patch(side, r, sea)
            i = j * rows + r
            for part, mask, where in ((low, is_low, left), (high, is_high, right)):
                tile_sea[i, :, where] = jnp.where(mask[:1], part[:1], tile_sea[i, :, where])
        return carry

    def patch_edges(j, carry):
        out = out_edge[j]
        for r in range(rows):
            low, high, is_low, is_high, left, right = patch(side, r, out)
            i = j * rows + r
            for part, mask, where in ((low, is_low, left), (high, is_high, right)):
                state = body1[j, pl.ds((r + 1) * C, 16), where]
                kept = state[:OUT_VARS].astype(F32) + part
                pred[i, :, where] = jnp.where(mask, kept, pred[i, :, where])
        return carry

    lax.fori_loop(0, faces, decode_edges, 0, unroll=True)

    def fill(n, carry):
        tile = inv_ref[n]
        used = tile < faces * rows
        sea_out[n] = jnp.where(used, tile_sea[jnp.where(used, tile, 0)], idle[n])
        return carry

    lax.fori_loop(0, 2 * tiles, fill, 0, unroll=8)
    start_all(sea_copy)
    sea_in[pl.ds(2 * t, 2)] = sea_out[pl.ds(2 * t, 2)]

    lax.fori_loop(0, faces, patch_edges, 0, unroll=True)

    def surface(i, carry):
        sea = jnp.broadcast_to(tile_sea[i], (8, side))
        wet = jnp.broadcast_to(land_ref[i // rows, pl.ds(i % rows, 1), :] == 1, (8, side))
        wet = wet & (iota((8, side), 0) == 0)
        out_vmem[i] = jnp.where(wet, sea, pred[i])
        return carry

    lax.fori_loop(0, faces * rows, surface, 0, unroll=4)
    save = pltpu.make_async_copy(out_vmem, out_ref, loaded.at[0])
    save.start()
    drain(sea_in.at[pl.ds(0, 2 * (tiles - 1))], misc.at[4])
    save_sea = pltpu.make_async_copy(sea_in, sea_ref, loaded.at[1])
    save_sea.start()

    for lv in levels:
        finish_sends(lv)
    drain(held_ref.at[pl.ds(0, 2 * (tiles - 1))], misc.at[1])
    drain(sea_out.at[pl.ds(0, 2 * (tiles - 1))], misc.at[3])
    save.wait()
    save_sea.wait()


def on_device(
    atmos_state,
    land_sea,
    owners,
    seam_table,
    ocean_state,
    conv_input,
    conv_encode,
    conv_coarse,
    conv_decode,
    output_head,
    ocean_in,
    ocean_out,
):
    channels, faces, rows, side = atmos_state.shape
    groups, tiles = lax.axis_size("face"), lax.axis_size("tile")
    count = faces * rows
    slots = ocean_state.shape[2]
    atmos = jnp.transpose(atmos_state, (1, 2, 0, 3))
    owner_ids = owners[:, 0]
    same = owner_ids[:, None] == owner_ids[None, :]
    earlier = jnp.arange(count)[None, :] < jnp.arange(count)[:, None]
    rank = jnp.sum((same & earlier).astype(jnp.int32), axis=1)
    slot = owner_ids * (slots // tiles) + rank
    hits = jnp.arange(slots)[:, None] == slot[None, :]
    inverse = count + jnp.sum(
        jnp.where(hits, jnp.arange(count)[None, :] - count, 0), axis=1
    )
    held = ocean_state[0, 0]
    half_rows, half_side = rows // 2, side // 2
    vmem = pltpu.VMEM
    scratch = [
        vmem((faces, (rows + 2) * C, side), BF),
        vmem((faces, (rows + 2) * C, side), BF),
        vmem((faces, (half_rows + 2) * C, half_side), BF),
        vmem((faces, (rows + 2) * C, side), BF),
        vmem((faces, (half_rows + 2) * C, half_side), BF),
        vmem((faces, (rows + 2) * C, side), BF),
        vmem((7, tiles * 16, side), BF),
        vmem((7, tiles * 16, half_side), BF),
        vmem((half_side, side), BF),
        vmem((side, half_side), BF),
        vmem((count, OUT_VARS, side), F32),
        vmem((slots, OCEAN_CH, side), F32),
        vmem((slots, 1, side), F32),
        vmem((slots, 1, side), F32),
    ]
    scratch += [vmem((3 * C, 3 * C), BF)] * 5
    scratch += [
        vmem((24, C), BF),
        vmem((C, max(side, 128)), F32),
        vmem((slots, C, side), F32),
        vmem((slots, 1, side), F32),
        vmem((count, 1, side), F32),
    ]
    scratch += [vmem((3 * C, 3 * C), BF)] * 5
    scratch += [
        vmem((5, faces, C, 128), F32),
        vmem((5, faces, C, 128), F32),
        vmem((faces, C, 128), F32),
        vmem((faces, C, 128), F32),
        vmem((count, C, side), F32),
        vmem((faces, 8, 128), F32),
        vmem((faces, C, 128), F32),
        vmem((faces, 8, 128), F32),
        vmem((count, OUT_VARS, side), F32),
        vmem((faces, OUT_VARS, 128), F32),
    ]
    loaded = (
        land_sea,
        held,
        conv_input,
        conv_encode,
        conv_coarse,
        conv_decode,
        output_head,
        ocean_in.T,
        ocean_out[None],
    )
    scratch += [vmem(v.shape, v.dtype) for v in loaded]
    scratch += [
        pltpu.SemaphoreType.DMA((len(loaded),)),
        vmem((C, side), F32),
        vmem((C, side), F32),
        vmem((C, 16), BF),
    ]
    for _ in range(5):
        scratch += [
            vmem((tiles, 16, 2 * C), BF),
            vmem((2, 16, 2 * C), BF),
            vmem((2 * faces, 16, 2 * C), BF),
            vmem((groups * 2 * faces, 16, 2 * C), BF),
            vmem((2, faces, 16, 2 * C), BF),
            vmem((tiles, 16, 2 * C), BF),
            vmem((2, 16, 2 * C), BF),
            vmem((2, faces, 16, 2 * C), BF),
        ]
    scratch += [pltpu.SemaphoreType.DMA((5, SEM_COLS)), pltpu.SemaphoreType.DMA((5,))]
    smem = pl.BlockSpec(memory_space=pltpu.SMEM)
    anywhere = pl.BlockSpec(memory_space=pl.ANY)
    out, sea = pl.pallas_call(
        functools.partial(kernel, groups, tiles, rows, faces),
        out_shape=(
            jax.ShapeDtypeStruct((count, OUT_VARS, side), F32),
            jax.ShapeDtypeStruct((slots, 1, side), F32),
        ),
        in_specs=[smem] * 3 + [anywhere] * (1 + len(loaded)),
        out_specs=(anywhere, anywhere),
        scratch_shapes=scratch,
        compiler_params=pltpu.CompilerParams(
            collective_id=0, has_side_effects=True, vmem_limit_bytes=56 * 1024 * 1024
        ),
        name="coupled_step",
    )(
        seam_table.T,
        inverse,
        slot,
        atmos,
        *loaded,
    )
    atmos_next = jnp.transpose(out.reshape(faces, rows, OUT_VARS, side), (2, 0, 1, 3)).astype(BF)
    ocean_next = jnp.concatenate([sea, held[:, :1]], axis=1)
    return atmos_next, ocean_next[None, None]


def solution(mesh):
    in_specs = (
        P(None, "face", "tile", None),
        P("face", "tile", None),
        P(("face", "tile"), None),
        P(),
        P("face", "tile", None, None, None),
        P(),
        P(),
        P(),
        P(),
        P(),
        P(),
        P(),
    )
    out_specs = (P(None, "face", "tile", None), P("face", "tile", None, None, None))
    return jax.shard_map(
        on_device, mesh=mesh, in_specs=in_specs, out_specs=out_specs, check_vma=False
    )
```

```python
import functools

import jax
import jax.numpy as jnp
from jax import lax
from jax.experimental import pallas as pl
from jax.experimental.pallas import tpu as pltpu
from jax.sharding import PartitionSpec as P

MESH = pl.DeviceIdType.MESH
BF = jnp.bfloat16
F32 = jnp.float32
C = 64
OUT_VARS = 8
FLUX_CH = 4
OCEAN_CH = 2
NT = (((1,), (1,)), ((), ()))
TN = (((0,), (0,)), ((), ()))

HALO_SEND, HALO_UP, HALO_DOWN, SCAT_SEND, SCAT_TOP, SCAT_BOT = range(6)
TAB_SEND, TAB_RECV, PICK_SEND, PICK_RECV, HALO_DOWN_SEND = 6, 7, 8, 10, 11
MIRROR_SEND, MIRROR_RECV, SEM_COLS = 12, 13, 14


def iota(shape, dim):
    return lax.broadcasted_iota(jnp.int32, shape, dim)


def gelu(x):
    inner = x * (0.7978845608028654 + 0.035677408136300125 * (x * x))
    half = 0.5 * x
    return half + half * jnp.tanh(inner)


def drain(ref, sem):
    pltpu.make_async_copy(ref, ref, sem).wait()


class Level:
    def __init__(self, rows, side, body, sems, bufs, sel, edge, strip):
        self.edge, self.strip, self.sent = edge, strip, C
        self.rows, self.side, self.body, self.sems = rows, side, body, sems
        self.scat, self.scat_in, self.tab, self.tabs, self.pick, self.gath = bufs[:6]
        self.send, self.mirror = bufs[6:]
        self.sel = sel


def kernel(
    groups,
    tiles,
    rows,
    faces,
    seam_ref,
    inv_ref,
    slot_ref,
    atmos_ref,
    land_hbm,
    held_hbm,
    w1_hbm,
    w2_hbm,
    w3_hbm,
    w4_hbm,
    head_hbm,
    oin_hbm,
    oout_hbm,
    out_ref,
    sea_ref,
    body1,
    body2,
    body3,
    bodys,
    body4,
    bodyc,
    sel_f,
    sel_c,
    up_mat,
    down_mat,
    pred,
    visit,
    sea_out,
    sea_in,
    w1,
    w2,
    w3,
    w4,
    w5,
    head,
    oout,
    before,
    idle,
    tile_sea,
    a1,
    a2,
    a3,
    a4,
    a5,
    edges,
    strips,
    edgec,
    made_edge,
    skip_sum,
    wet_edge,
    before_edge,
    state_edge,
    out_vmem,
    out_edge,
    land_ref,
    held_ref,
    w1_ref,
    w2_ref,
    w3_ref,
    w4_ref,
    head_ref,
    oin_ref,
    oout_ref,
    loaded,
    oin_a,
    oin_b,
    split,
    *rest,
):
    bufs, (sems, misc) = rest[:-2], rest[-2:]
    f = lax.axis_index("face")
    t = lax.axis_index("tile")
    side = rows * tiles
    half_rows, half_side = rows // 2, side // 2
    is_top, is_bot = t == 0, t == tiles - 1
    last = tiles - 1

    inputs = (
        (land_hbm, land_ref),
        (held_hbm, held_ref),
        (w1_hbm, w1_ref),
        (w2_hbm, w2_ref),
        (w3_hbm, w3_ref),
        (w4_hbm, w4_ref),
        (head_hbm, head_ref),
        (oin_hbm, oin_ref),
        (oout_hbm, oout_ref),
    )
    loads = [
        pltpu.make_async_copy(src, dst, loaded.at[i]) for i, (src, dst) in enumerate(inputs)
    ]
    atmos_ch = atmos_ref.shape[2]
    for j in range(faces):
        for r in range(rows):
            pltpu.make_async_copy(
                atmos_ref.at[j, r], body1.at[j, pl.ds((r + 1) * C, atmos_ch)], misc.at[0]
            ).start()
    for load in loads:
        load.start()

    levels = []
    for number, (n, s, body, sel) in enumerate(
        (
            (rows, side, body1, sel_f),
            (rows, side, body2, sel_f),
            (half_rows, half_side, body3, sel_c),
            (rows, side, bodys, sel_f),
            (half_rows, half_side, body4, sel_c),
        )
    ):
        own = bufs[8 * number : 8 * number + 8]
        levels.append(
            Level(n, s, body, sems.at[number], own, sel, edges.at[number], strips.at[number])
        )

    barrier = pltpu.get_barrier_semaphore()

    def greet(d, carry):
        peer = lax.rem(t + d, tiles)
        pl.semaphore_signal(barrier, inc=1, device_id=(f, peer), device_id_type=MESH)
        return carry

    lax.fori_loop(1, tiles, greet, 0)
    for d in range(1, groups):
        g = lax.rem(f + d, groups)
        pl.semaphore_signal(barrier, inc=1, device_id=(g, t), device_id_type=MESH)

    @pl.when(is_top | is_bot)
    def _():
        for n, s, sel in ((rows, side, sel_f), (half_rows, half_side, sel_c)):
            shape = (tiles * 16, s)
            q, x = iota(shape, 0), iota(shape, 1)
            k = q % 16
            start = (q // 16) * n
            for at, low, high, base in ((0, 0, 10, 0), (5, 10, 15, 10), (6, 10, 15, 5)):
                cell = k - base
                inner = (k >= low) & (k < high) & (cell <= n + 1)
                sel[at] = jnp.where((x == start + cell - 1) & inner, 1.0, 0.0).astype(BF)
            for at, least in ((1, 0), (2, 8)):
                cell = start + k - least
                inner = (k >= least) & (k < least + n)
                sel[at] = jnp.where((x == cell) & inner, 1.0, 0.0).astype(BF)
                sel[at + 2] = jnp.where((x == s - 1 - cell) & inner, 1.0, 0.0).astype(BF)

    shape = (half_side, side)
    up_mat[...] = jnp.where(iota(shape, 1) // 2 == iota(shape, 0), 1.0, 0.0).astype(BF)
    shape = (side, half_side)
    down_mat[...] = jnp.where(iota(shape, 0) // 2 == iota(shape, 1), 0.25, 0.0).astype(BF)

    for j in range(faces):
        for k in range(rows + 2):
            spare = C - atmos_ch
            if spare:
                body1[j, pl.ds(k * C + atmos_ch, spare), :] = jnp.zeros((spare, side), BF)
    for load in loads:
        load.wait()

    for target, along, ref, first, width in (
        (w1, a1, w1_ref, 0, w1_ref.shape[2] // 3),
        (w2, a2, w2_ref, 0, C),
        (w3, a3, w3_ref, 0, C),
        (w4, a4, w4_ref, 0, C),
        (w5, a5, w4_ref, C, C),
    ):
        channels = ref.shape[2] // 3
        for a in range(3):
            whole = ref[a].astype(F32)
            for b in range(3):
                at = b * channels + first
                block = whole[:, at : at + width]
                if width < C:
                    block = jnp.concatenate([block, jnp.zeros((C, C - width), F32)], axis=1)
                target[pl.ds(b * C, C), pl.ds(a * C, C)] = block.astype(BF)
                along[pl.ds(a * C, C), pl.ds(b * C, C)] = block.astype(BF)
    made = head_ref[...].astype(F32)
    gap = jnp.zeros((FLUX_CH, C), F32)
    head[...] = jnp.concatenate([made[:OUT_VARS]] + [made[OUT_VARS:]] * 3 + [gap], axis=0).astype(
        BF
    )
    diagonal = iota((C, C), 0) == iota((C, C), 1)

    def column(row):
        spread = jnp.where(diagonal, jnp.broadcast_to(row, (C, C)), 0.0)
        return jnp.sum(spread, axis=1, keepdims=True)

    oout[...] = jnp.broadcast_to(column(oout_ref[...]), oout.shape)
    oin = [column(oin_ref[c : c + 1, :]) for c in range(OCEAN_CH + FLUX_CH)]
    w_a, w_b = (jnp.broadcast_to(oin[c], (C, side)) for c in range(OCEAN_CH))
    oin_a[...] = w_a
    oin_b[...] = w_b
    flux_in = jnp.concatenate(oin[OCEAN_CH:], axis=1)
    first = flux_in.astype(BF)
    second = (flux_in - first.astype(F32)).astype(BF)
    third = (flux_in - first.astype(F32) - second.astype(F32)).astype(BF)
    split[...] = jnp.concatenate(
        [v.astype(F32) for v in (first, second, third)] + [jnp.zeros((C, FLUX_CH), F32)], axis=1
    ).astype(BF)

    drain(body1.at[:, pl.ds(0, rows * atmos_ch), :], misc.at[0])
    pl.semaphore_wait(barrier, tiles - 1 + groups - 1)

    def remote(src, dst, send, recv, device):
        return pltpu.make_async_remote_copy(
            src_ref=src,
            dst_ref=dst,
            send_sem=send,
            recv_sem=recv,
            device_id=device,
            device_id_type=MESH,
        )

    def halo_up(lv):
        n, s = lv.rows, lv.side
        return remote(
            lv.body.at[:, pl.ds(C, lv.sent), pl.ds(0, s)],
            lv.body.at[:, pl.ds((n + 1) * C, lv.sent), pl.ds(0, s)],
            lv.sems.at[HALO_SEND],
            lv.sems.at[HALO_DOWN],
            (f, jnp.maximum(t - 1, 0)),
        )

    def halo_down(lv):
        n, s = lv.rows, lv.side
        return remote(
            lv.body.at[:, pl.ds(n * C, lv.sent), pl.ds(0, s)],
            lv.body.at[:, pl.ds(0, lv.sent), pl.ds(0, s)],
            lv.sems.at[HALO_DOWN_SEND],
            lv.sems.at[HALO_UP],
            (f, jnp.minimum(t + 1, last)),
        )

    def scatter_piece(lv, which, dst):
        return remote(
            lv.scat.at[dst],
            lv.scat_in.at[which],
            lv.sems.at[SCAT_SEND],
            lv.sems.at[SCAT_TOP + which],
            (f, dst),
        )

    def begin_rows(lv):
        n, s = lv.rows, lv.side

        for which, cond in ((0, is_top), (1, is_bot)):

            @pl.when(cond)
            def _(which=which):
                start = C if which == 0 else n * C
                a, b, c = (lv.body[j, pl.ds(start, C), pl.ds(0, s)] for j in range(faces))
                zero = jnp.zeros_like(a)
                total = jnp.zeros((tiles * 16, 2 * C), F32)
                for at, pair in ((0, [a, b]), (5, [c, zero]), (6, [zero, c])):
                    total += lax.dot_general(
                        lv.sel[at],
                        jnp.concatenate(pair, axis=0),
                        NT,
                        preferred_element_type=F32,
                    )
                lv.scat[...] = total.astype(BF).reshape(tiles, 16, 2 * C)
                own = 0 if which == 0 else last
                lv.scat_in[which] = lv.scat[own]

                def send(d, carry):
                    scatter_piece(lv, which, lax.rem(own + d, tiles)).start()
                    return carry

                lax.fori_loop(1, tiles, send, 0)

        @pl.when(jnp.logical_not(is_top))
        def _():
            halo_up(lv).start()

        @pl.when(jnp.logical_not(is_bot))
        def _():
            halo_down(lv).start()

    def end_halos(lv):
        @pl.when(jnp.logical_not(is_top))
        def _():
            drain(lv.body.at[:, pl.ds(0, lv.sent), pl.ds(0, lv.side)], lv.sems.at[HALO_UP])

        @pl.when(jnp.logical_not(is_bot))
        def _():
            n = lv.rows
            at = pl.ds((n + 1) * C, lv.sent)
            drain(lv.body.at[:, at, pl.ds(0, lv.side)], lv.sems.at[HALO_DOWN])

    def end_scatter(lv):
        @pl.when(jnp.logical_not(is_top))
        def _():
            drain(lv.scat_in.at[0], lv.sems.at[SCAT_TOP])

        @pl.when(jnp.logical_not(is_bot))
        def _():
            drain(lv.scat_in.at[1], lv.sems.at[SCAT_BOT])

    def table_copy(lv, d):
        width = 2 * faces
        return remote(
            lv.tab,
            lv.tabs.at[pl.ds(f * width, width)],
            lv.sems.at[TAB_SEND],
            lv.sems.at[TAB_RECV],
            (lax.rem(f + d, groups), t),
        )

    lane = iota((C, 128), 1)

    def widened(data, right):
        missing = 128 - data.shape[1]
        if missing <= 0:
            return data
        zero = jnp.zeros((C, missing), data.dtype)
        return jnp.concatenate([zero, data] if right else [data, zero], axis=1)

    def extract(body, edge, s, j, ks, fresh, clear):
        total = jnp.zeros((C, 128), F32) if fresh else edge[j]
        wide = min(s, 128)
        for k in ks:
            here = pl.ds(k * C, C)
            left = widened(body[j, here, pl.ds(0, wide)].astype(F32), False)
            right = widened(body[j, here, pl.ds(s - wide, wide)].astype(F32), True)
            if clear and k == 0:
                left, right = (jnp.where(is_top, 0.0, v) for v in (left, right))
            if clear and k == ks[-1]:
                left, right = (jnp.where(is_bot, 0.0, v) for v in (left, right))
            total = jnp.where(lane // 2 == k, pltpu.roll(left, 2 * k, 1), total)
            total = jnp.where(
                lane // 2 == 32 + k, pltpu.roll(right, (66 + 2 * k) % 128, 1), total
            )
        edge[j] = total
        return total

    def extract_inner(body, edge, n, s):
        def one_face(j, carry):
            extract(body, edge, s, j, range(1, n + 1), True, False)
            return carry

        lax.fori_loop(0, faces, one_face, 0)

    def begin_tables(lv):
        end_halos(lv)
        n, s = lv.rows, lv.side
        shape = (32, 128)
        row, at = iota(shape, 0), iota(shape, 1)
        want = jnp.where(row < 16, 2 * row, 64 + 2 * (row - 16) + 1)
        pick = jnp.where((at == want) & (row % 16 < n + 2), 1.0, 0.0).astype(BF)

        def one_face(j, carry):
            edge = extract(lv.body, lv.edge, s, j, (0, n + 1), False, True)
            total = lax.dot_general(pick, edge.astype(BF), NT, preferred_element_type=F32)
            lv.tab[2 * j + 1] = jnp.concatenate([total[:16], total[16:]], axis=1).astype(BF)
            return carry

        lax.fori_loop(0, faces, one_face, 0, unroll=True)
        end_scatter(lv)
        lows, highs = [], []
        spot, row = iota((16, 128), 1), iota((16, 128), 0)
        for which in range(2):
            got = lv.scat_in[which].astype(F32)
            swapped = pltpu.roll(got, 64, 1)
            third = jnp.where(row < 5, pltpu.roll(got, 6, 0), pltpu.roll(swapped, 11, 0))
            lows.append((got, swapped, third))
            highs.append((swapped, got, pltpu.roll(third, 64, 1)))
        for j in range(faces):
            lv.tab[2 * j] = jnp.where(spot < 64, lows[0][j], highs[1][j]).astype(BF)
        for d in range(1, groups):
            table_copy(lv, d).start()
        lv.tabs[pl.ds(f * 2 * faces, 2 * faces)] = lv.tab[...]

    def end_tables(lv):
        drain(lv.tabs.at[pl.ds(0, (groups - 1) * 2 * faces)], lv.sems.at[TAB_RECV])

    def row_copy(lv, which):
        return remote(
            lv.send.at[which],
            lv.gath.at[t],
            lv.sems.at[PICK_SEND + which],
            lv.sems.at[PICK_RECV],
            (f, 0 if which == 0 else last),
        )

    def mirror_copy(lv):
        return remote(
            lv.pick, lv.mirror, lv.sems.at[MIRROR_SEND], lv.sems.at[MIRROR_RECV], (f, last - t)
        )

    def seam(j, s):
        at = (f * faces + j) * 4 + s
        return seam_ref[0, at], seam_ref[1, at]

    def begin_strips(lv):
        n = lv.rows
        shape = (16, 16)
        r, k = iota(shape, 0), iota(shape, 1)
        low = jnp.where((k == r + 1) & (r < n), 1.0, 0.0).astype(BF)
        high = jnp.where((k == r - 7) & (r >= 8) & (r < 8 + n), 1.0, 0.0).astype(BF)
        for which, cond in ((0, is_top), (1, is_bot)):
            parts = []
            for j in range(faces):
                p, _ = seam(j, which)
                spread = jnp.dot(
                    high if j == 2 else low, lv.tabs[p // 2], preferred_element_type=F32
                )
                parts.append(jnp.where(p % 2 == 1, spread[:, C:], spread[:, :C]))
            lv.send[which] = jnp.concatenate([parts[0] + parts[2], parts[1]], axis=1).astype(BF)

            @pl.when(jnp.logical_not(cond))
            def _(which=which):
                row_copy(lv, which).start()

            @pl.when(cond)
            def _(which=which):
                lv.gath[0 if which == 0 else last] = lv.send[which]

        for s in (2, 3):
            for j in range(faces):
                p, _ = seam(j, s)
                lv.pick[s - 2, j] = lv.tabs[p // 2]
        mirror_copy(lv).start()

    def column_strips(lv, fine):
        n = lv.rows
        shape = (16, 128)
        k, at = iota(shape, 0), iota(shape, 1)

        def one_face(j, carry):
            total = jnp.zeros((C, 128), F32)
            for s in (2, 3):
                p, rev = seam(j, s)
                piece = jnp.where(rev == 1, lv.mirror[s - 2, j], lv.pick[s - 2, j])
                kk = jnp.where(rev == 1, n + 1 - k, k)
                good = (kk >= jnp.where(is_top, 1, 0)) & (kk <= jnp.where(is_bot, n, n + 1))
                spot = at if s == 2 else at - 65
                index = (spot // 2 + 1) // 2 if fine else spot // 2
                good = good & (index == kk) & (spot % 2 == 0)
                good = good & ((at < 64) if s == 2 else (at > 64))
                chosen = jnp.where(good, 1.0, 0.0).astype(BF)
                both = lax.dot_general(piece, chosen, TN, preferred_element_type=F32)
                total += jnp.where(p % 2 == 1, both[C:], both[:C])
            lv.strip[j] = total
            return carry

        lax.fori_loop(0, faces, one_face, 0, unroll=True)

    def end_mirror(lv):
        drain(lv.mirror, lv.sems.at[MIRROR_RECV])

    def edge_terms(along, edge, strip):
        near = jnp.where(lane < 64, strip, pltpu.roll(edge, 1, 1))
        far = jnp.where(lane < 64, pltpu.roll(edge, 127, 1), strip)
        stack = jnp.concatenate([near, edge, far], axis=0).astype(BF)
        return jnp.dot(along[...], stack, preferred_element_type=F32)

    def edge_sum(terms):
        return (
            terms[:C]
            + pltpu.roll(terms[C : 2 * C], 126, 1)
            + pltpu.roll(terms[2 * C :], 124, 1)
        )

    def make_edges(lv, along):
        def one_face(j, carry):
            made_edge[j] = gelu(edge_sum(edge_terms(along, lv.edge[j], lv.strip[j])))
            return carry

        lax.fori_loop(0, faces, one_face, 0, unroll=True)

    def patch(s, r, values):
        wide = min(s, 128)
        spot = iota((values.shape[0], wide), 1)
        low = pltpu.roll(values, (128 - 2 * r) % 128, 1)[:, :wide]
        high = pltpu.roll(values, (2 * 128 + wide - 1 - 65 - 2 * r) % 128, 1)[:, :wide]
        return low, high, spot == 0, spot == wide - 1, pl.ds(0, wide), pl.ds(s - wide, wide)

    def fix(lv, target, r_list):
        n, s = lv.rows, lv.side

        def one_face(j, carry):
            values = made_edge[j]
            for r in r_list:
                low, high, is_low, is_high, left, right = patch(s, r, values)
                here = pl.ds((r + 1) * C, C)
                old = target[j, here, left].astype(F32)
                target[j, here, left] = jnp.where(is_low, low, old).astype(BF)
                old = target[j, here, right].astype(F32)
                target[j, here, right] = jnp.where(is_high, high, old).astype(BF)
            return carry

        lax.fori_loop(0, faces, one_face, 0, unroll=True)

    def end_strips(lv):
        n, s = lv.rows, lv.side
        for which, cond in ((0, is_top), (1, is_bot)):

            @pl.when(cond)
            def _(which=which):
                drain(lv.gath.at[pl.ds(0, tiles - 1)], lv.sems.at[PICK_RECV])
                for j in range(faces):
                    _, rev = seam(j, which)
                    pieces = lv.gath[...].reshape(tiles * 16, 2 * C)
                    chosen = lv.sel[(2 if j == 2 else 1) + 2 * rev]
                    both = lax.dot_general(pieces, chosen, TN, preferred_element_type=F32)
                    strip = both[C:] if j == 1 else both[:C]
                    at = 0 if which == 0 else (n + 1) * C
                    lv.body[j, pl.ds(at, C), pl.ds(0, s)] = strip.astype(BF)

    def finish_sends(lv):
        n, s = lv.rows, lv.side

        @pl.when(jnp.logical_not(is_top))
        def _():
            halo_up(lv).wait_send()
            row_copy(lv, 0).wait_send()

        @pl.when(jnp.logical_not(is_bot))
        def _():
            halo_down(lv).wait_send()
            row_copy(lv, 1).wait_send()

        @pl.when(is_top | is_bot)
        def _():
            drain(lv.scat.at[pl.ds(0, tiles - 1)], lv.sems.at[SCAT_SEND])

        drain(lv.tabs.at[pl.ds(0, (groups - 1) * 2 * faces)], lv.sems.at[TAB_SEND])
        mirror_copy(lv).wait_send()

    def taps(product, s):
        left = pltpu.roll(product[:C], 1, 1)
        right = pltpu.roll(product[2 * C :], s - 1, 1)
        return product[C : 2 * C] + left + right

    def conv_row(lv, w, target, j, r):
        n, s = lv.rows, lv.side
        window = lv.body[j, pl.ds(pl.multiple_of(r * C, C), 3 * C), :]
        product = jnp.dot(w[...], window, preferred_element_type=F32)
        made = gelu(taps(product, s)).astype(BF)
        target[j, pl.ds(pl.multiple_of(r * C + C, C), C), :] = made

    def inner_rows(first, stop, one_row):
        count = stop - first

        def body(i, carry):
            one_row(i // count, first + i % count)
            return carry

        if count > 0:
            lax.fori_loop(0, faces * count, body, 0, unroll=3)

    def outer_rows(n, one_row):
        for cond, r in ((is_top, 0), (is_bot, n - 1)):

            @pl.when(jnp.logical_not(cond))
            def _(r=r):
                for j in range(faces):
                    one_row(j, r)

    def end_row(lv, one_row):
        n = lv.rows
        for cond, k, r in ((is_top, 0, 0), (is_bot, n + 1, n - 1)):

            @pl.when(cond)
            def _(k=k, r=r):
                for j in range(faces):
                    extract(lv.body, lv.edge, lv.side, j, (k,), False, False)
                    one_row(j, r)

    def state_copy(d):
        dst = lax.rem(t + d, tiles)
        return remote(
            held_ref.at[pl.ds(2 * dst, 2)],
            visit.at[pl.ds(2 * t, 2)],
            misc.at[1],
            misc.at[2],
            (f, dst),
        )

    def sea_copy(d):
        dst = lax.rem(t + d, tiles)
        return remote(
            sea_out.at[pl.ds(2 * dst, 2)],
            sea_in.at[pl.ds(2 * t, 2)],
            misc.at[3],
            misc.at[4],
            (f, dst),
        )

    def start_all(copy):
        def body(d, carry):
            copy(d).start()
            return carry

        lax.fori_loop(1, tiles, body, 0)

    lv1, lv2, lv3, lvs, lv4 = levels
    lv1.sent = atmos_ch
    begin_rows(lv1)

    def start_state():
        start_all(state_copy)
        visit[pl.ds(2 * t, 2)] = held_ref[pl.ds(2 * t, 2)]

    def early_ocean():
        drain(visit.at[pl.ds(0, 2 * (tiles - 1))], misc.at[2])

        def one_slot(n, carry):
            old = visit[n]
            total = oin_a[...] * old[:1] + oin_b[...] * old[1:]
            before[n] = total
            moved = jnp.sum(oout[:, :side] * gelu(total), axis=0, keepdims=True)
            idle[n] = old[:1] + moved
            return carry

        lax.fori_loop(0, 2 * tiles, one_slot, 0, unroll=2)

    def to_edges(total, row, r, wide):
        spot = iota(total.shape, 1)
        low, high = row[:, :wide], row[:, side - wide :]
        if wide < 128:
            zero = jnp.zeros((row.shape[0], 128 - wide), row.dtype)
            low = jnp.concatenate([low, zero], axis=1)
            high = jnp.concatenate([zero, high], axis=1)
        total = jnp.where(spot == 2 * r, pltpu.roll(low, 2 * r, 1), total)
        return jnp.where(spot == 65 + 2 * r, pltpu.roll(high, (66 + 2 * r) % 128, 1), total)

    def ocean_edges():
        wide = min(side, 128)

        def one_face(j, carry):
            wet = jnp.zeros((8, 128), F32)
            state = jnp.zeros((8, 128), F32)
            total = jnp.zeros((C, 128), F32)
            for r in range(rows):
                slot = slot_ref[j * rows + r]
                land = jnp.broadcast_to(land_ref[j, pl.ds(r, 1), :], (8, side)).astype(F32)
                wet = to_edges(wet, land, r, wide)
                old = jnp.broadcast_to(visit[slot][:1], (8, side))
                state = to_edges(state, old, r, wide)
                total = to_edges(total, before[slot], r, wide)
            wet_edge[j] = wet
            state_edge[j] = state
            before_edge[j] = total
            return carry

        lax.fori_loop(0, faces, one_face, 0)

    def level(lv, w, along, target, held_back, fill_rows, fill_tables, fill_strips):
        n = lv.rows

        def one_row(j, r):
            conv_row(lv, w, target, j, r)

        extract_inner(lv.body, lv.edge, n, lv.side)
        inner_rows(1, n - 1 - held_back, one_row)
        fill_rows()
        begin_tables(lv)
        fill_tables()
        outer_rows(n, one_row)
        end_tables(lv)
        begin_strips(lv)
        inner_rows(n - 1 - held_back, n - 1, one_row)
        fill_strips()
        end_mirror(lv)
        column_strips(lv, False)
        end_strips(lv)
        end_row(lv, one_row)
        make_edges(lv, along)

    def nothing():
        pass

    level(lv1, w1, a1, body2, min(rows - 2, 3), nothing, start_state, nothing)
    fix(lv1, body2, (0, rows - 1))
    begin_rows(lv2)
    fix(lv1, body2, range(1, rows - 1))

    def fill_strips2():
        early_ocean()
        ocean_edges()

    level(lv2, w2, a2, bodys, 0, nothing, nothing, fill_strips2)

    def pool(qs):
        def one_face(j, carry):
            for q in qs:
                pair = bodys[j, pl.ds((2 * q + 1) * C, 2 * C), :]
                summed = jnp.dot(pair, down_mat[...], preferred_element_type=F32)
                body3[j, pl.ds((q + 1) * C, C), :] = (summed[:C] + summed[C:]).astype(BF)
            return carry

        lax.fori_loop(0, faces, one_face, 0, unroll=True)

    outer = (0, 1, rows - 2, rows - 1)
    fix(lv2, bodys, outer)
    pool((0, half_rows - 1))
    begin_rows(lv3)
    fix(lv2, bodys, [r for r in range(rows) if r not in outer])
    pool(range(1, half_rows - 1))

    def skip_row(j, r):
        window = pl.ds(pl.multiple_of(r * C, C), 3 * C)
        product = jnp.dot(w4[...], bodys[j, window, :], preferred_element_type=F32)
        skip_sum[j * rows + r] = taps(product, side)

    skip_early = 1 + (rows - 2) // 3

    def fill_rows3():
        extract_inner(bodys, lvs.edge, rows, side)
        inner_rows(1, skip_early, skip_row)

    def fill_strips3():
        inner_rows(skip_early, rows - 1, skip_row)
        begin_tables(lvs)
        outer_rows(rows, skip_row)

    def fill_tables3():
        begin_rows(lvs)

    level(lv3, w3, a3, body4, 0, fill_rows3, fill_tables3, fill_strips3)
    fix(lv3, body4, (0, half_rows - 1))
    begin_rows(lv4)
    fix(lv3, body4, range(1, half_rows - 1))

    def widen(j, qs):
        for q in qs:
            made = jnp.dot(
                body4[j, pl.ds(q * C, C), :], up_mat[...], preferred_element_type=F32
            ).astype(BF)
            for k in (2 * q - 1, 2 * q):
                if 0 <= k <= rows + 1:
                    bodyc[j, pl.ds(k * C, C), :] = made

    def widen_all(qs):
        def body(j, carry):
            widen(j, qs)
            return carry

        lax.fori_loop(0, faces, body, 0, unroll=True)

    def tile_values(j, r, out, width, start):
        where = pl.ds(start, width)
        state = body1[j, pl.ds(pl.multiple_of(r * C + C, C), 16), where]
        wet = jnp.broadcast_to(land_ref[j, pl.ds(r, 1), where] == 1, (16, width))
        return (
            state[:OUT_VARS].astype(F32) + out[:OUT_VARS],
            jnp.where(wet, out[OUT_VARS:], 0.0).astype(BF),
        )

    def decode_row(j, r):
        i = j * rows + r
        window = pl.ds(pl.multiple_of(r * C, C), 3 * C)
        product = jnp.dot(w5[...], bodyc[j, window, :], preferred_element_type=F32)
        decoded = gelu(skip_sum[i] + taps(product, side)).astype(BF)
        out = jnp.dot(head[...], decoded, preferred_element_type=F32)
        pred[i], flux = tile_values(j, r, out, side, 0)
        slot = slot_ref[i]
        hidden = gelu(before[slot] + jnp.dot(split[...], flux, preferred_element_type=F32))
        moved = jnp.sum(oout[:, :side] * hidden, axis=0, keepdims=True)
        tile_sea[i] = visit[slot][:1] + moved

    widen_all(range(1, half_rows + 1))
    extract_inner(body4, lv4.edge, half_rows, half_side)
    early = 1 + (rows - 2) // 2
    inner_rows(1, early, decode_row)
    begin_tables(lv4)
    end_tables(lvs)
    begin_strips(lvs)
    widen_all((0, half_rows + 1))
    outer_rows(rows, decode_row)
    end_tables(lv4)
    begin_strips(lv4)

    def coarse_edges(j, carry):
        extract(bodyc, edgec, side, j, range(rows + 2), True, True)
        return carry

    lax.fori_loop(0, faces, coarse_edges, 0, unroll=True)
    inner_rows(early, rows - 1, decode_row)
    end_mirror(lvs)
    column_strips(lvs, False)
    end_strips(lvs)
    for cond, k, r in ((is_top, 0, 0), (is_bot, rows + 1, rows - 1)):

        @pl.when(cond)
        def _(k=k, r=r):
            for j in range(faces):
                extract(bodys, lvs.edge, side, j, (k,), False, False)
                skip_row(j, r)

    end_mirror(lv4)
    column_strips(lv4, True)
    end_strips(lv4)
    for cond, q, k, r in (
        (is_top, 0, 0, 0),
        (is_bot, half_rows + 1, rows + 1, rows - 1),
    ):

        @pl.when(cond)
        def _(q=q, k=k, r=r):
            for j in range(faces):
                widen(j, (q,))
                extract(bodyc, edgec, side, j, (k,), False, False)
                decode_row(j, r)

    def decode_edges(j, carry):
        terms = edge_terms(a4, lvs.edge[j], lvs.strip[j])
        terms += edge_terms(a5, edgec[j], lv4.strip[j])
        values = gelu(edge_sum(terms)).astype(BF)
        out = jnp.dot(head[...], values, preferred_element_type=F32)
        out_edge[j] = out[:OUT_VARS]
        wet = jnp.concatenate([wet_edge[j]] * 2, axis=0) == 1.0
        flux = jnp.where(wet, out[OUT_VARS:], 0.0).astype(BF)
        hidden = gelu(before_edge[j] + jnp.dot(split[...], flux, preferred_element_type=F32))
        moved = jnp.sum(oout[:, :128] * hidden, axis=0, keepdims=True)
        sea = state_edge[j] + moved
        for r in range(rows):
            low, high, is_low, is_high, left, right = patch(side, r, sea)
            i = j * rows + r
            for part, mask, where in ((low, is_low, left), (high, is_high, right)):
                tile_sea[i, :, where] = jnp.where(mask[:1], part[:1], tile_sea[i, :, where])
        return carry

    def patch_edges(j, carry):
        out = out_edge[j]
        for r in range(rows):
            low, high, is_low, is_high, left, right = patch(side, r, out)
            i = j * rows + r
            for part, mask, where in ((low, is_low, left), (high, is_high, right)):
                state = body1[j, pl.ds((r + 1) * C, 16), where]
                kept = state[:OUT_VARS].astype(F32) + part
                pred[i, :, where] = jnp.where(mask, kept, pred[i, :, where])
        return carry

    lax.fori_loop(0, faces, decode_edges, 0, unroll=True)

    def fill(n, carry):
        tile = inv_ref[n]
        used = tile < faces * rows
        sea_out[n] = jnp.where(used, tile_sea[jnp.where(used, tile, 0)], idle[n])
        return carry

    lax.fori_loop(0, 2 * tiles, fill, 0, unroll=8)
    start_all(sea_copy)
    sea_in[pl.ds(2 * t, 2)] = sea_out[pl.ds(2 * t, 2)]

    lax.fori_loop(0, faces, patch_edges, 0, unroll=True)

    def surface(i, carry):
        sea = jnp.broadcast_to(tile_sea[i], (8, side))
        wet = jnp.broadcast_to(land_ref[i // rows, pl.ds(i % rows, 1), :] == 1, (8, side))
        wet = wet & (iota((8, side), 0) == 0)
        out_vmem[i] = jnp.where(wet, sea, pred[i]).astype(BF)
        return carry

    lax.fori_loop(0, faces * rows, surface, 0, unroll=4)
    save = pltpu.make_async_copy(out_vmem, out_ref, loaded.at[0])
    save.start()
    drain(sea_in.at[pl.ds(0, 2 * (tiles - 1))], misc.at[4])
    save_sea = pltpu.make_async_copy(sea_in, sea_ref, loaded.at[1])
    save_sea.start()

    for lv in levels:
        finish_sends(lv)
    drain(held_ref.at[pl.ds(0, 2 * (tiles - 1))], misc.at[1])
    drain(sea_out.at[pl.ds(0, 2 * (tiles - 1))], misc.at[3])
    save.wait()
    save_sea.wait()


def on_device(
    atmos_state,
    land_sea,
    owners,
    seam_table,
    ocean_state,
    conv_input,
    conv_encode,
    conv_coarse,
    conv_decode,
    output_head,
    ocean_in,
    ocean_out,
):
    channels, faces, rows, side = atmos_state.shape
    groups, tiles = lax.axis_size("face"), lax.axis_size("tile")
    count = faces * rows
    slots = ocean_state.shape[2]
    atmos = jnp.transpose(atmos_state, (1, 2, 0, 3))
    owner_ids = owners[:, 0]
    same = owner_ids[:, None] == owner_ids[None, :]
    earlier = jnp.arange(count)[None, :] < jnp.arange(count)[:, None]
    rank = jnp.sum((same & earlier).astype(jnp.int32), axis=1)
    slot = owner_ids * (slots // tiles) + rank
    hits = jnp.arange(slots)[:, None] == slot[None, :]
    inverse = count + jnp.sum(
        jnp.where(hits, jnp.arange(count)[None, :] - count, 0), axis=1
    )
    held = ocean_state[0, 0]
    half_rows, half_side = rows // 2, side // 2
    vmem = pltpu.VMEM
    scratch = [
        vmem((faces, (rows + 2) * C, side), BF),
        vmem((faces, (rows + 2) * C, side), BF),
        vmem((faces, (half_rows + 2) * C, half_side), BF),
        vmem((faces, (rows + 2) * C, side), BF),
        vmem((faces, (half_rows + 2) * C, half_side), BF),
        vmem((faces, (rows + 2) * C, side), BF),
        vmem((7, tiles * 16, side), BF),
        vmem((7, tiles * 16, half_side), BF),
        vmem((half_side, side), BF),
        vmem((side, half_side), BF),
        vmem((count, OUT_VARS, side), F32),
        vmem((slots, OCEAN_CH, side), F32),
        vmem((slots, 1, side), F32),
        vmem((slots, 1, side), F32),
    ]
    scratch += [vmem((3 * C, 3 * C), BF)] * 5
    scratch += [
        vmem((24, C), BF),
        vmem((C, max(side, 128)), F32),
        vmem((slots, C, side), F32),
        vmem((slots, 1, side), F32),
        vmem((count, 1, side), F32),
    ]
    scratch += [vmem((3 * C, 3 * C), BF)] * 5
    scratch += [
        vmem((5, faces, C, 128), F32),
        vmem((5, faces, C, 128), F32),
        vmem((faces, C, 128), F32),
        vmem((faces, C, 128), F32),
        vmem((count, C, side), F32),
        vmem((faces, 8, 128), F32),
        vmem((faces, C, 128), F32),
        vmem((faces, 8, 128), F32),
        vmem((count, OUT_VARS, side), BF),
        vmem((faces, OUT_VARS, 128), F32),
    ]
    loaded = (
        land_sea,
        held,
        conv_input,
        conv_encode,
        conv_coarse,
        conv_decode,
        output_head,
        ocean_in.T,
        ocean_out[None],
    )
    scratch += [vmem(v.shape, v.dtype) for v in loaded]
    scratch += [
        pltpu.SemaphoreType.DMA((len(loaded),)),
        vmem((C, side), F32),
        vmem((C, side), F32),
        vmem((C, 16), BF),
    ]
    for _ in range(5):
        scratch += [
            vmem((tiles, 16, 2 * C), BF),
            vmem((2, 16, 2 * C), BF),
            vmem((2 * faces, 16, 2 * C), BF),
            vmem((groups * 2 * faces, 16, 2 * C), BF),
            vmem((2, faces, 16, 2 * C), BF),
            vmem((tiles, 16, 2 * C), BF),
            vmem((2, 16, 2 * C), BF),
            vmem((2, faces, 16, 2 * C), BF),
        ]
    scratch += [pltpu.SemaphoreType.DMA((5, SEM_COLS)), pltpu.SemaphoreType.DMA((5,))]
    smem = pl.BlockSpec(memory_space=pltpu.SMEM)
    anywhere = pl.BlockSpec(memory_space=pl.ANY)
    out, sea = pl.pallas_call(
        functools.partial(kernel, groups, tiles, rows, faces),
        out_shape=(
            jax.ShapeDtypeStruct((count, OUT_VARS, side), BF),
            jax.ShapeDtypeStruct((slots, 1, side), F32),
        ),
        in_specs=[smem] * 3 + [anywhere] * (1 + len(loaded)),
        out_specs=(anywhere, anywhere),
        scratch_shapes=scratch,
        compiler_params=pltpu.CompilerParams(
            collective_id=0, has_side_effects=True, vmem_limit_bytes=56 * 1024 * 1024
        ),
        name="coupled_step",
    )(
        seam_table.T,
        inverse,
        slot,
        atmos,
        *loaded,
    )
    atmos_next = jnp.transpose(out.reshape(faces, rows, OUT_VARS, side), (2, 0, 1, 3))
    ocean_next = jnp.concatenate([sea, held[:, :1]], axis=1)
    return atmos_next, ocean_next[None, None]


def solution(mesh):
    in_specs = (
        P(None, "face", "tile", None),
        P("face", "tile", None),
        P(("face", "tile"), None),
        P(),
        P("face", "tile", None, None, None),
        P(),
        P(),
        P(),
        P(),
        P(),
        P(),
        P(),
    )
    out_specs = (P(None, "face", "tile", None), P("face", "tile", None, None, None))
    return jax.shard_map(
        on_device, mesh=mesh, in_specs=in_specs, out_specs=out_specs, check_vma=False
    )
```
